32 devices in a mesh: lat: 8 (over z, y), lon: 2 (over x), comp: 2 (over core).
Axes of the slice: x: 2, y: 2, z: 4, core: 2. Of those that a mesh axis runs over, the one named last changes fastest.
Arguments:
- atm_state: bfloat16 [192, 256, 384], P('lat', ('lon', 'comp')), may hold values from -6 to 6
- ocean_state: bfloat16 [192, 256, 256], P(('lat', 'comp'), 'lon'), may hold values from -6 to 6
- wet_mask: int32 [192, 256], P(('lat', 'comp'), 'lon'), may hold values 0 or 1
- legendre: bfloat16 [512, 384, 192], P(('lat', 'lon', 'comp')), may hold values from -4 to 4
- quad_weight: float32 [192], replicated, may hold values from 0.5 to 2
- spec_real: bfloat16 [384, 384], replicated, may hold values from -0.3125 to 0.3125
- spec_imag: bfloat16 [384, 384], replicated, may hold values from -0.3125 to 0.3125
- degree_gain: float32 [384], replicated, may hold values from 0.5 to 2
- atm_gain: float32 [2, 384], replicated, may hold values from 0.1 to 1.9
- atm_up: bfloat16 [384, 768], replicated, may hold values from -0.3125 to 0.3125
- atm_down: bfloat16 [768, 384], replicated, may hold values from -0.21875 to 0.21875
- atm_to_surface: bfloat16 [384, 32], replicated, may hold values from -0.3125 to 0.3125
- surface_to_atm: bfloat16 [32, 384], replicated, may hold values from -1 to 1
- ocean_to_surface: bfloat16 [256, 32], replicated, may hold values from -0.375 to 0.375
- surface_to_ocean: bfloat16 [32, 256], replicated, may hold values from -1 to 1
- ocean_kernel: bfloat16 [2, 7, 7, 256], replicated, may hold values from -0.875 to 0.875
- ocean_gain: float32 [2, 256], replicated, may hold values from 0.1 to 1.9
- ocean_up: bfloat16 [2, 256, 1024], replicated, may hold values from -0.375 to 0.375
- ocean_down: bfloat16 [2, 1024, 256], replicated, may hold values from -0.1875 to 0.1875
Outputs:
- atm_out: bfloat16 [192, 256, 384], P('lat', ('lon', 'comp'))
- ocean_out: bfloat16 [192, 256, 256], P(('lat', 'comp'), 'lon')
The draws below stay inside these ranges and needn't reach their ends.
All inputs are finite; a program needn't handle non-finite values. No bound on the sum of `wet_mask` on one device may be relied on, other than what follows from the above.
Results may differ from the reference program's by a relative error of at most 0.01.
Values may be sent and summed in bfloat16 or wider, within the bound.
A program may use at most 128 MiB of HBM per device.

```python
import math
import jax
import jax.numpy as jnp
from jax import lax

C = 384
HID = 768
OC = 256
OHID = 1024
SURF = 32
MODES = 512
DEG = 384
STENCIL_TAPS = 7
OCEAN_DILATION = 2
LAT_DEV = 24
NLAT = 192
NLON = 256
MODES_DEV = 16
N_LAT = 8
DEVICES = 32


def with_ends(entries, own_key, smallest, high):
    shape = entries.shape
    place = [jax.random.randint(jax.random.fold_in(own_key, axis), (), 0, shape[axis]) for axis in range(len(shape))]
    entries = entries.at[tuple(place)].set(smallest)
    longest = shape.index(max(shape))
    place[longest] = (place[longest] + 1) % shape[longest]
    return entries.at[tuple(place)].set(high)


def level_of(own_key, shape, cuts, least, high):
    level = 1.0
    for axis_at, parts in cuts:
        steps = jax.random.uniform(jax.random.fold_in(jax.random.fold_in(own_key, 6), axis_at), (parts,), jnp.float32, least / len(cuts), high / len(cuts))
        level = level * jnp.repeat(jnp.exp(steps), shape[axis_at] // parts).reshape((-1,) + (1,) * (len(shape) - 1 - axis_at))
    return level


def noise(rng, shape, scale, reach, split=(), kind=jnp.bfloat16):
    values = scale * jax.random.normal(rng, shape, jnp.float32)
    if split:
        values = values * level_of(rng, shape, split, -0.22, 0.18)
    return jnp.clip(values, -reach, reach).astype(kind)


def setup_inputs(seed: int = 0) -> dict:
    arg_keys = jax.random.split(jax.random.key(seed), 20)
    return {
        "atm_state": noise(arg_keys[0], (NLAT, NLON, C), 1.0, 6.0, ((0, 8), (1, 4))),
        "ocean_state": noise(arg_keys[1], (NLAT, NLON, OC), 1.0, 6.0, ((0, 16), (1, 2))),
        "wet_mask": with_ends((jax.random.randint(arg_keys[2], (NLAT, NLON), 0, 3) < 2).astype(jnp.int32), jax.random.fold_in(arg_keys[2], 1), 0, 1),
        "legendre": noise(arg_keys[3], (MODES, DEG, NLAT), 1.0, 4.0, ((0, 32),)),
        "quad_weight": jnp.clip(jnp.exp(jax.random.uniform(arg_keys[4], (NLAT,), jnp.float32, math.log(0.5), math.log(2.0))), 0.5, 2.0),
        "spec_real": noise(arg_keys[5], (C, C), C ** -0.5, 0.3125),
        "spec_imag": noise(arg_keys[6], (C, C), C ** -0.5, 0.3125),
        "degree_gain": jnp.clip(jnp.exp(jax.random.uniform(arg_keys[7], (DEG,), jnp.float32, math.log(0.5), math.log(2.0))), 0.5, 2.0),
        "atm_gain": jnp.clip(1.0 + 0.18 * jax.random.normal(arg_keys[8], (2, C), jnp.float32), 0.1, 1.9),
        "atm_up": noise(arg_keys[9], (C, HID), C ** -0.5, 0.3125),
        "atm_down": noise(arg_keys[10], (HID, C), HID ** -0.5, 0.21875),
        "atm_to_surface": noise(arg_keys[11], (C, SURF), C ** -0.5, 0.3125),
        "surface_to_atm": noise(arg_keys[12], (SURF, C), SURF ** -0.5, 1.0),
        "ocean_to_surface": noise(arg_keys[13], (OC, SURF), OC ** -0.5, 0.375),
        "surface_to_ocean": noise(arg_keys[14], (SURF, OC), SURF ** -0.5, 1.0),
        "ocean_kernel": noise(arg_keys[15], (2, STENCIL_TAPS, STENCIL_TAPS, OC), (STENCIL_TAPS * STENCIL_TAPS) ** -0.5, 0.875),
        "ocean_gain": jnp.clip(1.0 + 0.18 * jax.random.normal(arg_keys[16], (2, OC), jnp.float32), 0.1, 1.9),
        "ocean_up": noise(arg_keys[17], (2, OC, OHID), OC ** -0.5, 0.375),
        "ocean_down": noise(arg_keys[18], (2, OHID, OC), OHID ** -0.5, 0.1875),
    }


epsilon = 1e-05

def layer_norm(values, gain):
    centred = values - lax.optimization_barrier(jnp.mean(values, axis=-1, keepdims=True))
    spread = lax.optimization_barrier(jnp.mean(centred * centred, axis=-1, keepdims=True))
    return centred * lax.rsqrt(spread + epsilon) * gain

def wave_table(row_index, circle):
    longitude = jnp.arange(circle, dtype=jnp.int32)
    wavenumber = row_index // 2
    phases = wavenumber[:, None] * longitude[None, :] % circle
    angles = phases.astype(jnp.float32) * (2.0 * math.pi / circle)
    waves = jnp.where((row_index % 2 == 0)[:, None], jnp.cos(angles), -jnp.sin(angles))
    return (wavenumber, waves)

def forward_table(row_index, circle):
    wavenumber, waves = wave_table(row_index, circle)
    return (waves.T / math.sqrt(circle)).astype(jnp.bfloat16)

def inverse_table(row_index, circle):
    wavenumber, waves = wave_table(row_index, circle)
    factor = jnp.where(wavenumber == 0, 1.0, 2.0).astype(jnp.float32)
    return (waves * factor[:, None] / math.sqrt(circle)).astype(jnp.bfloat16)

def spectral_filter(gathered, table, quad_weight, spec_real, spec_imag, degree_gain):
    count = table.shape[0]
    lat_total = table.shape[2]
    channels = gathered.shape[2]
    split_parts = gathered.reshape(lat_total, count, 2, channels)
    weighted = (table.astype(jnp.float32) * (quad_weight / lat_total)).astype(jnp.bfloat16)
    coeffs = jnp.einsum('mln,nmpc->mplc', weighted.astype(jnp.float32), split_parts.astype(jnp.float32)).astype(jnp.bfloat16)
    real_part = coeffs[:, 0]
    imag_part = coeffs[:, 1]
    mixed_real = jnp.dot(real_part, spec_real, preferred_element_type=jnp.float32) - jnp.dot(imag_part, spec_imag, preferred_element_type=jnp.float32)
    mixed_imag = jnp.dot(real_part, spec_imag, preferred_element_type=jnp.float32) + jnp.dot(imag_part, spec_real, preferred_element_type=jnp.float32)
    scaled = (jnp.stack([mixed_real, mixed_imag], axis=1) * degree_gain[:, None]).astype(jnp.bfloat16)
    returned = jnp.einsum('mln,mplc->nmpc', table.astype(jnp.float32), scaled.astype(jnp.float32)).astype(jnp.bfloat16)
    return returned.reshape(lat_total, 2 * count, channels)

def ocean_block(padded_field, kernel, gain, up_weight, down_weight):
    stencil_reach = STENCIL_TAPS // 2 * OCEAN_DILATION
    tile_height = padded_field.shape[0] - 2 * stencil_reach
    tile_breadth = padded_field.shape[1] - 2 * stencil_reach
    stencil = jnp.zeros((tile_height, tile_breadth, padded_field.shape[2]), jnp.float32)
    for row_offset_tap in range(STENCIL_TAPS):
        for column_tap in range(STENCIL_TAPS):
            stencil_window = padded_field[row_offset_tap * OCEAN_DILATION:row_offset_tap * OCEAN_DILATION + tile_height, column_tap * OCEAN_DILATION:column_tap * OCEAN_DILATION + tile_breadth]
            stencil = stencil + stencil_window.astype(jnp.float32) * kernel[row_offset_tap, column_tap].astype(jnp.float32)
    normed = layer_norm(stencil, gain).astype(jnp.bfloat16)
    hidden = jax.nn.gelu(jnp.dot(normed, up_weight, preferred_element_type=jnp.float32)).astype(jnp.bfloat16)
    centre = padded_field[stencil_reach:stencil_reach + tile_height, stencil_reach:stencil_reach + tile_breadth]
    return (centre.astype(jnp.float32) + jnp.dot(hidden, down_weight, preferred_element_type=jnp.float32)).astype(jnp.bfloat16)

def ocean_layer(state, kernel, gain, up_weight, down_weight):
    stencil_reach = STENCIL_TAPS // 2 * OCEAN_DILATION
    padded_field = jnp.pad(state, ((stencil_reach, stencil_reach), (stencil_reach, stencil_reach), (0, 0)))

    def one_band(band_index):
        start = (band_index * LAT_DEV).astype(jnp.int32)
        piece = lax.dynamic_slice_in_dim(padded_field, start, LAT_DEV + 2 * stencil_reach, 0)
        return ocean_block(piece, kernel, gain, up_weight, down_weight)
    bands = lax.map(one_band, jnp.arange(N_LAT, dtype=jnp.int32))
    return bands.reshape(NLAT, NLON, OC)

def reference(atm_state, ocean_state, wet_mask, legendre, quad_weight, spec_real, spec_imag, degree_gain, atm_gain, atm_up, atm_down, atm_to_surface, surface_to_atm, ocean_to_surface, surface_to_ocean, ocean_kernel, ocean_gain, ocean_up, ocean_down):
    wet = wet_mask.astype(jnp.float32)[:, :, None]
    ocean_flux = (jnp.dot(ocean_state, ocean_to_surface, preferred_element_type=jnp.float32) * wet).astype(jnp.bfloat16)
    forced = atm_state.astype(jnp.float32) + jnp.dot(ocean_flux, surface_to_atm, preferred_element_type=jnp.float32)
    normed = layer_norm(forced, atm_gain[0]).astype(jnp.bfloat16)
    row_index = jnp.arange(2 * MODES, dtype=jnp.int32)
    forward = forward_table(row_index, NLON)
    inverse = inverse_table(row_index, NLON)

    def to_spectrum(lat_band):
        return jnp.einsum('anc,nr->arc', lat_band.astype(jnp.float32), forward.astype(jnp.float32)).astype(jnp.bfloat16)
    spectrum = lax.map(to_spectrum, normed.reshape(N_LAT, LAT_DEV, NLON, C))
    spectrum = spectrum.reshape(NLAT, DEVICES, 2 * MODES_DEV, C)
    owner_blocks = jnp.moveaxis(spectrum, 1, 0)
    table_blocks = legendre.reshape(DEVICES, MODES_DEV, DEG, NLAT)

    def one_owner(pieces):
        return spectral_filter(pieces[0], pieces[1], quad_weight, spec_real, spec_imag, degree_gain)
    filtered = lax.map(one_owner, (owner_blocks, table_blocks))
    returned = jnp.moveaxis(filtered, 0, 1).reshape(N_LAT, LAT_DEV, 2 * MODES, C)

    def finish(pieces):
        lat_band, forced_band = pieces
        spatial = jnp.einsum('arc,rn->anc', lat_band.astype(jnp.float32), inverse.astype(jnp.float32)).astype(jnp.bfloat16)
        mixed = forced_band + spatial.astype(jnp.float32)
        normed_two = layer_norm(mixed, atm_gain[1]).astype(jnp.bfloat16)
        hidden = jax.nn.gelu(jnp.dot(normed_two, atm_up, preferred_element_type=jnp.float32)).astype(jnp.bfloat16)
        return (mixed + jnp.dot(hidden, atm_down, preferred_element_type=jnp.float32)).astype(jnp.bfloat16)
    atm_out = lax.map(finish, (returned, forced.reshape(N_LAT, LAT_DEV, NLON, C))).reshape(NLAT, NLON, C)
    atm_flux = jnp.dot(atm_state, atm_to_surface, preferred_element_type=jnp.float32).astype(jnp.bfloat16)
    current = (ocean_state.astype(jnp.float32) + wet * jnp.dot(atm_flux, surface_to_ocean, preferred_element_type=jnp.float32)).astype(jnp.bfloat16)
    for block_index in range(2):
        current = ocean_layer(current, ocean_kernel[block_index], ocean_gain[block_index], ocean_up[block_index], ocean_down[block_index])
    ocean_out = jnp.where(wet_mask[:, :, None] == 1, current, ocean_state)
    return (atm_out, ocean_out)
```

```python
import functools
import math

import jax
import jax.numpy as jnp
import numpy as np
from jax import lax
from jax.experimental import pallas as pl
from jax.experimental.pallas import tpu as pltpu
from jax.sharding import PartitionSpec as P

MODES = 512
STENCIL_TAPS = 7
OCEAN_DILATION = 2
COLUMNS = ("lon", "comp")
EVERY = ("lat", "lon", "comp")


epsilon = 1e-05


def padded(block, sides, width):
    for axis, dim in sides:
        count = lax.axis_size(axis)
        forward = [(i, i + 1) for i in range(count - 1)]
        backward = [(target, source) for source, target in forward]
        low = lax.ppermute(
            lax.slice_in_dim(block, block.shape[dim] - width, None, axis=dim), axis, forward
        )
        high = lax.ppermute(lax.slice_in_dim(block, 0, width, axis=dim), axis, backward)
        block = jnp.concatenate([low, block, high], axis=dim)
    return block


def layer_norm(values, gain):
    centred = values - jnp.mean(values, axis=-1, keepdims=True)
    spread = jnp.mean(centred * centred, axis=-1, keepdims=True)
    return centred * lax.rsqrt(spread + epsilon) * gain


def wave_table(row_index, circle):
    longitude = jnp.arange(circle, dtype=jnp.int32)
    wavenumber = row_index // 2
    phases = wavenumber[:, None] * longitude[None, :] % circle
    angles = phases.astype(jnp.float32) * (2.0 * math.pi / circle)
    waves = jnp.where((row_index % 2 == 0)[:, None], jnp.cos(angles), -jnp.sin(angles))
    return (wavenumber, waves)


def forward_table(row_index, circle):
    _, waves = wave_table(row_index, circle)
    return (waves.T / math.sqrt(circle)).astype(jnp.bfloat16)


def inverse_table(row_index, circle):
    wavenumber, waves = wave_table(row_index, circle)
    factor = jnp.where(wavenumber == 0, 1.0, 2.0).astype(jnp.float32)
    return (waves * factor[:, None] / math.sqrt(circle)).astype(jnp.bfloat16)


def reorder_rows(total_rows, owned, lat_count, col_count):
    positions = jnp.arange(total_rows, dtype=jnp.int32)
    stride = lat_count * owned
    return (
        owned * (positions % stride // owned * col_count + positions // stride) + positions % owned
    )


def spectral_filter(gathered, table, quad_weight, spec_real, spec_imag, degree_gain):
    count = table.shape[0]
    lat_total = table.shape[2]
    channels = gathered.shape[2]
    split_parts = gathered.reshape(lat_total, count, 2, channels)
    weighted = (table.astype(jnp.float32) * (quad_weight / lat_total)).astype(jnp.bfloat16)
    coeffs = jnp.einsum(
        "mln,nmpc->mplc", weighted, split_parts, preferred_element_type=jnp.float32
    ).astype(jnp.bfloat16)
    real_part = coeffs[:, 0]
    imag_part = coeffs[:, 1]
    mixed_real = jnp.dot(real_part, spec_real, preferred_element_type=jnp.float32) - jnp.dot(
        imag_part, spec_imag, preferred_element_type=jnp.float32
    )
    mixed_imag = jnp.dot(real_part, spec_imag, preferred_element_type=jnp.float32) + jnp.dot(
        imag_part, spec_real, preferred_element_type=jnp.float32
    )
    scaled = (jnp.stack([mixed_real, mixed_imag], axis=1) * degree_gain[:, None]).astype(
        jnp.bfloat16
    )
    returned = jnp.einsum(
        "mln,mplc->nmpc", table, scaled, preferred_element_type=jnp.float32
    ).astype(jnp.bfloat16)
    return returned.reshape(lat_total, 2 * count, channels)


def folds(circle, lat_dev, col_count, devices):
    return (
        MODES == 2 * circle
        and lat_dev % col_count == 0
        and devices % 4 == 0
        and (circle // 2) % devices == 0
        and (MODES // devices) % 4 == 0
    )


def place_of(kind, i, group):
    return kind * group + (group - 1 - i if kind % 2 else i)


def folded_waves(circle, devices):
    longitude = jnp.arange(circle, dtype=jnp.int32)
    position = jnp.arange(circle, dtype=jnp.int32)
    group = devices // 4
    owned = circle // devices
    owner = position // owned
    kind, place = owner // group, owner % group
    place = jnp.where(kind % 2 == 1, group - 1 - place, place)
    row_index = (4 * place + kind) * owned + position % owned
    wavenumber = jnp.where(row_index == 1, circle // 2, row_index // 2)
    phases = wavenumber[:, None] * longitude[None, :] % circle
    angles = phases.astype(jnp.float32) * (2.0 * math.pi / circle)
    cosine = ((row_index % 2 == 0) | (row_index == 1))[:, None]
    return jnp.where(cosine, jnp.cos(angles), -jnp.sin(angles)) / math.sqrt(circle)


def folded_operators(table, quad_weight, degree_gain):
    devices = lax.axis_size(EVERY)
    me = lax.axis_index(EVERY)
    count, _, lat_total = table.shape
    group = devices // 4
    part = count // 4
    family = me // group
    scaled = (table.astype(jnp.float32) * degree_gain[:, None]).astype(jnp.bfloat16)
    operators = jnp.einsum(
        "mlt,mlu->mtu", table, scaled, preferred_element_type=jnp.float32
    )
    operators = operators * (quad_weight / lat_total)
    first_scale = jnp.where(me == 0, 0.5, 1.0).astype(jnp.float32)
    scales = jnp.where(jnp.arange(count) == 0, first_scale, 1.0)
    operators = (operators * scales[:, None, None]).astype(jnp.bfloat16)
    turn = []
    for base in (group, 3 * group):
        for i in range(group):
            turn.append((base + (i + 1) % group, base + i))
    rotated = lax.ppermute(operators[:1], EVERY, turn)
    mirrored = jnp.concatenate([rotated, jnp.flip(operators[1:], axis=0)], axis=0)
    ordered = jnp.where(family % 2 == 1, mirrored, operators)
    received = [lax.dynamic_slice_in_dim(ordered, family * part, part, axis=0)]
    for shift in range(1, 4):
        pairs = []
        for i in range(group):
            for kind in range(4):
                pairs.append((place_of(kind, i, group), place_of(kind ^ shift, i, group)))
        piece = lax.dynamic_slice_in_dim(ordered, (family ^ shift) * part, part, axis=0)
        received.append(lax.ppermute(piece, EVERY, pairs))
    received = [value.astype(jnp.float32) for value in received]
    same = received[0] + received[2]
    other = received[1] + received[3]
    direct = jnp.where(family % 2 == 0, same, other)
    mirror = jnp.where(family % 2 == 0, other, same)
    lone = ((me == 0) & (jnp.arange(part) == 0))[:, None, None]
    both = direct + mirror
    gap = jnp.where(lone, 0.0, direct - mirror)
    top = jnp.concatenate([jnp.where(lone, direct, both), -gap], axis=2)
    bottom = jnp.concatenate([gap, jnp.where(lone, mirror, both)], axis=2)
    return (2.0 * top).astype(jnp.bfloat16), (2.0 * bottom).astype(jnp.bfloat16)


def folded_spectral(normed, legendre, quad_weight, spec_real, spec_imag, degree_gain, circle):
    width = normed.shape[2]
    top, bottom = folded_operators(legendre, quad_weight, degree_gain)
    slots = top.shape[0]
    waves = folded_waves(circle, lax.axis_size(EVERY)).astype(jnp.bfloat16)
    columns = lax.all_to_all(normed, COLUMNS, split_axis=0, concat_axis=1, tiled=True)
    spectrum = jnp.einsum(
        "rn,tnc->trc", waves, columns, preferred_element_type=jnp.float32
    ).astype(jnp.bfloat16)
    gathered = lax.all_to_all(spectrum, EVERY, split_axis=1, concat_axis=0, tiled=True)
    lat_total = gathered.shape[0]
    channels = jnp.concatenate([spec_real, spec_imag], axis=1)
    turned = gathered.reshape(lat_total, slots, 2, width).transpose(1, 2, 0, 3)
    mixed = jnp.dot(turned, channels, preferred_element_type=jnp.float32).astype(jnp.bfloat16)
    upper = jnp.concatenate([mixed[:, 0, :, :width], mixed[:, 1, :, width:]], axis=1)
    lower = jnp.concatenate([mixed[:, 0, :, width:], mixed[:, 1, :, :width]], axis=1)
    cosine = jnp.einsum("stu,suc->stc", top, upper, preferred_element_type=jnp.float32)
    sine = jnp.einsum("stu,suc->stc", bottom, lower, preferred_element_type=jnp.float32)
    filtered = jnp.stack([cosine, sine], axis=1).astype(jnp.bfloat16)
    filtered = filtered.reshape(2 * slots, lat_total, width).transpose(1, 0, 2)
    returned = lax.all_to_all(filtered, EVERY, split_axis=0, concat_axis=1, tiled=True)
    spatial = jnp.einsum(
        "rn,trc->tnc", waves, returned, preferred_element_type=jnp.float32
    ).astype(jnp.bfloat16)
    spectral = lax.all_to_all(spatial, COLUMNS, split_axis=1, concat_axis=0, tiled=True)
    return spectral, (spectrum, filtered)


def plain_spectral(normed, legendre, quad_weight, spec_real, spec_imag, degree_gain, circle):
    lat_count = lax.axis_size("lat")
    col_count = lax.axis_size(("lon", "comp"))
    total_rows = 2 * MODES
    owned = 2 * legendre.shape[0]
    natural = jnp.arange(total_rows, dtype=jnp.int32)
    columns = lax.all_to_all(normed, ("lon", "comp"), split_axis=2, concat_axis=1, tiled=True)
    forward = forward_table(natural, circle)
    inverse = inverse_table(reorder_rows(total_rows, owned, lat_count, col_count), circle)
    spectrum = jnp.einsum(
        "anc,nr->arc", columns, forward, preferred_element_type=jnp.float32
    ).astype(jnp.bfloat16)
    gathered = lax.all_to_all(
        lax.all_to_all(spectrum, "lat", split_axis=1, concat_axis=0, tiled=True),
        ("lon", "comp"),
        split_axis=1,
        concat_axis=2,
        tiled=True,
    )
    filtered = spectral_filter(gathered, legendre, quad_weight, spec_real, spec_imag, degree_gain)
    returned = lax.all_to_all(
        lax.all_to_all(filtered, "lat", split_axis=0, concat_axis=1, tiled=True),
        ("lon", "comp"),
        split_axis=2,
        concat_axis=1,
        tiled=True,
    )
    spatial = jnp.einsum(
        "arc,rn->anc", returned, inverse, preferred_element_type=jnp.float32
    ).astype(jnp.bfloat16)
    spectral = lax.all_to_all(spatial, COLUMNS, split_axis=1, concat_axis=2, tiled=True)
    return spectral, (spectrum, filtered)


def ocean_block(padded_field, kernel, gain, up_weight, down_weight):
    stencil_reach = STENCIL_TAPS // 2 * OCEAN_DILATION
    tile_height = padded_field.shape[0] - 2 * stencil_reach
    tile_breadth = padded_field.shape[1] - 2 * stencil_reach
    stencil = jnp.zeros((tile_height, tile_breadth, padded_field.shape[2]), jnp.float32)
    for row_offset_tap in range(STENCIL_TAPS):
        for column_tap in range(STENCIL_TAPS):
            stencil_window = padded_field[
                row_offset_tap * OCEAN_DILATION : row_offset_tap * OCEAN_DILATION + tile_height,
                column_tap * OCEAN_DILATION : column_tap * OCEAN_DILATION + tile_breadth,
            ]
            stencil = stencil + stencil_window.astype(jnp.float32) * kernel[
                row_offset_tap, column_tap
            ].astype(jnp.float32)
    normed = layer_norm(stencil, gain).astype(jnp.bfloat16)
    hidden = jax.nn.gelu(jnp.dot(normed, up_weight, preferred_element_type=jnp.float32)).astype(
        jnp.bfloat16
    )
    centre = padded_field[
        stencil_reach : stencil_reach + tile_height, stencil_reach : stencil_reach + tile_breadth
    ]
    return (
        centre.astype(jnp.float32)
        + jnp.dot(hidden, down_weight, preferred_element_type=jnp.float32)
    ).astype(jnp.bfloat16)


def ocean_kernel_body(
    field_ref, taps_ref, gain_ref, up_ref, down_ref, after_ref, out_ref, wide, normed
):
    rows, cols, width = out_ref.shape
    step = OCEAN_DILATION
    lanes = 128

    @pl.loop(0, rows + (STENCIL_TAPS - 1) * step)
    def _(row):
        wide[row] = field_ref[row].astype(jnp.float32)

    @pl.loop(0, rows // 2)
    def _(pair):
        base = pair // step * (2 * step) + pair % step
        for half in range(width // lanes):
            part = slice(half * lanes, (half + 1) * lanes)
            sums = [jnp.zeros((cols, lanes), jnp.float32) for _ in range(2)]
            for a in range(STENCIL_TAPS + 1):
                for b in range(STENCIL_TAPS):
                    window = wide[base + a * step, b * step : b * step + cols, part]
                    for which in range(2):
                        tap = a - which
                        if 0 <= tap < STENCIL_TAPS:
                            weight = taps_ref[tap * STENCIL_TAPS + b, :, part]
                            sums[which] = sums[which] + window * weight
            for which in range(2):
                normed[which * cols : (which + 1) * cols, part] = sums[which]
        stencil = normed[...]
        values = layer_norm(stencil, gain_ref[...]).astype(jnp.bfloat16)
        hidden = jax.nn.gelu(
            jnp.dot(values, up_ref[...], preferred_element_type=jnp.float32)
        ).astype(jnp.bfloat16)
        moved = jnp.dot(hidden, down_ref[...], preferred_element_type=jnp.float32)
        reach = STENCIL_TAPS // 2 * step
        for which in range(2):
            row = base + which * step
            centre = wide[row + reach, reach : reach + cols, :]
            out_ref[row] = (centre + moved[which * cols : (which + 1) * cols]).astype(
                out_ref.dtype
            )


def fast_ocean_block(field, kernel, gain, up_weight, down_weight, after):
    reach = STENCIL_TAPS // 2 * OCEAN_DILATION
    rows, cols, width = field.shape[0] - 2 * reach, field.shape[1] - 2 * reach, field.shape[2]
    hidden = up_weight.shape[1]
    taps = kernel.astype(jnp.float32).reshape(STENCIL_TAPS * STENCIL_TAPS, 1, width)
    whole = pl.BlockSpec(memory_space=pltpu.VMEM)
    cells = rows * cols
    return pl.pallas_call(
        ocean_kernel_body,
        out_shape=jax.ShapeDtypeStruct((rows, cols, width), jnp.bfloat16),
        in_specs=[whole] * 5 + [pl.BlockSpec(memory_space=pl.ANY)],
        out_specs=whole,
        scratch_shapes=[
            pltpu.VMEM(field.shape, jnp.float32),
            pltpu.VMEM((2 * cols, width), jnp.float32),
        ],
        compiler_params=pltpu.CompilerParams(vmem_limit_bytes=32 * 1024 * 1024),
        cost_estimate=pl.CostEstimate(
            flops=4 * cells * width * hidden + 98 * cells * width * 64,
            bytes_accessed=4 * field.size + 4 * up_weight.size,
            transcendentals=cells * hidden,
        ),
    )(field, taps, gain[None, :], up_weight, down_weight, after)


MESH_ID = pl.DeviceIdType.MESH


def fits(atm_state, ocean_state, legendre):
    devices = lax.axis_size(EVERY)
    col_count = lax.axis_size(COLUMNS)
    lat_dev, lon_dev, width = atm_state.shape
    rows, cols, sea_width = ocean_state.shape
    circle = lon_dev * col_count
    reach = STENCIL_TAPS // 2 * OCEAN_DILATION
    return (
        folds(circle, lat_dev, col_count, devices)
        and lax.axis_size("lon") == 2
        and lax.axis_size("comp") == 2
        and circle // devices == 8
        and legendre.shape[0] == 16
        and lat_dev // col_count % 2 == 0
        and lat_dev == 2 * rows
        and cols == 2 * lon_dev
        and cols == 128
        and rows == 2 * reach
        and rows % (2 * OCEAN_DILATION) == 0
        and 128 < legendre.shape[2] <= 192
        and lon_dev % 16 == 0
        and width % 128 == 0
        and sea_width == 256
    )


def whole_step_body(
    lat_total,
    atm_hbm,
    sea_hbm,
    wet_ref,
    legendre_hbm,
    quad_ref,
    real_hbm,
    imag_hbm,
    degree_ref,
    gain_ref,
    up_hbm,
    down_hbm,
    to_sea_ref,
    from_sea_ref,
    to_air_ref,
    from_air_ref,
    taps_in_ref,
    sea_gain_ref,
    sea_up_hbm,
    sea_down_hbm,
    waves_hbm,
    waves_back_hbm,
    air_out,
    sea_out,
    air,
    sea,
    legendre,
    spec_real,
    spec_imag,
    air_up,
    air_down,
    sea_up,
    sea_down,
    waves,
    waves_back,
    taps,
    wet_square,
    wet_full,
    flux_out,
    flux_in,
    forced,
    normed,
    columns,
    spec_send,
    gathered,
    flat,
    returned,
    spatial,
    spectral,
    op_send,
    op_recv,
    op_lone,
    op_lone_recv,
    both,
    gap,
    field,
    edges,
    sides,
    wide,
    stencil,
    load_sem,
    local_sem,
    flux_sem,
    column_sem,
    owner_sem,
    back_sem,
    grid_sem,
    op_sem,
    halo_sem,
):
    f32, bf16 = jnp.float32, jnp.bfloat16
    lat = lax.axis_index("lat")
    lon = lax.axis_index("lon")
    comp = lax.axis_index("comp")
    col_count = lax.axis_size(COLUMNS)
    devices = lax.axis_size(EVERY)
    group = devices // 4
    col = lon * 2 + comp
    me = lat * col_count + col
    tile = lat * 2 + comp
    tiles = lax.axis_size("lat") * 2
    lat_dev, lon_dev, width = air.shape
    rows, cols, sea_width = sea.shape
    band = lat_dev // col_count
    pairs = band // 2
    circle = lon_dev * col_count
    step = OCEAN_DILATION
    reach = STENCIL_TAPS // 2 * step
    slots = both.shape[0]
    block = 256

    def at_device(index):
        return (index // col_count, index % col_count // 2, index % 2)

    def at_tile(index, side):
        return (index // 2, side, index % 2)

    def remote(source, target, sems, k, where):
        return pltpu.make_async_remote_copy(
            src_ref=source,
            dst_ref=target,
            send_sem=sems.at[0, k],
            recv_sem=sems.at[1, k],
            device_id=where,
            device_id_type=MESH_ID,
        )

    barrier = pltpu.get_barrier_semaphore()

    @pl.loop(1, devices)
    def _(k):
        pl.semaphore_signal(
            barrier, inc=1, device_id=at_device((me + k) % devices), device_id_type=MESH_ID
        )

    loads = {}
    for index, (name, source, target) in enumerate(
        (
            ("sea", sea_hbm, sea),
            ("air", atm_hbm, air),
            ("legendre", legendre_hbm, legendre),
            ("waves", waves_hbm, waves),
            ("sea_up", sea_up_hbm, sea_up),
            ("sea_down", sea_down_hbm, sea_down),
            ("real", real_hbm, spec_real),
            ("imag", imag_hbm, spec_imag),
            ("back", waves_back_hbm, waves_back),
            ("up", up_hbm, air_up),
            ("down", down_hbm, air_down),
        )
    ):
        loads[name] = pltpu.make_async_copy(source, target, load_sem.at[index])
        loads[name].start()

    wet_square[...] = jnp.zeros_like(wet_square)
    wet_square[0:rows, :] = wet_ref[...].astype(f32)
    turned = jnp.transpose(wet_square[...])
    for i in range(rows):
        wet_full[i] = jnp.broadcast_to(turned[:, i : i + 1], (cols, 128))

    loads["sea"].wait()

    @pl.loop(0, rows)
    def _(i):
        flux = jnp.dot(sea[i], to_air_ref[...], preferred_element_type=f32)
        flux = (flux * wet_full[i][:, 0 : flux.shape[1]]).astype(bf16)
        flux_out[0, 0, i] = flux[0:lon_dev]
        flux_out[0, 1, i] = flux[lon_dev : 2 * lon_dev]

    loads["air"].wait()

    @pl.loop(0, rows // 2)
    def _(i):
        for half in range(2):
            block_of = air[pl.ds(half * rows + 2 * i, 2)].reshape(2 * lon_dev, width)
            flux = jnp.dot(block_of, to_sea_ref[...], preferred_element_type=f32).astype(bf16)
            flux_out[1, half, 2 * i] = flux[0:lon_dev]
            flux_out[1, half, 2 * i + 1] = flux[lon_dev : 2 * lon_dev]

    pl.semaphore_wait(barrier, devices - 1)
    partner = (lat, lon, 1 - comp)
    moves = []
    for kind in range(2):
        moves.append(
            remote(
                flux_out.at[kind, 1 - comp], flux_in.at[kind, comp], flux_sem, kind, partner
            )
        )
        moves[-1].start()
    kept = []
    for kind in range(2):
        kept.append(
            pltpu.make_async_copy(
                flux_out.at[kind, comp], flux_in.at[kind, comp], local_sem.at[kind]
            )
        )
        kept[-1].start()

    for k in range(2):
        for a in range(STENCIL_TAPS):
            line = taps_in_ref[k, a].astype(f32)
            for b in range(STENCIL_TAPS):
                taps[(k * STENCIL_TAPS + a) * STENCIL_TAPS + b] = line[b : b + 1]

    for move in kept:
        move.wait()
    for move in moves:
        move.wait()

    per = block // lon_dev

    @pl.loop(0, lat_dev // per)
    def _(i):
        half = i // (rows // per)
        start = i % (rows // per) * per
        flux = flux_in[0, half, pl.ds(start, per)].reshape(block, -1)
        value = air[pl.ds(i * per, per)].reshape(block, width).astype(f32)
        value = value + jnp.dot(flux, from_sea_ref[...], preferred_element_type=f32)
        forced[pl.ds(i * per, per)] = value.reshape(per, lon_dev, width)
        value = layer_norm(value, gain_ref[0:1]).astype(bf16)
        normed[pl.ds(i * per, per)] = value.reshape(per, lon_dev, width)

    to_columns = []
    for k in range(1, col_count):
        other = (col + k) % col_count
        move = remote(
            normed.at[pl.ds(other * band, band)],
            columns.at[col],
            column_sem,
            k - 1,
            (lat, other // 2, other % 2),
        )
        move.start()
        to_columns.append(move)
    own_columns = pltpu.make_async_copy(
        normed.at[pl.ds(col * band, band)], columns.at[col], local_sem.at[0]
    )
    own_columns.start()

    @pl.loop(0, rows)
    def _(i):
        flux = jnp.concatenate([flux_in[1, 0, i], flux_in[1, 1, i]], axis=0)
        added = jnp.dot(flux, from_air_ref[...], preferred_element_type=f32)
        mask = wet_full[i]
        mask = jnp.concatenate([mask, mask], axis=1)
        field[0, i] = (sea[i].astype(f32) + mask * added).astype(bf16)

    strip = 16
    near = pl.multiple_of((cols - strip) * (1 - lon), strip)

    def halo_moves(k):
        source = field.at[k]
        strips = source.at[:, pl.ds(near, strip), :]
        low, high = pl.ds(0, reach), pl.ds(rows - reach, reach)
        side = remote(
            strips, sides.at[k, pl.ds(reach, rows)], halo_sem.at[k], 0, at_tile(tile, 1 - lon)
        )
        back = (
            remote(source.at[low], edges.at[k, 1], halo_sem.at[k], 1, at_tile(tile - 1, lon)),
            remote(
                source.at[low, pl.ds(near, strip), :],
                sides.at[k, pl.ds(reach + rows, reach)],
                halo_sem.at[k],
                2,
                at_tile(tile - 1, 1 - lon),
            ),
        )
        ahead = (
            remote(source.at[high], edges.at[k, 0], halo_sem.at[k], 3, at_tile(tile + 1, lon)),
            remote(
                source.at[high, pl.ds(near, strip), :],
                sides.at[k, pl.ds(0, reach)],
                halo_sem.at[k],
                4,
                at_tile(tile + 1, 1 - lon),
            ),
        )
        return side, back, ahead

    def send_halo(k):
        side, back, ahead = halo_moves(k)

        @pl.when(tile > 0)
        def _():
            for move in back:
                move.start()

        @pl.when(tile < tiles - 1)
        def _():
            for move in ahead:
                move.start()

        side.start()

    def take_halo(k):
        side, back, ahead = halo_moves(k)
        side.wait()

        @pl.when(tile > 0)
        def _():
            for move in back:
                move.wait_send()
            for move in ahead:
                move.wait_recv()

        @pl.when(tile < tiles - 1)
        def _():
            for move in ahead:
                move.wait_send()
            for move in back:
                move.wait_recv()

        def margins(row, values):
            left = jnp.where(lon == 1, values[8:16], 0.0)
            right = jnp.where(lon == 0, values[0:8], 0.0)
            wide[row, 0:8] = left
            wide[row, cols + 8 : cols + 16] = right

        @pl.loop(0, rows)
        def _(i):
            wide[reach + i, 8 : cols + 8] = field[k, i].astype(f32)
            margins(reach + i, sides[k, reach + i].astype(f32))

        for which in range(2):
            first = which * (reach + rows)
            present = tile > 0 if which == 0 else tile < tiles - 1

            @pl.when(present)
            def _():
                @pl.loop(0, reach)
                def _(i):
                    wide[first + i, 8 : cols + 8] = edges[k, which, i].astype(f32)
                    margins(first + i, sides[k, first + i].astype(f32))

            @pl.when(jnp.logical_not(present))
            def _():
                @pl.loop(0, reach)
                def _(i):
                    wide[first + i] = jnp.zeros(wide.shape[1:], f32)

    send_halo(0)

    loads["legendre"].wait()
    kind = me // group
    odd = kind % 2
    place = me % group
    count = legendre.shape[0]
    edge = lat_total - 128

    def operator(k):
        index = odd * ((count - k) % count) + (1 - odd) * k
        table = legendre[index]
        scaled = (table.astype(f32) * degree_ref[...]).astype(bf16)
        value = lax.dot_general(
            table, scaled, (((0,), (0,)), ((), ())), preferred_element_type=f32
        )
        value = value * jnp.where((me == 0) & (index == 0), 0.5, 1.0).astype(f32)
        return (value * (quad_ref[...] / lat_total)).astype(bf16)

    @pl.loop(0, count // 2)
    def _(k):
        which, spot = k // 2, k % 2
        first, second = operator(2 * k), operator(2 * k + 1)
        op_send[which, 2 * spot] = first[:, 0:128]
        op_send[which, 2 * spot + 1] = second[:, 0:128]
        tail = jnp.concatenate([first[:, 128:lat_total], second[:, 128:lat_total]], axis=1)
        op_send[which, 4 + spot, :, 0 : 2 * edge] = tail

        @pl.when(k == 0)
        def _():
            op_lone[0] = first[:, 0:128]
            op_lone[1, :, 0 : 2 * edge] = tail

    spot_of = odd * (group - 1 - place) + (1 - odd) * place
    op_moves = []
    for shift, other in ((1, kind + 1 - 2 * odd), (2, (kind + 2) % 4), (3, 3 - kind)):
        other_odd = other % 2
        there = other * group + other_odd * (group - 1 - spot_of) + (1 - other_odd) * spot_of
        move = remote(
            op_send.at[other], op_recv.at[shift - 1], op_sem, shift - 1, at_device(there)
        )
        move.start()
        op_moves.append(move)
    lone_move = remote(
        op_lone, op_lone_recv.at[kind // 2], op_sem, 3 + kind // 2, at_device((group - place) % group)
    )

    @pl.when(odd == 1)
    def _():
        lone_move.start()

    def sea_pairs(k, first, last):
        @pl.loop(first, last)
        def _(pair):
            base = pair // step * (2 * step) + pair % step
            for half in range(sea_width // 128):
                part = slice(half * 128, (half + 1) * 128)
                sums = [jnp.zeros((cols, 128), f32) for _ in range(2)]
                for a in range(STENCIL_TAPS + 1):
                    for b in range(STENCIL_TAPS):
                        start = 8 - reach + b * step
                        window = wide[base + a * step, start : start + cols, part]
                        for which in range(2):
                            tap = a - which
                            if 0 <= tap < STENCIL_TAPS:
                                weight = taps[
                                    (k * STENCIL_TAPS + tap) * STENCIL_TAPS + b, :, part
                                ]
                                sums[which] = sums[which] + window * weight
                for which in range(2):
                    stencil[which * cols : (which + 1) * cols, part] = sums[which]
            values = layer_norm(stencil[...], sea_gain_ref[k : k + 1]).astype(bf16)
            hidden = jax.nn.gelu(
                jnp.dot(values, sea_up[k], preferred_element_type=f32)
            ).astype(bf16)
            moved = jnp.dot(hidden, sea_down[k], preferred_element_type=f32)
            for which in range(2):
                row = base + which * step
                centre = wide[row + reach, 8 : 8 + cols, :]
                value = (centre + moved[which * cols : (which + 1) * cols]).astype(bf16)
                if k == 0:
                    field[1, row] = value
                else:
                    mask = wet_full[row]
                    mask = jnp.concatenate([mask, mask], axis=1)
                    sea_out[row] = jnp.where(mask > 0.5, value, sea[row])

    take_halo(0)
    loads["sea_up"].wait()
    loads["sea_down"].wait()
    sea_pairs(0, 0, 2)

    loads["waves"].wait()
    own_columns.wait()
    for move in to_columns:
        move.wait()

    def transform(t):
        lines = jnp.concatenate([columns[b, t] for b in range(col_count)], axis=0)
        value = jnp.dot(waves[...], lines, preferred_element_type=f32)
        return value.reshape(devices, 8, width)

    @pl.loop(0, pairs)
    def _(p):
        joined = jnp.concatenate([transform(2 * p), transform(2 * p + 1)], axis=1)
        spec_send[:, p] = joined.astype(bf16)

    def exchange(source, target, sems):
        def move(k):
            other = (me + k) % devices
            return remote(source.at[other], target.at[me], sems, k, at_device(other))

        return move

    to_owner = exchange(spec_send, gathered, owner_sem)

    @pl.loop(1, devices)
    def _(k):
        to_owner(k).start()

    own = pltpu.make_async_copy(spec_send.at[me], gathered.at[me], local_sem.at[1])
    own.start()

    sea_pairs(0, 2, rows // 2)
    send_halo(1)

    for move in op_moves:
        move.wait()

    @pl.when(odd == 1)
    def _():
        lone_move.wait_send()

    @pl.when(kind == 0)
    def _():
        for which in range(2):
            remote(
                op_lone, op_lone_recv.at[which], op_sem, 3 + which, at_device(me)
            ).wait_recv()
            op_recv[2 * which, 0] = op_lone_recv[which, 0]
            op_recv[2 * which, 4, :, 0:edge] = op_lone_recv[which, 1, :, 0:edge]

    for s in range(slots):
        lone = (me == 0) & (s == 0)
        for piece in range(2):
            if piece == 0:
                into = slice(0, 128)

                def part_of(ref):
                    return ref[s].astype(f32)

            else:
                into = slice(128, lat_total)

                def part_of(ref):
                    lanes = slice(s % 2 * edge, (s % 2 + 1) * edge)
                    return ref[4 + s // 2, :, lanes].astype(f32)

            same = part_of(op_send.at[kind]) + part_of(op_recv.at[1])
            other = part_of(op_recv.at[0]) + part_of(op_recv.at[2])
            direct = jnp.where(odd == 0, same, other)
            mirror = jnp.where(odd == 0, other, same)
            total = jnp.where(lone, direct, direct + mirror)
            rest = jnp.where(lone, mirror, direct + mirror)
            skew = jnp.where(lone, 0.0, direct - mirror)
            both[s, 0, :, into] = (2.0 * total).astype(bf16)
            both[s, 1, :, into] = (2.0 * rest).astype(bf16)
            gap[s, :, into] = (2.0 * skew).astype(bf16)

    loads["real"].wait()
    loads["imag"].wait()
    own.wait()

    @pl.loop(1, devices)
    def _(k):
        to_owner(k).wait()

    chunk = devices // 8
    lines = chunk * band * 8

    @pl.loop(0, 8)
    def _(i):
        value = gathered[pl.ds(i * chunk, chunk)].astype(f32).reshape(lines, width)
        for c in range(width // 128):
            flat[c, pl.ds(i * lines, lines), :] = value[:, c * 128 : (c + 1) * 128]

    def take_rows(q):
        taken = [
            flat[c, pl.ds(q, lat_total, stride=8), :] for c in range(width // 128)
        ]
        return jnp.concatenate(taken, axis=1).astype(bf16)

    def put_rows(q, value):
        for c in range(width // 128):
            flat[c, pl.ds(q, lat_total, stride=8), :] = value[:, c * 128 : (c + 1) * 128]

    for s in range(slots):
        re, im = take_rows(2 * s), take_rows(2 * s + 1)

        def mix(value, matrix):
            return jnp.dot(value, matrix[...], preferred_element_type=f32).astype(bf16)

        def act(matrix, value):
            return jnp.dot(matrix, value, preferred_element_type=f32)

        cosine = act(both[s, 0], mix(re, spec_real)) - act(gap[s], mix(im, spec_imag))
        sine = act(gap[s], mix(re, spec_imag)) + act(both[s, 1], mix(im, spec_real))
        put_rows(2 * s, cosine)
        put_rows(2 * s + 1, sine)

    @pl.loop(0, 8)
    def _(i):
        value = [flat[c, pl.ds(i * lines, lines), :] for c in range(width // 128)]
        value = jnp.concatenate(value, axis=1).astype(bf16)
        gathered[pl.ds(i * chunk, chunk)] = value.reshape(chunk, pairs, 16, width)

    from_owner = exchange(gathered, returned, back_sem)

    @pl.loop(1, devices)
    def _(k):
        from_owner(k).start()

    own = pltpu.make_async_copy(gathered.at[me], returned.at[me], local_sem.at[0])
    own.start()

    take_halo(1)
    sea_pairs(1, 0, rows // 2)

    loads["back"].wait()
    own.wait()

    @pl.loop(1, devices)
    def _(k):
        from_owner(k).wait()

    @pl.loop(0, pairs)
    def _(p):
        value = returned[:, p].astype(f32)
        for which in range(2):
            lines = value[:, 8 * which : 8 * which + 8].reshape(circle, width).astype(bf16)
            line = jnp.dot(waves_back[...], lines, preferred_element_type=f32).astype(bf16)
            for b in range(col_count):
                spatial[b, 2 * p + which] = line[b * lon_dev : (b + 1) * lon_dev]

    to_grid = []
    for k in range(1, col_count):
        other = (col + k) % col_count
        move = remote(
            spatial.at[other],
            spectral.at[pl.ds(col * band, band)],
            grid_sem,
            k - 1,
            (lat, other // 2, other % 2),
        )
        move.start()
        to_grid.append(move)
    own = pltpu.make_async_copy(
        spatial.at[col], spectral.at[pl.ds(col * band, band)], local_sem.at[1]
    )
    own.start()

    loads["up"].wait()
    loads["down"].wait()
    own.wait()
    for move in to_grid:
        move.wait()

    @pl.loop(0, lat_dev // per)
    def _(i):
        here = pl.ds(i * per, per)
        mixed = forced[here].reshape(block, width)
        mixed = mixed + spectral[here].reshape(block, width).astype(f32)
        value = layer_norm(mixed, gain_ref[1:2]).astype(bf16)
        hidden = jax.nn.gelu(
            jnp.dot(value, air_up[...], preferred_element_type=f32)
        ).astype(bf16)
        mixed = mixed + jnp.dot(hidden, air_down[...], preferred_element_type=f32)
        air_out[here] = mixed.astype(bf16).reshape(per, lon_dev, width)


def whole_step(
    atm_state,
    ocean_state,
    wet_mask,
    legendre,
    quad_weight,
    spec_real,
    spec_imag,
    degree_gain,
    atm_gain,
    atm_up,
    atm_down,
    atm_to_surface,
    surface_to_atm,
    ocean_to_surface,
    surface_to_ocean,
    ocean_kernel,
    ocean_gain,
    ocean_up,
    ocean_down,
):
    bf16, f32 = jnp.bfloat16, jnp.float32
    devices = lax.axis_size(EVERY)
    col_count = lax.axis_size(COLUMNS)
    lat_dev, lon_dev, width = atm_state.shape
    rows, cols, sea_width = ocean_state.shape
    circle = lon_dev * col_count
    lat_total = legendre.shape[2]
    band = lat_dev // col_count
    reach = STENCIL_TAPS // 2 * OCEAN_DILATION
    slots = legendre.shape[0] // 4
    surface = atm_to_surface.shape[1]
    with jax.ensure_compile_time_eval():
        table = np.asarray(folded_waves(circle, devices).astype(f32))
    waves = jnp.asarray(table, f32).astype(bf16)
    waves_back = jnp.asarray(table.T, f32).astype(bf16)
    vmem = pl.BlockSpec(memory_space=pltpu.VMEM)
    hbm = pl.BlockSpec(memory_space=pl.ANY)
    tall = (devices, band // 2, 16, width)
    squares = (lat_total, 128)
    dma = pltpu.SemaphoreType.DMA
    return pl.pallas_call(
        functools.partial(whole_step_body, lat_total),
        out_shape=(
            jax.ShapeDtypeStruct(atm_state.shape, bf16),
            jax.ShapeDtypeStruct(ocean_state.shape, bf16),
        ),
        in_specs=[
            hbm, hbm, vmem, hbm, vmem, hbm, hbm, vmem, vmem, hbm, hbm,
            vmem, vmem, vmem, vmem, vmem, vmem, hbm, hbm, hbm, hbm,
        ],
        out_specs=(vmem, vmem),
        scratch_shapes=[
            pltpu.VMEM(atm_state.shape, bf16),
            pltpu.VMEM(ocean_state.shape, bf16),
            pltpu.VMEM(legendre.shape, bf16),
            pltpu.VMEM(spec_real.shape, bf16),
            pltpu.VMEM(spec_imag.shape, bf16),
            pltpu.VMEM(atm_up.shape, bf16),
            pltpu.VMEM(atm_down.shape, bf16),
            pltpu.VMEM(ocean_up.shape, bf16),
            pltpu.VMEM(ocean_down.shape, bf16),
            pltpu.VMEM(waves.shape, bf16),
            pltpu.VMEM(waves.shape, bf16),
            pltpu.VMEM((2 * STENCIL_TAPS * STENCIL_TAPS, 1, sea_width), f32),
            pltpu.VMEM((128, 128), f32),
            pltpu.VMEM((rows, cols, 128), f32),
            pltpu.VMEM((2, 2, rows, lon_dev, surface), bf16),
            pltpu.VMEM((2, 2, rows, lon_dev, surface), bf16),
            pltpu.VMEM(atm_state.shape, f32),
            pltpu.VMEM(atm_state.shape, bf16),
            pltpu.VMEM((col_count, band, lon_dev, width), bf16),
            pltpu.VMEM(tall, bf16),
            pltpu.VMEM(tall, bf16),
            pltpu.VMEM((width // 128, devices * band * 8, 128), f32),
            pltpu.VMEM(tall, bf16),
            pltpu.VMEM((col_count, band, lon_dev, width), bf16),
            pltpu.VMEM(atm_state.shape, bf16),
            pltpu.VMEM((4, 6) + squares, bf16),
            pltpu.VMEM((3, 6) + squares, bf16),
            pltpu.VMEM((2,) + squares, bf16),
            pltpu.VMEM((2, 2) + squares, bf16),
            pltpu.VMEM((slots, 2, lat_total, lat_total), bf16),
            pltpu.VMEM((slots, lat_total, lat_total), bf16),
            pltpu.VMEM((2,) + ocean_state.shape, bf16),
            pltpu.VMEM((2, 2, reach, cols, sea_width), bf16),
            pltpu.VMEM((2, rows + 2 * reach, 16, sea_width), bf16),
            pltpu.VMEM((rows + 2 * reach, cols + 16, sea_width), f32),
            pltpu.VMEM((2 * cols, sea_width), f32),
            dma((11,)),
            dma((2,)),
            dma((2, 2)),
            dma((2, 3)),
            dma((2, devices)),
            dma((2, devices)),
            dma((2, 3)),
            dma((2, 5)),
            dma((2, 2, 5)),
        ],
        compiler_params=pltpu.CompilerParams(
            collective_id=0, has_side_effects=True, vmem_limit_bytes=60 * 1024 * 1024
        ),
    )(
        atm_state,
        ocean_state,
        wet_mask,
        legendre,
        quad_weight[None, :],
        spec_real,
        spec_imag,
        degree_gain[:, None],
        atm_gain,
        atm_up,
        atm_down,
        atm_to_surface,
        surface_to_atm,
        ocean_to_surface,
        surface_to_ocean,
        ocean_kernel,
        ocean_gain,
        ocean_up,
        ocean_down,
        waves,
        waves_back,
    )


def local(
    atm_state,
    ocean_state,
    wet_mask,
    legendre,
    quad_weight,
    spec_real,
    spec_imag,
    degree_gain,
    atm_gain,
    atm_up,
    atm_down,
    atm_to_surface,
    surface_to_atm,
    ocean_to_surface,
    surface_to_ocean,
    ocean_kernel,
    ocean_gain,
    ocean_up,
    ocean_down,
):
    col_count = lax.axis_size(COLUMNS)
    lat_dev, lon_dev, _ = atm_state.shape
    circle = lon_dev * col_count
    if fits(atm_state, ocean_state, legendre):
        return whole_step(
            atm_state,
            ocean_state,
            wet_mask,
            legendre,
            quad_weight,
            spec_real,
            spec_imag,
            degree_gain,
            atm_gain,
            atm_up,
            atm_down,
            atm_to_surface,
            surface_to_atm,
            ocean_to_surface,
            surface_to_ocean,
            ocean_kernel,
            ocean_gain,
            ocean_up,
            ocean_down,
        )
    wet = wet_mask.astype(jnp.float32)[:, :, None]
    ocean_flux = (
        jnp.dot(ocean_state, ocean_to_surface, preferred_element_type=jnp.float32) * wet
    ).astype(jnp.bfloat16)
    atm_flux = jnp.dot(atm_state, atm_to_surface, preferred_element_type=jnp.float32).astype(
        jnp.bfloat16
    )
    flux_here = lax.all_to_all(ocean_flux, "comp", split_axis=1, concat_axis=0, tiled=True)
    flux_sea = lax.all_to_all(atm_flux, "comp", split_axis=0, concat_axis=1, tiled=True)
    forced = atm_state.astype(jnp.float32) + jnp.dot(
        flux_here, surface_to_atm, preferred_element_type=jnp.float32
    )
    normed = layer_norm(forced, atm_gain[0]).astype(jnp.bfloat16)
    run_spectral = (
        folded_spectral
        if folds(circle, lat_dev, col_count, lax.axis_size(EVERY))
        else plain_spectral
    )
    spectral, stages = run_spectral(
        normed, legendre, quad_weight, spec_real, spec_imag, degree_gain, circle
    )
    mixed = forced + spectral.astype(jnp.float32)
    normed_two = layer_norm(mixed, atm_gain[1]).astype(jnp.bfloat16)
    hidden = jax.nn.gelu(jnp.dot(normed_two, atm_up, preferred_element_type=jnp.float32)).astype(
        jnp.bfloat16
    )
    atm_out = (mixed + jnp.dot(hidden, atm_down, preferred_element_type=jnp.float32)).astype(
        jnp.bfloat16
    )
    ocean_in = (
        ocean_state.astype(jnp.float32)
        + wet * jnp.dot(flux_sea, surface_to_ocean, preferred_element_type=jnp.float32)
    ).astype(jnp.bfloat16)
    stencil_reach = STENCIL_TAPS // 2 * OCEAN_DILATION
    sides = ((("lat", "comp"), 0), ("lon", 1))
    current = ocean_in
    quick = ocean_in.shape[0] % (2 * OCEAN_DILATION) == 0 and ocean_in.shape[2] % 128 == 0
    for k in range(2):
        field = padded(current, sides, stencil_reach)
        weights = (ocean_kernel[k], ocean_gain[k], ocean_up[k], ocean_down[k])
        if quick:
            current = fast_ocean_block(field, *weights, stages[k])
        else:
            current = ocean_block(field, *weights)
    ocean_out = jnp.where(wet_mask[:, :, None] == 1, current, ocean_state)
    return (atm_out, ocean_out)


def solution(mesh):
    placed = (
        P("lat", ("lon", "comp"), None),
        P(("lat", "comp"), "lon", None),
        P(("lat", "comp"), "lon"),
        P(("lat", "lon", "comp"), None, None),
        P(),
        P(),
        P(),
        P(),
        P(),
        P(),
        P(),
        P(),
        P(),
        P(),
        P(),
        P(),
        P(),
        P(),
        P(),
    )

    return jax.shard_map(
        local,
        mesh=mesh,
        in_specs=placed,
        out_specs=(P("lat", ("lon", "comp"), None), P(("lat", "comp"), "lon", None)),
        check_vma=False,
    )
```

```python
import functools
import math

import jax
import jax.numpy as jnp
import numpy as np
from jax import lax
from jax.experimental import pallas as pl
from jax.experimental.pallas import tpu as pltpu
from jax.sharding import PartitionSpec as P

MODES = 512
STENCIL_TAPS = 7
OCEAN_DILATION = 2
COLUMNS = ("lon", "comp")
EVERY = ("lat", "lon", "comp")


epsilon = 1e-05


def padded(block, sides, width):
    for axis, dim in sides:
        count = lax.axis_size(axis)
        forward = [(i, i + 1) for i in range(count - 1)]
        backward = [(target, source) for source, target in forward]
        low = lax.ppermute(
            lax.slice_in_dim(block, block.shape[dim] - width, None, axis=dim), axis, forward
        )
        high = lax.ppermute(lax.slice_in_dim(block, 0, width, axis=dim), axis, backward)
        block = jnp.concatenate([low, block, high], axis=dim)
    return block


def layer_norm(values, gain):
    centred = values - jnp.mean(values, axis=-1, keepdims=True)
    spread = jnp.mean(centred * centred, axis=-1, keepdims=True)
    return centred * lax.rsqrt(spread + epsilon) * gain


def wave_table(row_index, circle):
    longitude = jnp.arange(circle, dtype=jnp.int32)
    wavenumber = row_index // 2
    phases = wavenumber[:, None] * longitude[None, :] % circle
    angles = phases.astype(jnp.float32) * (2.0 * math.pi / circle)
    waves = jnp.where((row_index % 2 == 0)[:, None], jnp.cos(angles), -jnp.sin(angles))
    return (wavenumber, waves)


def forward_table(row_index, circle):
    _, waves = wave_table(row_index, circle)
    return (waves.T / math.sqrt(circle)).astype(jnp.bfloat16)


def inverse_table(row_index, circle):
    wavenumber, waves = wave_table(row_index, circle)
    factor = jnp.where(wavenumber == 0, 1.0, 2.0).astype(jnp.float32)
    return (waves * factor[:, None] / math.sqrt(circle)).astype(jnp.bfloat16)


def reorder_rows(total_rows, owned, lat_count, col_count):
    positions = jnp.arange(total_rows, dtype=jnp.int32)
    stride = lat_count * owned
    return (
        owned * (positions % stride // owned * col_count + positions // stride) + positions % owned
    )


def spectral_filter(gathered, table, quad_weight, spec_real, spec_imag, degree_gain):
    count = table.shape[0]
    lat_total = table.shape[2]
    channels = gathered.shape[2]
    split_parts = gathered.reshape(lat_total, count, 2, channels)
    weighted = (table.astype(jnp.float32) * (quad_weight / lat_total)).astype(jnp.bfloat16)
    coeffs = jnp.einsum(
        "mln,nmpc->mplc", weighted, split_parts, preferred_element_type=jnp.float32
    ).astype(jnp.bfloat16)
    real_part = coeffs[:, 0]
    imag_part = coeffs[:, 1]
    mixed_real = jnp.dot(real_part, spec_real, preferred_element_type=jnp.float32) - jnp.dot(
        imag_part, spec_imag, preferred_element_type=jnp.float32
    )
    mixed_imag = jnp.dot(real_part, spec_imag, preferred_element_type=jnp.float32) + jnp.dot(
        imag_part, spec_real, preferred_element_type=jnp.float32
    )
    scaled = (jnp.stack([mixed_real, mixed_imag], axis=1) * degree_gain[:, None]).astype(
        jnp.bfloat16
    )
    returned = jnp.einsum(
        "mln,mplc->nmpc", table, scaled, preferred_element_type=jnp.float32
    ).astype(jnp.bfloat16)
    return returned.reshape(lat_total, 2 * count, channels)


def folds(circle, lat_dev, col_count, devices):
    return (
        MODES == 2 * circle
        and lat_dev % col_count == 0
        and devices % 4 == 0
        and (circle // 2) % devices == 0
        and (MODES // devices) % 4 == 0
    )


def place_of(kind, i, group):
    return kind * group + (group - 1 - i if kind % 2 else i)


def folded_waves(circle, devices):
    longitude = jnp.arange(circle, dtype=jnp.int32)
    position = jnp.arange(circle, dtype=jnp.int32)
    group = devices // 4
    owned = circle // devices
    owner = position // owned
    kind, place = owner // group, owner % group
    place = jnp.where(kind % 2 == 1, group - 1 - place, place)
    row_index = (4 * place + kind) * owned + position % owned
    wavenumber = jnp.where(row_index == 1, circle // 2, row_index // 2)
    phases = wavenumber[:, None] * longitude[None, :] % circle
    angles = phases.astype(jnp.float32) * (2.0 * math.pi / circle)
    cosine = ((row_index % 2 == 0) | (row_index == 1))[:, None]
    return jnp.where(cosine, jnp.cos(angles), -jnp.sin(angles)) / math.sqrt(circle)


def folded_operators(table, quad_weight, degree_gain):
    devices = lax.axis_size(EVERY)
    me = lax.axis_index(EVERY)
    count, _, lat_total = table.shape
    group = devices // 4
    part = count // 4
    family = me // group
    scaled = (table.astype(jnp.float32) * degree_gain[:, None]).astype(jnp.bfloat16)
    operators = jnp.einsum(
        "mlt,mlu->mtu", table, scaled, preferred_element_type=jnp.float32
    )
    operators = operators * (quad_weight / lat_total)
    first_scale = jnp.where(me == 0, 0.5, 1.0).astype(jnp.float32)
    scales = jnp.where(jnp.arange(count) == 0, first_scale, 1.0)
    operators = (operators * scales[:, None, None]).astype(jnp.bfloat16)
    turn = []
    for base in (group, 3 * group):
        for i in range(group):
            turn.append((base + (i + 1) % group, base + i))
    rotated = lax.ppermute(operators[:1], EVERY, turn)
    mirrored = jnp.concatenate([rotated, jnp.flip(operators[1:], axis=0)], axis=0)
    ordered = jnp.where(family % 2 == 1, mirrored, operators)
    received = [lax.dynamic_slice_in_dim(ordered, family * part, part, axis=0)]
    for shift in range(1, 4):
        pairs = []
        for i in range(group):
            for kind in range(4):
                pairs.append((place_of(kind, i, group), place_of(kind ^ shift, i, group)))
        piece = lax.dynamic_slice_in_dim(ordered, (family ^ shift) * part, part, axis=0)
        received.append(lax.ppermute(piece, EVERY, pairs))
    received = [value.astype(jnp.float32) for value in received]
    same = received[0] + received[2]
    other = received[1] + received[3]
    direct = jnp.where(family % 2 == 0, same, other)
    mirror = jnp.where(family % 2 == 0, other, same)
    lone = ((me == 0) & (jnp.arange(part) == 0))[:, None, None]
    both = direct + mirror
    gap = jnp.where(lone, 0.0, direct - mirror)
    top = jnp.concatenate([jnp.where(lone, direct, both), -gap], axis=2)
    bottom = jnp.concatenate([gap, jnp.where(lone, mirror, both)], axis=2)
    return (2.0 * top).astype(jnp.bfloat16), (2.0 * bottom).astype(jnp.bfloat16)


def folded_spectral(normed, legendre, quad_weight, spec_real, spec_imag, degree_gain, circle):
    width = normed.shape[2]
    top, bottom = folded_operators(legendre, quad_weight, degree_gain)
    slots = top.shape[0]
    waves = folded_waves(circle, lax.axis_size(EVERY)).astype(jnp.bfloat16)
    columns = lax.all_to_all(normed, COLUMNS, split_axis=0, concat_axis=1, tiled=True)
    spectrum = jnp.einsum(
        "rn,tnc->trc", waves, columns, preferred_element_type=jnp.float32
    ).astype(jnp.bfloat16)
    gathered = lax.all_to_all(spectrum, EVERY, split_axis=1, concat_axis=0, tiled=True)
    lat_total = gathered.shape[0]
    channels = jnp.concatenate([spec_real, spec_imag], axis=1)
    turned = gathered.reshape(lat_total, slots, 2, width).transpose(1, 2, 0, 3)
    mixed = jnp.dot(turned, channels, preferred_element_type=jnp.float32).astype(jnp.bfloat16)
    upper = jnp.concatenate([mixed[:, 0, :, :width], mixed[:, 1, :, width:]], axis=1)
    lower = jnp.concatenate([mixed[:, 0, :, width:], mixed[:, 1, :, :width]], axis=1)
    cosine = jnp.einsum("stu,suc->stc", top, upper, preferred_element_type=jnp.float32)
    sine = jnp.einsum("stu,suc->stc", bottom, lower, preferred_element_type=jnp.float32)
    filtered = jnp.stack([cosine, sine], axis=1).astype(jnp.bfloat16)
    filtered = filtered.reshape(2 * slots, lat_total, width).transpose(1, 0, 2)
    returned = lax.all_to_all(filtered, EVERY, split_axis=0, concat_axis=1, tiled=True)
    spatial = jnp.einsum(
        "rn,trc->tnc", waves, returned, preferred_element_type=jnp.float32
    ).astype(jnp.bfloat16)
    spectral = lax.all_to_all(spatial, COLUMNS, split_axis=1, concat_axis=0, tiled=True)
    return spectral, (spectrum, filtered)


def plain_spectral(normed, legendre, quad_weight, spec_real, spec_imag, degree_gain, circle):
    lat_count = lax.axis_size("lat")
    col_count = lax.axis_size(("lon", "comp"))
    total_rows = 2 * MODES
    owned = 2 * legendre.shape[0]
    natural = jnp.arange(total_rows, dtype=jnp.int32)
    columns = lax.all_to_all(normed, ("lon", "comp"), split_axis=2, concat_axis=1, tiled=True)
    forward = forward_table(natural, circle)
    inverse = inverse_table(reorder_rows(total_rows, owned, lat_count, col_count), circle)
    spectrum = jnp.einsum(
        "anc,nr->arc", columns, forward, preferred_element_type=jnp.float32
    ).astype(jnp.bfloat16)
    gathered = lax.all_to_all(
        lax.all_to_all(spectrum, "lat", split_axis=1, concat_axis=0, tiled=True),
        ("lon", "comp"),
        split_axis=1,
        concat_axis=2,
        tiled=True,
    )
    filtered = spectral_filter(gathered, legendre, quad_weight, spec_real, spec_imag, degree_gain)
    returned = lax.all_to_all(
        lax.all_to_all(filtered, "lat", split_axis=0, concat_axis=1, tiled=True),
        ("lon", "comp"),
        split_axis=2,
        concat_axis=1,
        tiled=True,
    )
    spatial = jnp.einsum(
        "arc,rn->anc", returned, inverse, preferred_element_type=jnp.float32
    ).astype(jnp.bfloat16)
    spectral = lax.all_to_all(spatial, COLUMNS, split_axis=1, concat_axis=2, tiled=True)
    return spectral, (spectrum, filtered)


def ocean_block(padded_field, kernel, gain, up_weight, down_weight):
    stencil_reach = STENCIL_TAPS // 2 * OCEAN_DILATION
    tile_height = padded_field.shape[0] - 2 * stencil_reach
    tile_breadth = padded_field.shape[1] - 2 * stencil_reach
    stencil = jnp.zeros((tile_height, tile_breadth, padded_field.shape[2]), jnp.float32)
    for row_offset_tap in range(STENCIL_TAPS):
        for column_tap in range(STENCIL_TAPS):
            stencil_window = padded_field[
                row_offset_tap * OCEAN_DILATION : row_offset_tap * OCEAN_DILATION + tile_height,
                column_tap * OCEAN_DILATION : column_tap * OCEAN_DILATION + tile_breadth,
            ]
            stencil = stencil + stencil_window.astype(jnp.float32) * kernel[
                row_offset_tap, column_tap
            ].astype(jnp.float32)
    normed = layer_norm(stencil, gain).astype(jnp.bfloat16)
    hidden = jax.nn.gelu(jnp.dot(normed, up_weight, preferred_element_type=jnp.float32)).astype(
        jnp.bfloat16
    )
    centre = padded_field[
        stencil_reach : stencil_reach + tile_height, stencil_reach : stencil_reach + tile_breadth
    ]
    return (
        centre.astype(jnp.float32)
        + jnp.dot(hidden, down_weight, preferred_element_type=jnp.float32)
    ).astype(jnp.bfloat16)


def ocean_kernel_body(
    field_ref, taps_ref, gain_ref, up_ref, down_ref, after_ref, out_ref, wide, normed
):
    rows, cols, width = out_ref.shape
    step = OCEAN_DILATION
    lanes = 128

    @pl.loop(0, rows + (STENCIL_TAPS - 1) * step)
    def _(row):
        wide[row] = field_ref[row].astype(jnp.float32)

    @pl.loop(0, rows // 2)
    def _(pair):
        base = pair // step * (2 * step) + pair % step
        for half in range(width // lanes):
            part = slice(half * lanes, (half + 1) * lanes)
            sums = [jnp.zeros((cols, lanes), jnp.float32) for _ in range(2)]
            for a in range(STENCIL_TAPS + 1):
                for b in range(STENCIL_TAPS):
                    window = wide[base + a * step, b * step : b * step + cols, part]
                    for which in range(2):
                        tap = a - which
                        if 0 <= tap < STENCIL_TAPS:
                            weight = taps_ref[tap * STENCIL_TAPS + b, :, part]
                            sums[which] = sums[which] + window * weight
            for which in range(2):
                normed[which * cols : (which + 1) * cols, part] = sums[which]
        stencil = normed[...]
        values = layer_norm(stencil, gain_ref[...]).astype(jnp.bfloat16)
        hidden = jax.nn.gelu(
            jnp.dot(values, up_ref[...], preferred_element_type=jnp.float32)
        ).astype(jnp.bfloat16)
        moved = jnp.dot(hidden, down_ref[...], preferred_element_type=jnp.float32)
        reach = STENCIL_TAPS // 2 * step
        for which in range(2):
            row = base + which * step
            centre = wide[row + reach, reach : reach + cols, :]
            out_ref[row] = (centre + moved[which * cols : (which + 1) * cols]).astype(
                out_ref.dtype
            )


def fast_ocean_block(field, kernel, gain, up_weight, down_weight, after):
    reach = STENCIL_TAPS // 2 * OCEAN_DILATION
    rows, cols, width = field.shape[0] - 2 * reach, field.shape[1] - 2 * reach, field.shape[2]
    hidden = up_weight.shape[1]
    taps = kernel.astype(jnp.float32).reshape(STENCIL_TAPS * STENCIL_TAPS, 1, width)
    whole = pl.BlockSpec(memory_space=pltpu.VMEM)
    cells = rows * cols
    return pl.pallas_call(
        ocean_kernel_body,
        out_shape=jax.ShapeDtypeStruct((rows, cols, width), jnp.bfloat16),
        in_specs=[whole] * 5 + [pl.BlockSpec(memory_space=pl.ANY)],
        out_specs=whole,
        scratch_shapes=[
            pltpu.VMEM(field.shape, jnp.float32),
            pltpu.VMEM((2 * cols, width), jnp.float32),
        ],
        compiler_params=pltpu.CompilerParams(vmem_limit_bytes=32 * 1024 * 1024),
        cost_estimate=pl.CostEstimate(
            flops=4 * cells * width * hidden + 98 * cells * width * 64,
            bytes_accessed=4 * field.size + 4 * up_weight.size,
            transcendentals=cells * hidden,
        ),
    )(field, taps, gain[None, :], up_weight, down_weight, after)


MESH_ID = pl.DeviceIdType.MESH


def fits(atm_state, ocean_state, legendre):
    devices = lax.axis_size(EVERY)
    col_count = lax.axis_size(COLUMNS)
    lat_dev, lon_dev, width = atm_state.shape
    rows, cols, sea_width = ocean_state.shape
    circle = lon_dev * col_count
    reach = STENCIL_TAPS // 2 * OCEAN_DILATION
    return (
        folds(circle, lat_dev, col_count, devices)
        and lax.axis_size("lon") == 2
        and lax.axis_size("comp") == 2
        and circle // devices == 8
        and legendre.shape[0] == 16
        and lat_dev // col_count % 2 == 0
        and lat_dev == 2 * rows
        and cols == 2 * lon_dev
        and cols == 128
        and rows == 2 * reach
        and reach % 2 == 0
        and rows % (2 * OCEAN_DILATION) == 0
        and 128 < legendre.shape[2] <= 192
        and legendre.shape[2] % 16 == 0
        and lon_dev % 16 == 0
        and width % 128 == 0
        and sea_width == 256
    )


def whole_step_body(
    lat_total,
    atm_hbm,
    sea_hbm,
    wet_ref,
    legendre_hbm,
    quad_ref,
    real_hbm,
    imag_hbm,
    degree_ref,
    gain_ref,
    up_hbm,
    down_hbm,
    to_sea_ref,
    from_sea_ref,
    to_air_ref,
    from_air_ref,
    taps_in_ref,
    sea_gain_ref,
    sea_up_hbm,
    sea_down_hbm,
    waves_hbm,
    waves_back_hbm,
    air_out,
    sea_out,
    air,
    sea,
    legendre,
    spec_real,
    spec_imag,
    air_up,
    air_down,
    sea_up,
    sea_down,
    waves,
    waves_back,
    taps,
    wet_square,
    wet_full,
    flux_out,
    flux_in,
    forced,
    normed,
    columns,
    spec_send,
    gathered,
    flat,
    turned_rows,
    mixed_real,
    mixed_imag,
    filtered,
    returned,
    spatial,
    spectral,
    op_send,
    op_recv,
    op_own,
    op_lone,
    op_lone_recv,
    both,
    gap,
    field,
    edges,
    strips,
    sides,
    wide,
    stencil,
    load_sem,
    local_sem,
    flux_sem,
    column_sem,
    column_own,
    owner_sem,
    owner_own,
    back_sem,
    back_own,
    grid_sem,
    grid_own,
    op_sem,
    halo_sem,
):
    f32, bf16 = jnp.float32, jnp.bfloat16
    lat = lax.axis_index("lat")
    lon = lax.axis_index("lon")
    comp = lax.axis_index("comp")
    col_count = lax.axis_size(COLUMNS)
    devices = lax.axis_size(EVERY)
    group = devices // 4
    col = lon * 2 + comp
    me = lat * col_count + col
    tile = lat * 2 + comp
    tiles = lax.axis_size("lat") * 2
    lat_dev, lon_dev, width = air.shape
    rows, cols, sea_width = sea.shape
    band = lat_dev // col_count
    pairs = band // 2
    circle = lon_dev * col_count
    step = OCEAN_DILATION
    reach = STENCIL_TAPS // 2 * step
    slots = both.shape[0]

    def at_device(index):
        return (index // col_count, index % col_count // 2, index % 2)

    def at_tile(index, side):
        return (index // 2, side, index % 2)

    def remote(source, target, sems, k, where):
        place_in = k if isinstance(k, tuple) else (k,)
        return pltpu.make_async_remote_copy(
            src_ref=source,
            dst_ref=target,
            send_sem=sems.at[(0,) + place_in],
            recv_sem=sems.at[(1,) + place_in],
            device_id=where,
            device_id_type=MESH_ID,
        )

    def across(left, right):
        return lax.dot_general(left, right, (((1,), (1,)), ((), ())), preferred_element_type=f32)

    barrier = pltpu.get_barrier_semaphore()

    @pl.loop(1, devices)
    def _(k):
        pl.semaphore_signal(
            barrier, inc=1, device_id=at_device((me + k) % devices), device_id_type=MESH_ID
        )

    loads = {}
    for index, (name, source, target) in enumerate(
        (
            ("legendre", legendre_hbm, legendre),
            ("sea", sea_hbm, sea),
            ("air", atm_hbm, air),
            ("waves", waves_hbm, waves),
            ("sea_up", sea_up_hbm, sea_up),
            ("sea_down", sea_down_hbm, sea_down),
            ("real", real_hbm, spec_real),
            ("imag", imag_hbm, spec_imag),
            ("back", waves_back_hbm, waves_back),
            ("up", up_hbm, air_up),
            ("down", down_hbm, air_down),
        )
    ):
        loads[name] = pltpu.make_async_copy(source, target, load_sem.at[index])
    for name in ("legendre", "sea", "air"):
        loads[name].start()

    wet_square[...] = jnp.zeros_like(wet_square)
    wet_square[0:rows, :] = wet_ref[...].astype(f32)
    turned = jnp.transpose(wet_square[...])
    for i in range(rows):
        wet_full[i] = jnp.broadcast_to(turned[:, i : i + 1], (cols, 128))

    for a in range(STENCIL_TAPS):
        for b in range(STENCIL_TAPS):
            line = taps_in_ref[a, b].astype(f32)
            for k in range(2):
                taps[(k * STENCIL_TAPS + a) * STENCIL_TAPS + b] = line[k : k + 1]

    loads["legendre"].wait()
    kind = me // group
    odd = kind % 2
    place = me % group
    count = legendre.shape[0]
    edge = lat_total - 128
    row_at = lax.broadcasted_iota(jnp.int32, (lat_total, lat_total), 0)
    lane_at = lax.broadcasted_iota(jnp.int32, (lat_total, lat_total), 1)
    upper, diagonal = row_at <= lane_at, row_at == lane_at

    def operator(k):
        index = odd * ((count - k) % count) + (1 - odd) * k
        table = legendre[index]
        scaled = (table.astype(f32) * degree_ref[...]).astype(bf16)
        return across(table, scaled) * jnp.where((me == 0) & (index == 0), 0.5, 1.0).astype(f32)

    @pl.loop(0, 4)
    def _(which):
        tails, marks = [], []
        for spot in range(2):
            first, second = operator(4 * which + 2 * spot), operator(4 * which + 2 * spot + 1)
            square = jnp.where(upper, first, second).astype(bf16)
            op_send[which, spot * lat_total : (spot + 1) * lat_total] = square[:, 0:128]
            tails.append(square[:, 128:lat_total])
            line = jnp.sum(jnp.where(diagonal, second, 0.0), axis=0, keepdims=True)
            marks.append(line[:, 0:128])
            marks.append(
                jnp.concatenate([line[:, 128:lat_total], jnp.zeros((1, 128 - edge), f32)], axis=1)
            )

            @pl.when(which == kind)
            def _():
                op_own[2 * spot] = first.astype(bf16)
                op_own[2 * spot + 1] = second.astype(bf16)

            if spot == 0:

                @pl.when(which == 0)
                def _():
                    op_lone[0] = first[:, 0:128].astype(bf16)
                    op_lone[1, :, 0:edge] = first[:, 128:lat_total].astype(bf16)

        op_send[which, 2 * lat_total : 3 * lat_total, 0 : 2 * edge] = jnp.concatenate(tails, axis=1)
        at = lax.broadcasted_iota(jnp.int32, (16, 128), 0)
        lines = jnp.zeros((16, 128), f32)
        for i in range(4):
            lines = jnp.where(at == i, marks[i], lines)
        op_send[which, 3 * lat_total : 3 * lat_total + 16] = lines.astype(bf16)

    pl.semaphore_wait(barrier, devices - 1)
    spot_of = odd * (group - 1 - place) + (1 - odd) * place
    op_moves = []
    for shift, other in ((2, (kind + 2) % 4), (3, 3 - kind), (1, kind + 1 - 2 * odd)):
        other_odd = other % 2
        there = other * group + other_odd * (group - 1 - spot_of) + (1 - other_odd) * spot_of
        move = remote(
            op_send.at[other], op_recv.at[shift - 1], op_sem, shift - 1, at_device(there)
        )
        move.start()
        op_moves.append(move)
    lone_move = remote(
        op_lone, op_lone_recv.at[kind // 2], op_sem, 3 + kind // 2, at_device((group - place) % group)
    )

    @pl.when(odd == 1)
    def _():
        lone_move.start()

    loads["sea"].wait()

    @pl.loop(0, rows)
    def _(i):
        flux = across(sea[i], to_air_ref[...])
        flux = (flux * wet_full[i][:, 0 : flux.shape[1]]).astype(bf16)
        flux_out[0, 0, i] = flux[0:lon_dev]
        flux_out[0, 1, i] = flux[lon_dev : 2 * lon_dev]

    partner = (lat, lon, 1 - comp)
    moves = []
    for part in range(2):
        moves.append(
            remote(flux_out.at[part, 1 - comp], flux_in.at[part, comp], flux_sem, part, partner)
        )
    moves[0].start()
    loads["air"].wait()

    @pl.loop(0, rows // 2)
    def _(i):
        for half in range(2):
            block_of = air[pl.ds(half * rows + 2 * i, 2)].reshape(2 * lon_dev, width)
            flux = across(block_of, to_sea_ref[...]).astype(bf16)
            flux_out[1, half, 2 * i] = flux[0:lon_dev]
            flux_out[1, half, 2 * i + 1] = flux[lon_dev : 2 * lon_dev]

    moves[1].start()
    kept = []
    for part in range(2):
        kept.append(
            pltpu.make_async_copy(
                flux_out.at[part, comp], flux_in.at[part, comp], local_sem.at[part]
            )
        )
        kept[-1].start()
    for name in (
        "waves", "sea_up", "sea_down", "real", "imag", "back", "up", "down"
    ):
        loads[name].start()
    for move in kept:
        move.wait()
    moves[0].wait()


    def column_moves(p):
        found = []
        for k in range(1, col_count):
            other = (col + k) % col_count
            found.append(
                remote(
                    normed.at[p, other],
                    columns.at[p, col],
                    column_sem,
                    (p, k - 1),
                    (lat, other // 2, other % 2),
                )
            )
        own = pltpu.make_async_copy(normed.at[p, col], columns.at[p, col], column_own.at[p])
        return found + [own]

    half_block = 2 * lon_dev
    for p in range(pairs):

        @pl.loop(0, col_count // 2)
        def _(jj):
            for j2 in range(2):
                j = 2 * jj + j2
                row = band * j + 2 * p
                flux = flux_in[0, row // rows, pl.ds(row % rows, 2)].reshape(half_block, -1)
                value = air[pl.ds(row, 2)].reshape(half_block, width).astype(f32)
                value = value + jnp.dot(flux, from_sea_ref[...], preferred_element_type=f32)
                forced[p, j] = value.reshape(2, lon_dev, width)
                value = layer_norm(value, gain_ref[0:1]).astype(bf16)
                normed[p, j] = value.reshape(2, lon_dev, width)

        for move in column_moves(p):
            move.start()

    moves[1].wait()

    @pl.loop(0, rows)
    def _(i):
        flux = jnp.concatenate([flux_in[1, 0, i], flux_in[1, 1, i]], axis=0)
        added = jnp.dot(flux, from_air_ref[...], preferred_element_type=f32)
        mask = wet_full[i]
        mask = jnp.concatenate([mask, mask], axis=1)
        field[0, i] = (sea[i].astype(f32) + mask * added).astype(bf16)

    half_reach = reach // 2

    def pack_strips(k):
        @pl.loop(0, rows // 2)
        def _(i):
            found = []
            for which in range(2):
                low = field[k, 2 * i + which, 0:16].astype(f32)
                high = field[k, 2 * i + which, cols - 16 : cols].astype(f32)
                found.append(jnp.where(lon == 0, high[8:16], low[0:8]))
            strips[k, i] = jnp.concatenate(found, axis=0).astype(bf16)

    def halo_moves(k):
        source, strip = field.at[k], strips.at[k]
        low, high = pl.ds(0, reach), pl.ds(rows - reach, reach)
        sems = halo_sem.at[k]
        side = remote(
            strip, sides.at[k, pl.ds(half_reach, rows // 2)], sems, 0, at_tile(tile, 1 - lon)
        )
        back = (
            remote(source.at[low], edges.at[k, 1], sems, 1, at_tile(tile - 1, lon)),
            remote(
                strip.at[pl.ds(0, half_reach)],
                sides.at[k, pl.ds(half_reach + rows // 2, half_reach)],
                sems,
                2,
                at_tile(tile - 1, 1 - lon),
            ),
        )
        ahead = (
            remote(source.at[high], edges.at[k, 0], sems, 3, at_tile(tile + 1, lon)),
            remote(
                strip.at[pl.ds(rows // 2 - half_reach, half_reach)],
                sides.at[k, pl.ds(0, half_reach)],
                sems,
                4,
                at_tile(tile + 1, 1 - lon),
            ),
        )
        return side, back, ahead

    def send_halo(k):
        pack_strips(k)
        side, back, ahead = halo_moves(k)

        @pl.when(tile > 0)
        def _():
            for move in back:
                move.start()

        @pl.when(tile < tiles - 1)
        def _():
            for move in ahead:
                move.start()

        side.start()

    def take_halo(k):
        @pl.loop(0, rows)
        def _(i):
            wide[reach + i, 8 : cols + 8] = field[k, i].astype(f32)

        side, back, ahead = halo_moves(k)
        side.wait()

        @pl.when(tile > 0)
        def _():
            for move in back:
                move.wait_send()
            for move in ahead:
                move.wait_recv()

        @pl.when(tile < tiles - 1)
        def _():
            for move in ahead:
                move.wait_send()
            for move in back:
                move.wait_recv()

        def margins(first, pair, values):
            for which in range(2):
                part = values[8 * which : 8 * which + 8]
                wide[first + 2 * pair + which, 0:8] = jnp.where(lon == 1, part, 0.0)
                wide[first + 2 * pair + which, cols + 8 : cols + 16] = jnp.where(
                    lon == 0, part, 0.0
                )

        @pl.loop(0, rows // 2)
        def _(i):
            margins(reach, i, sides[k, half_reach + i].astype(f32))

        for which in range(2):
            first = which * (reach + rows)
            present = tile > 0 if which == 0 else tile < tiles - 1

            @pl.when(present)
            def _():
                @pl.loop(0, reach)
                def _(i):
                    wide[first + i, 8 : cols + 8] = edges[k, which, i].astype(f32)

                @pl.loop(0, half_reach)
                def _(i):
                    margins(first, i, sides[k, first // 2 + i].astype(f32))

            @pl.when(jnp.logical_not(present))
            def _():
                @pl.loop(0, reach)
                def _(i):
                    wide[first + i] = jnp.zeros(wide.shape[1:], f32)

    send_halo(0)

    def sea_pairs(k, first, last):
        @pl.loop(first, last)
        def _(pair):
            base = pair // step * (2 * step) + pair % step
            for half in range(sea_width // 128):
                part = slice(half * 128, (half + 1) * 128)
                sums = [jnp.zeros((cols, 128), f32) for _ in range(2)]
                for a in range(STENCIL_TAPS + 1):
                    for b in range(STENCIL_TAPS):
                        start = 8 - reach + b * step
                        window = wide[base + a * step, start : start + cols, part]
                        for which in range(2):
                            tap = a - which
                            if 0 <= tap < STENCIL_TAPS:
                                weight = taps[
                                    (k * STENCIL_TAPS + tap) * STENCIL_TAPS + b, :, part
                                ]
                                sums[which] = sums[which] + window * weight
                for which in range(2):
                    stencil[which * cols : (which + 1) * cols, part] = sums[which]
            values = layer_norm(stencil[...], sea_gain_ref[k : k + 1]).astype(bf16)
            hidden = jax.nn.gelu(
                jnp.dot(values, sea_up[k], preferred_element_type=f32)
            ).astype(bf16)
            moved = jnp.dot(hidden, sea_down[k], preferred_element_type=f32)
            for which in range(2):
                row = base + which * step
                centre = wide[row + reach, 8 : 8 + cols, :]
                value = (centre + moved[which * cols : (which + 1) * cols]).astype(bf16)
                if k == 0:
                    field[1, row] = value
                else:
                    mask = wet_full[row]
                    mask = jnp.concatenate([mask, mask], axis=1)
                    sea_out[row] = jnp.where(mask > 0.5, value, sea[row])

    def exchange(source, target, sems, own_sems):
        def away(p, k):
            other = (me + k) % devices
            return remote(
                source.at[p, other], target.at[p, me], sems, (p, k), at_device(other)
            )

        def own(p):
            return pltpu.make_async_copy(source.at[p, me], target.at[p, me], own_sems.at[p])

        def start(p):
            @pl.loop(1, devices)
            def _(k):
                away(p, k).start()

            own(p).start()

        def wait(p):
            own(p).wait()

            @pl.loop(1, devices)
            def _(k):
                away(p, k).wait()

        return start, wait

    start_owner, wait_owner = exchange(spec_send, gathered, owner_sem, owner_own)
    loads["waves"].wait()

    for p in range(pairs):
        for move in column_moves(p):
            move.wait()
        found = []
        for which in range(2):
            lines = jnp.concatenate([columns[p, b, which] for b in range(col_count)], axis=0)
            value = jnp.dot(waves[...], lines, preferred_element_type=f32)
            found.append(value.reshape(devices, 8, width))
        spec_send[p] = jnp.concatenate(found, axis=1).astype(bf16)
        start_owner(p)

    take_halo(0)
    loads["sea_up"].wait()
    loads["sea_down"].wait()
    sea_pairs(0, 0, rows // 2)
    send_halo(1)

    for move in op_moves:
        move.wait()

    @pl.when(odd == 1)
    def _():
        lone_move.wait_send()

    @pl.when(kind == 0)
    def _():
        for which in range(2):
            remote(op_lone, op_lone_recv.at[which], op_sem, 3 + which, at_device(me)).wait_recv()

    pair_at, rest_at = row_at // (2 * devices), row_at % (2 * devices)
    source_at = band * (rest_at % devices) + 2 * pair_at + rest_at // devices
    order = jnp.where(lane_at == source_at, 1.0, 0.0).astype(bf16)
    unit = jnp.where(diagonal, 1.0, 0.0).astype(bf16)

    def unpack(which, spot):
        lanes = slice(spot * edge, (spot + 1) * edge)
        square = jnp.concatenate(
            [
                op_recv[which, spot * lat_total : (spot + 1) * lat_total],
                op_recv[which, 2 * lat_total : 3 * lat_total, lanes],
            ],
            axis=1,
        )
        flipped = across(unit, square)
        square = square.astype(f32)
        lines = op_recv[which, 3 * lat_total : 3 * lat_total + 16].astype(f32)
        line = jnp.concatenate(
            [lines[2 * spot : 2 * spot + 1], lines[2 * spot + 1 : 2 * spot + 2, 0:edge]], axis=1
        )
        first = jnp.where(upper, square, flipped)
        second = jnp.where(upper, jnp.where(diagonal, line, flipped), square)
        return first, second

    def lone_operator(which):
        return jnp.concatenate(
            [op_lone_recv[which, 0], op_lone_recv[which, 1, :, 0:edge]], axis=1
        ).astype(f32)

    scale = 2.0 / lat_total * quad_ref[...]
    for spot in range(2):
        near, middle, far = unpack(0, spot), unpack(1, spot), unpack(2, spot)
        for i in range(2):
            s = 2 * spot + i
            lone = (me == 0) & (s == 0)
            one, three = near[i], far[i]
            if s == 0:
                one = jnp.where(kind == 0, lone_operator(0), one)
                three = jnp.where(kind == 0, lone_operator(1), three)
            same = op_own[s].astype(f32) + middle[i]
            other = one + three
            direct = jnp.where(odd == 0, same, other)
            mirror = jnp.where(odd == 0, other, same)

            def ordered(value):
                value = (value * scale).astype(bf16)
                value = jnp.dot(order, value, preferred_element_type=f32).astype(bf16)
                return across(value, order).astype(bf16)

            both[s, 0] = ordered(jnp.where(lone, direct, direct + mirror))
            both[s, 1] = ordered(jnp.where(lone, mirror, direct + mirror))
            gap[s] = ordered(jnp.where(lone, 0.0, direct - mirror))

    loads["real"].wait()
    loads["imag"].wait()

    lane_parts = width // 128
    bunch = 2 * devices
    for p in range(pairs):
        wait_owner(p)
        value = gathered[p].astype(f32).reshape(16 * devices, width)
        for c in range(lane_parts):
            flat[p, c] = value[:, c * 128 : (c + 1) * 128]
        for q in range(8):
            for which in range(2):
                taken = [
                    flat[p, c, pl.ds(8 * which + q, devices, stride=16), :]
                    for c in range(lane_parts)
                ]
                at = q * bunch + which * devices
                turned_rows[at : at + devices] = jnp.concatenate(taken, axis=1).astype(bf16)
        for target, matrix in ((mixed_real, spec_real), (mixed_imag, spec_imag)):
            value = jnp.dot(turned_rows[...], matrix[...], preferred_element_type=f32)
            target[:, p * bunch : (p + 1) * bunch] = value.astype(bf16).reshape(8, bunch, width)


    def act(matrix, value):
        return jnp.dot(matrix, value, preferred_element_type=f32)

    for s in range(slots):
        re, im = 2 * s, 2 * s + 1
        cosine = act(both[s, 0], mixed_real[re]) - act(gap[s], mixed_imag[im])
        sine = act(gap[s], mixed_imag[re]) + act(both[s, 1], mixed_real[im])
        for q, value in ((re, cosine), (im, sine)):
            for p in range(pairs):
                for which in range(2):
                    at = p * bunch + which * devices
                    for c in range(lane_parts):
                        flat[p, c, pl.ds(8 * which + q, devices, stride=16), :] = value[
                            at : at + devices, c * 128 : (c + 1) * 128
                        ]

    start_back, wait_back = exchange(filtered, returned, back_sem, back_own)
    for p in range(pairs):
        value = jnp.concatenate([flat[p, c] for c in range(lane_parts)], axis=1)
        filtered[p] = value.astype(bf16).reshape(devices, 16, width)
        start_back(p)

    take_halo(1)
    sea_pairs(1, 0, rows // 2)

    def grid_moves(p):
        found = []
        for k in range(1, col_count):
            other = (col + k) % col_count
            found.append(
                remote(
                    spatial.at[p, other],
                    spectral.at[p, col],
                    grid_sem,
                    (p, k - 1),
                    (lat, other // 2, other % 2),
                )
            )
        own = pltpu.make_async_copy(spatial.at[p, col], spectral.at[p, col], grid_own.at[p])
        return found + [own]

    def to_grid(p):
        wait_back(p)
        value = returned[p].astype(f32)
        for which in range(2):
            lines = value[:, 8 * which : 8 * which + 8].reshape(circle, width).astype(bf16)
            line = jnp.dot(waves_back[...], lines, preferred_element_type=f32).astype(bf16)
            for b in range(col_count):
                spatial[p, b, which] = line[b * lon_dev : (b + 1) * lon_dev]
        for move in grid_moves(p):
            move.start()

    def finish(p):
        for move in grid_moves(p):
            move.wait()

        @pl.loop(0, col_count // 2)
        def _(jj):
            here = pl.ds(2 * jj, 2)
            value = forced[p, here].reshape(2 * half_block, width)
            value = value + spectral[p, here].reshape(2 * half_block, width).astype(f32)
            inner = layer_norm(value, gain_ref[1:2]).astype(bf16)
            hidden = jax.nn.gelu(
                jnp.dot(inner, air_up[...], preferred_element_type=f32)
            ).astype(bf16)
            value = value + jnp.dot(hidden, air_down[...], preferred_element_type=f32)
            value = value.astype(bf16).reshape(2, 2, lon_dev, width)
            for j2 in range(2):
                air_out[pl.ds(band * (2 * jj + j2) + 2 * p, 2)] = value[j2]

    loads["back"].wait()
    loads["up"].wait()
    loads["down"].wait()
    for p in range(pairs):
        to_grid(p)
        if p > 0:
            finish(p - 1)
    finish(pairs - 1)


def whole_step(
    atm_state,
    ocean_state,
    wet_mask,
    legendre,
    quad_weight,
    spec_real,
    spec_imag,
    degree_gain,
    atm_gain,
    atm_up,
    atm_down,
    atm_to_surface,
    surface_to_atm,
    ocean_to_surface,
    surface_to_ocean,
    ocean_kernel,
    ocean_gain,
    ocean_up,
    ocean_down,
):
    bf16, f32 = jnp.bfloat16, jnp.float32
    devices = lax.axis_size(EVERY)
    col_count = lax.axis_size(COLUMNS)
    lat_dev, lon_dev, width = atm_state.shape
    rows, cols, sea_width = ocean_state.shape
    circle = lon_dev * col_count
    lat_total = legendre.shape[2]
    band = lat_dev // col_count
    reach = STENCIL_TAPS // 2 * OCEAN_DILATION
    slots = legendre.shape[0] // 4
    surface = atm_to_surface.shape[1]
    with jax.ensure_compile_time_eval():
        table = np.asarray(folded_waves(circle, devices).astype(f32))
    waves = jnp.asarray(table, f32).astype(bf16)
    waves_back = jnp.asarray(table.T, f32).astype(bf16)
    vmem = pl.BlockSpec(memory_space=pltpu.VMEM)
    hbm = pl.BlockSpec(memory_space=pl.ANY)
    pairs = band // 2
    tall = (pairs, devices, 16, width)
    patches = (pairs, col_count, 2, lon_dev, width)
    dma = pltpu.SemaphoreType.DMA
    return pl.pallas_call(
        functools.partial(whole_step_body, lat_total),
        out_shape=(
            jax.ShapeDtypeStruct(atm_state.shape, bf16),
            jax.ShapeDtypeStruct(ocean_state.shape, bf16),
        ),
        in_specs=[
            hbm, hbm, vmem, hbm, vmem, hbm, hbm, vmem, vmem, hbm, hbm,
            vmem, vmem, vmem, vmem, vmem, vmem, hbm, hbm, hbm, hbm,
        ],
        out_specs=(vmem, vmem),
        scratch_shapes=[
            pltpu.VMEM(atm_state.shape, bf16),
            pltpu.VMEM(ocean_state.shape, bf16),
            pltpu.VMEM((legendre.shape[0], lat_total, legendre.shape[1]), bf16),
            pltpu.VMEM(spec_real.shape, bf16),
            pltpu.VMEM(spec_imag.shape, bf16),
            pltpu.VMEM(atm_up.shape, bf16),
            pltpu.VMEM(atm_down.shape, bf16),
            pltpu.VMEM(ocean_up.shape, bf16),
            pltpu.VMEM(ocean_down.shape, bf16),
            pltpu.VMEM(waves.shape, bf16),
            pltpu.VMEM(waves.shape, bf16),
            pltpu.VMEM((2 * STENCIL_TAPS * STENCIL_TAPS, 1, sea_width), f32),
            pltpu.VMEM((128, 128), f32),
            pltpu.VMEM((rows, cols, 128), f32),
            pltpu.VMEM((2, 2, rows, lon_dev, surface), bf16),
            pltpu.VMEM((2, 2, rows, lon_dev, surface), bf16),
            pltpu.VMEM(patches, f32),
            pltpu.VMEM(patches, bf16),
            pltpu.VMEM(patches, bf16),
            pltpu.VMEM(tall, bf16),
            pltpu.VMEM(tall, bf16),
            pltpu.VMEM((pairs, width // 128, 16 * devices, 128), f32),
            pltpu.VMEM((16 * devices, width), bf16),
            pltpu.VMEM((8, lat_total, width), bf16),
            pltpu.VMEM((8, lat_total, width), bf16),
            pltpu.VMEM(tall, bf16),
            pltpu.VMEM(tall, bf16),
            pltpu.VMEM(patches, bf16),
            pltpu.VMEM(patches, bf16),
            pltpu.VMEM((4, 3 * lat_total + 16, 128), bf16),
            pltpu.VMEM((3, 3 * lat_total + 16, 128), bf16),
            pltpu.VMEM((slots, lat_total, lat_total), bf16),
            pltpu.VMEM((2, lat_total, 128), bf16),
            pltpu.VMEM((2, 2, lat_total, 128), bf16),
            pltpu.VMEM((slots, 2, lat_total, lat_total), bf16),
            pltpu.VMEM((slots, lat_total, lat_total), bf16),
            pltpu.VMEM((2,) + ocean_state.shape, bf16),
            pltpu.VMEM((2, 2, reach, cols, sea_width), bf16),
            pltpu.VMEM((2, rows // 2, 16, sea_width), bf16),
            pltpu.VMEM((2, rows // 2 + reach, 16, sea_width), bf16),
            pltpu.VMEM((rows + 2 * reach, cols + 16, sea_width), f32),
            pltpu.VMEM((2 * cols, sea_width), f32),
            dma((11,)),
            dma((2,)),
            dma((2, 2)),
            dma((2, pairs, 3)),
            dma((pairs,)),
            dma((2, pairs, devices)),
            dma((pairs,)),
            dma((2, pairs, devices)),
            dma((pairs,)),
            dma((2, pairs, 3)),
            dma((pairs,)),
            dma((2, 5)),
            dma((2, 2, 5)),
        ],
        compiler_params=pltpu.CompilerParams(
            collective_id=0, has_side_effects=True, vmem_limit_bytes=60 * 1024 * 1024
        ),
    )(
        atm_state,
        ocean_state,
        wet_mask,
        jnp.swapaxes(legendre, 1, 2),
        quad_weight[None, :],
        spec_real,
        spec_imag,
        degree_gain[None, :],
        atm_gain,
        atm_up,
        atm_down,
        atm_to_surface.T,
        surface_to_atm,
        ocean_to_surface.T,
        surface_to_ocean,
        ocean_kernel.transpose(1, 2, 0, 3),
        ocean_gain,
        ocean_up,
        ocean_down,
        waves,
        waves_back,
    )


def local(
    atm_state,
    ocean_state,
    wet_mask,
    legendre,
    quad_weight,
    spec_real,
    spec_imag,
    degree_gain,
    atm_gain,
    atm_up,
    atm_down,
    atm_to_surface,
    surface_to_atm,
    ocean_to_surface,
    surface_to_ocean,
    ocean_kernel,
    ocean_gain,
    ocean_up,
    ocean_down,
):
    col_count = lax.axis_size(COLUMNS)
    lat_dev, lon_dev, _ = atm_state.shape
    circle = lon_dev * col_count
    if fits(atm_state, ocean_state, legendre):
        return whole_step(
            atm_state,
            ocean_state,
            wet_mask,
            legendre,
            quad_weight,
            spec_real,
            spec_imag,
            degree_gain,
            atm_gain,
            atm_up,
            atm_down,
            atm_to_surface,
            surface_to_atm,
            ocean_to_surface,
            surface_to_ocean,
            ocean_kernel,
            ocean_gain,
            ocean_up,
            ocean_down,
        )
    wet = wet_mask.astype(jnp.float32)[:, :, None]
    ocean_flux = (
        jnp.dot(ocean_state, ocean_to_surface, preferred_element_type=jnp.float32) * wet
    ).astype(jnp.bfloat16)
    atm_flux = jnp.dot(atm_state, atm_to_surface, preferred_element_type=jnp.float32).astype(
        jnp.bfloat16
    )
    flux_here = lax.all_to_all(ocean_flux, "comp", split_axis=1, concat_axis=0, tiled=True)
    flux_sea = lax.all_to_all(atm_flux, "comp", split_axis=0, concat_axis=1, tiled=True)
    forced = atm_state.astype(jnp.float32) + jnp.dot(
        flux_here, surface_to_atm, preferred_element_type=jnp.float32
    )
    normed = layer_norm(forced, atm_gain[0]).astype(jnp.bfloat16)
    run_spectral = (
        folded_spectral
        if folds(circle, lat_dev, col_count, lax.axis_size(EVERY))
        else plain_spectral
    )
    spectral, stages = run_spectral(
        normed, legendre, quad_weight, spec_real, spec_imag, degree_gain, circle
    )
    mixed = forced + spectral.astype(jnp.float32)
    normed_two = layer_norm(mixed, atm_gain[1]).astype(jnp.bfloat16)
    hidden = jax.nn.gelu(jnp.dot(normed_two, atm_up, preferred_element_type=jnp.float32)).astype(
        jnp.bfloat16
    )
    atm_out = (mixed + jnp.dot(hidden, atm_down, preferred_element_type=jnp.float32)).astype(
        jnp.bfloat16
    )
    ocean_in = (
        ocean_state.astype(jnp.float32)
        + wet * jnp.dot(flux_sea, surface_to_ocean, preferred_element_type=jnp.float32)
    ).astype(jnp.bfloat16)
    stencil_reach = STENCIL_TAPS // 2 * OCEAN_DILATION
    sides = ((("lat", "comp"), 0), ("lon", 1))
    current = ocean_in
    quick = ocean_in.shape[0] % (2 * OCEAN_DILATION) == 0 and ocean_in.shape[2] % 128 == 0
    for k in range(2):
        field = padded(current, sides, stencil_reach)
        weights = (ocean_kernel[k], ocean_gain[k], ocean_up[k], ocean_down[k])
        if quick:
            current = fast_ocean_block(field, *weights, stages[k])
        else:
            current = ocean_block(field, *weights)
    ocean_out = jnp.where(wet_mask[:, :, None] == 1, current, ocean_state)
    return (atm_out, ocean_out)


def solution(mesh):
    placed = (
        P("lat", ("lon", "comp"), None),
        P(("lat", "comp"), "lon", None),
        P(("lat", "comp"), "lon"),
        P(("lat", "lon", "comp"), None, None),
        P(),
        P(),
        P(),
        P(),
        P(),
        P(),
        P(),
        P(),
        P(),
        P(),
        P(),
        P(),
        P(),
        P(),
        P(),
    )

    return jax.shard_map(
        local,
        mesh=mesh,
        in_specs=placed,
        out_specs=(P("lat", ("lon", "comp"), None), P(("lat", "comp"), "lon", None)),
        check_vma=False,
    )
```

```python
import functools
import math

import jax
import jax.numpy as jnp
import numpy as np
from jax import lax
from jax.experimental import pallas as pl
from jax.experimental.pallas import tpu as pltpu
from jax.sharding import PartitionSpec as P

MODES = 512
STENCIL_TAPS = 7
OCEAN_DILATION = 2
COLUMNS = ("lon", "comp")
EVERY = ("lat", "lon", "comp")


epsilon = 1e-05


def padded(block, sides, width):
    for axis, dim in sides:
        count = lax.axis_size(axis)
        forward = [(i, i + 1) for i in range(count - 1)]
        backward = [(target, source) for source, target in forward]
        low = lax.ppermute(
            lax.slice_in_dim(block, block.shape[dim] - width, None, axis=dim), axis, forward
        )
        high = lax.ppermute(lax.slice_in_dim(block, 0, width, axis=dim), axis, backward)
        block = jnp.concatenate([low, block, high], axis=dim)
    return block


def layer_norm(values, gain):
    centred = values - jnp.mean(values, axis=-1, keepdims=True)
    spread = jnp.mean(centred * centred, axis=-1, keepdims=True)
    return centred * lax.rsqrt(spread + epsilon) * gain


def wave_table(row_index, circle):
    longitude = jnp.arange(circle, dtype=jnp.int32)
    wavenumber = row_index // 2
    phases = wavenumber[:, None] * longitude[None, :] % circle
    angles = phases.astype(jnp.float32) * (2.0 * math.pi / circle)
    waves = jnp.where((row_index % 2 == 0)[:, None], jnp.cos(angles), -jnp.sin(angles))
    return (wavenumber, waves)


def forward_table(row_index, circle):
    _, waves = wave_table(row_index, circle)
    return (waves.T / math.sqrt(circle)).astype(jnp.bfloat16)


def inverse_table(row_index, circle):
    wavenumber, waves = wave_table(row_index, circle)
    factor = jnp.where(wavenumber == 0, 1.0, 2.0).astype(jnp.float32)
    return (waves * factor[:, None] / math.sqrt(circle)).astype(jnp.bfloat16)


def reorder_rows(total_rows, owned, lat_count, col_count):
    positions = jnp.arange(total_rows, dtype=jnp.int32)
    stride = lat_count * owned
    return (
        owned * (positions % stride // owned * col_count + positions // stride) + positions % owned
    )


def spectral_filter(gathered, table, quad_weight, spec_real, spec_imag, degree_gain):
    count = table.shape[0]
    lat_total = table.shape[2]
    channels = gathered.shape[2]
    split_parts = gathered.reshape(lat_total, count, 2, channels)
    weighted = (table.astype(jnp.float32) * (quad_weight / lat_total)).astype(jnp.bfloat16)
    coeffs = jnp.einsum(
        "mln,nmpc->mplc", weighted, split_parts, preferred_element_type=jnp.float32
    ).astype(jnp.bfloat16)
    real_part = coeffs[:, 0]
    imag_part = coeffs[:, 1]
    mixed_real = jnp.dot(real_part, spec_real, preferred_element_type=jnp.float32) - jnp.dot(
        imag_part, spec_imag, preferred_element_type=jnp.float32
    )
    mixed_imag = jnp.dot(real_part, spec_imag, preferred_element_type=jnp.float32) + jnp.dot(
        imag_part, spec_real, preferred_element_type=jnp.float32
    )
    scaled = (jnp.stack([mixed_real, mixed_imag], axis=1) * degree_gain[:, None]).astype(
        jnp.bfloat16
    )
    returned = jnp.einsum(
        "mln,mplc->nmpc", table, scaled, preferred_element_type=jnp.float32
    ).astype(jnp.bfloat16)
    return returned.reshape(lat_total, 2 * count, channels)


def folds(circle, lat_dev, col_count, devices):
    return (
        MODES == 2 * circle
        and lat_dev % col_count == 0
        and devices % 4 == 0
        and (circle // 2) % devices == 0
        and (MODES // devices) % 4 == 0
    )


def place_of(kind, i, group):
    return kind * group + (group - 1 - i if kind % 2 else i)


def folded_waves(circle, devices):
    longitude = jnp.arange(circle, dtype=jnp.int32)
    position = jnp.arange(circle, dtype=jnp.int32)
    group = devices // 4
    owned = circle // devices
    owner = position // owned
    kind, place = owner // group, owner % group
    place = jnp.where(kind % 2 == 1, group - 1 - place, place)
    row_index = (4 * place + kind) * owned + position % owned
    wavenumber = jnp.where(row_index == 1, circle // 2, row_index // 2)
    phases = wavenumber[:, None] * longitude[None, :] % circle
    angles = phases.astype(jnp.float32) * (2.0 * math.pi / circle)
    cosine = ((row_index % 2 == 0) | (row_index == 1))[:, None]
    return jnp.where(cosine, jnp.cos(angles), -jnp.sin(angles)) / math.sqrt(circle)


def folded_operators(table, quad_weight, degree_gain):
    devices = lax.axis_size(EVERY)
    me = lax.axis_index(EVERY)
    count, _, lat_total = table.shape
    group = devices // 4
    part = count // 4
    family = me // group
    scaled = (table.astype(jnp.float32) * degree_gain[:, None]).astype(jnp.bfloat16)
    operators = jnp.einsum(
        "mlt,mlu->mtu", table, scaled, preferred_element_type=jnp.float32
    )
    operators = operators * (quad_weight / lat_total)
    first_scale = jnp.where(me == 0, 0.5, 1.0).astype(jnp.float32)
    scales = jnp.where(jnp.arange(count) == 0, first_scale, 1.0)
    operators = (operators * scales[:, None, None]).astype(jnp.bfloat16)
    turn = []
    for base in (group, 3 * group):
        for i in range(group):
            turn.append((base + (i + 1) % group, base + i))
    rotated = lax.ppermute(operators[:1], EVERY, turn)
    mirrored = jnp.concatenate([rotated, jnp.flip(operators[1:], axis=0)], axis=0)
    ordered = jnp.where(family % 2 == 1, mirrored, operators)
    received = [lax.dynamic_slice_in_dim(ordered, family * part, part, axis=0)]
    for shift in range(1, 4):
        pairs = []
        for i in range(group):
            for kind in range(4):
                pairs.append((place_of(kind, i, group), place_of(kind ^ shift, i, group)))
        piece = lax.dynamic_slice_in_dim(ordered, (family ^ shift) * part, part, axis=0)
        received.append(lax.ppermute(piece, EVERY, pairs))
    received = [value.astype(jnp.float32) for value in received]
    same = received[0] + received[2]
    other = received[1] + received[3]
    direct = jnp.where(family % 2 == 0, same, other)
    mirror = jnp.where(family % 2 == 0, other, same)
    lone = ((me == 0) & (jnp.arange(part) == 0))[:, None, None]
    both = direct + mirror
    gap = jnp.where(lone, 0.0, direct - mirror)
    top = jnp.concatenate([jnp.where(lone, direct, both), -gap], axis=2)
    bottom = jnp.concatenate([gap, jnp.where(lone, mirror, both)], axis=2)
    return (2.0 * top).astype(jnp.bfloat16), (2.0 * bottom).astype(jnp.bfloat16)


def folded_spectral(normed, legendre, quad_weight, spec_real, spec_imag, degree_gain, circle):
    width = normed.shape[2]
    top, bottom = folded_operators(legendre, quad_weight, degree_gain)
    slots = top.shape[0]
    waves = folded_waves(circle, lax.axis_size(EVERY)).astype(jnp.bfloat16)
    columns = lax.all_to_all(normed, COLUMNS, split_axis=0, concat_axis=1, tiled=True)
    spectrum = jnp.einsum(
        "rn,tnc->trc", waves, columns, preferred_element_type=jnp.float32
    ).astype(jnp.bfloat16)
    gathered = lax.all_to_all(spectrum, EVERY, split_axis=1, concat_axis=0, tiled=True)
    lat_total = gathered.shape[0]
    channels = jnp.concatenate([spec_real, spec_imag], axis=1)
    turned = gathered.reshape(lat_total, slots, 2, width).transpose(1, 2, 0, 3)
    mixed = jnp.dot(turned, channels, preferred_element_type=jnp.float32).astype(jnp.bfloat16)
    upper = jnp.concatenate([mixed[:, 0, :, :width], mixed[:, 1, :, width:]], axis=1)
    lower = jnp.concatenate([mixed[:, 0, :, width:], mixed[:, 1, :, :width]], axis=1)
    cosine = jnp.einsum("stu,suc->stc", top, upper, preferred_element_type=jnp.float32)
    sine = jnp.einsum("stu,suc->stc", bottom, lower, preferred_element_type=jnp.float32)
    filtered = jnp.stack([cosine, sine], axis=1).astype(jnp.bfloat16)
    filtered = filtered.reshape(2 * slots, lat_total, width).transpose(1, 0, 2)
    returned = lax.all_to_all(filtered, EVERY, split_axis=0, concat_axis=1, tiled=True)
    spatial = jnp.einsum(
        "rn,trc->tnc", waves, returned, preferred_element_type=jnp.float32
    ).astype(jnp.bfloat16)
    spectral = lax.all_to_all(spatial, COLUMNS, split_axis=1, concat_axis=0, tiled=True)
    return spectral, (spectrum, filtered)


def plain_spectral(normed, legendre, quad_weight, spec_real, spec_imag, degree_gain, circle):
    lat_count = lax.axis_size("lat")
    col_count = lax.axis_size(("lon", "comp"))
    total_rows = 2 * MODES
    owned = 2 * legendre.shape[0]
    natural = jnp.arange(total_rows, dtype=jnp.int32)
    columns = lax.all_to_all(normed, ("lon", "comp"), split_axis=2, concat_axis=1, tiled=True)
    forward = forward_table(natural, circle)
    inverse = inverse_table(reorder_rows(total_rows, owned, lat_count, col_count), circle)
    spectrum = jnp.einsum(
        "anc,nr->arc", columns, forward, preferred_element_type=jnp.float32
    ).astype(jnp.bfloat16)
    gathered = lax.all_to_all(
        lax.all_to_all(spectrum, "lat", split_axis=1, concat_axis=0, tiled=True),
        ("lon", "comp"),
        split_axis=1,
        concat_axis=2,
        tiled=True,
    )
    filtered = spectral_filter(gathered, legendre, quad_weight, spec_real, spec_imag, degree_gain)
    returned = lax.all_to_all(
        lax.all_to_all(filtered, "lat", split_axis=0, concat_axis=1, tiled=True),
        ("lon", "comp"),
        split_axis=2,
        concat_axis=1,
        tiled=True,
    )
    spatial = jnp.einsum(
        "arc,rn->anc", returned, inverse, preferred_element_type=jnp.float32
    ).astype(jnp.bfloat16)
    spectral = lax.all_to_all(spatial, COLUMNS, split_axis=1, concat_axis=2, tiled=True)
    return spectral, (spectrum, filtered)


def ocean_block(padded_field, kernel, gain, up_weight, down_weight):
    stencil_reach = STENCIL_TAPS // 2 * OCEAN_DILATION
    tile_height = padded_field.shape[0] - 2 * stencil_reach
    tile_breadth = padded_field.shape[1] - 2 * stencil_reach
    stencil = jnp.zeros((tile_height, tile_breadth, padded_field.shape[2]), jnp.float32)
    for row_offset_tap in range(STENCIL_TAPS):
        for column_tap in range(STENCIL_TAPS):
            stencil_window = padded_field[
                row_offset_tap * OCEAN_DILATION : row_offset_tap * OCEAN_DILATION + tile_height,
                column_tap * OCEAN_DILATION : column_tap * OCEAN_DILATION + tile_breadth,
            ]
            stencil = stencil + stencil_window.astype(jnp.float32) * kernel[
                row_offset_tap, column_tap
            ].astype(jnp.float32)
    normed = layer_norm(stencil, gain).astype(jnp.bfloat16)
    hidden = jax.nn.gelu(jnp.dot(normed, up_weight, preferred_element_type=jnp.float32)).astype(
        jnp.bfloat16
    )
    centre = padded_field[
        stencil_reach : stencil_reach + tile_height, stencil_reach : stencil_reach + tile_breadth
    ]
    return (
        centre.astype(jnp.float32)
        + jnp.dot(hidden, down_weight, preferred_element_type=jnp.float32)
    ).astype(jnp.bfloat16)


def ocean_kernel_body(
    field_ref, taps_ref, gain_ref, up_ref, down_ref, after_ref, out_ref, wide, normed
):
    rows, cols, width = out_ref.shape
    step = OCEAN_DILATION
    lanes = 128

    @pl.loop(0, rows + (STENCIL_TAPS - 1) * step)
    def _(row):
        wide[row] = field_ref[row].astype(jnp.float32)

    @pl.loop(0, rows // 2)
    def _(pair):
        base = pair // step * (2 * step) + pair % step
        for half in range(width // lanes):
            part = slice(half * lanes, (half + 1) * lanes)
            sums = [jnp.zeros((cols, lanes), jnp.float32) for _ in range(2)]
            for a in range(STENCIL_TAPS + 1):
                for b in range(STENCIL_TAPS):
                    window = wide[base + a * step, b * step : b * step + cols, part]
                    for which in range(2):
                        tap = a - which
                        if 0 <= tap < STENCIL_TAPS:
                            weight = taps_ref[tap * STENCIL_TAPS + b, :, part]
                            sums[which] = sums[which] + window * weight
            for which in range(2):
                normed[which * cols : (which + 1) * cols, part] = sums[which]
        stencil = normed[...]
        values = layer_norm(stencil, gain_ref[...]).astype(jnp.bfloat16)
        hidden = jax.nn.gelu(
            jnp.dot(values, up_ref[...], preferred_element_type=jnp.float32)
        ).astype(jnp.bfloat16)
        moved = jnp.dot(hidden, down_ref[...], preferred_element_type=jnp.float32)
        reach = STENCIL_TAPS // 2 * step
        for which in range(2):
            row = base + which * step
            centre = wide[row + reach, reach : reach + cols, :]
            out_ref[row] = (centre + moved[which * cols : (which + 1) * cols]).astype(
                out_ref.dtype
            )


def fast_ocean_block(field, kernel, gain, up_weight, down_weight, after):
    reach = STENCIL_TAPS // 2 * OCEAN_DILATION
    rows, cols, width = field.shape[0] - 2 * reach, field.shape[1] - 2 * reach, field.shape[2]
    hidden = up_weight.shape[1]
    taps = kernel.astype(jnp.float32).reshape(STENCIL_TAPS * STENCIL_TAPS, 1, width)
    whole = pl.BlockSpec(memory_space=pltpu.VMEM)
    cells = rows * cols
    return pl.pallas_call(
        ocean_kernel_body,
        out_shape=jax.ShapeDtypeStruct((rows, cols, width), jnp.bfloat16),
        in_specs=[whole] * 5 + [pl.BlockSpec(memory_space=pl.ANY)],
        out_specs=whole,
        scratch_shapes=[
            pltpu.VMEM(field.shape, jnp.float32),
            pltpu.VMEM((2 * cols, width), jnp.float32),
        ],
        compiler_params=pltpu.CompilerParams(vmem_limit_bytes=32 * 1024 * 1024),
        cost_estimate=pl.CostEstimate(
            flops=4 * cells * width * hidden + 98 * cells * width * 64,
            bytes_accessed=4 * field.size + 4 * up_weight.size,
            transcendentals=cells * hidden,
        ),
    )(field, taps, gain[None, :], up_weight, down_weight, after)


MESH_ID = pl.DeviceIdType.MESH


def fits(atm_state, ocean_state, legendre):
    devices = lax.axis_size(EVERY)
    col_count = lax.axis_size(COLUMNS)
    lat_dev, lon_dev, width = atm_state.shape
    rows, cols, sea_width = ocean_state.shape
    circle = lon_dev * col_count
    reach = STENCIL_TAPS // 2 * OCEAN_DILATION
    return (
        folds(circle, lat_dev, col_count, devices)
        and lax.axis_size("lon") == 2
        and lax.axis_size("comp") == 2
        and circle // devices == 8
        and legendre.shape[0] == 16
        and lat_dev // col_count == 6
        and lat_dev == 2 * rows
        and cols == 2 * lon_dev
        and cols == 128
        and rows == 2 * reach
        and rows % 6 == 0
        and reach % 2 == 0
        and rows % (2 * OCEAN_DILATION) == 0
        and 128 < legendre.shape[2] <= 192
        and legendre.shape[2] % 16 == 0
        and lon_dev % 16 == 0
        and width % 128 == 0
        and sea_width == 256
    )


def whole_step_body(
    lat_total,
    atm_hbm,
    sea_hbm,
    wet_ref,
    legendre_hbm,
    quad_ref,
    real_hbm,
    imag_hbm,
    degree_ref,
    gain_ref,
    up_hbm,
    down_hbm,
    to_sea_ref,
    from_sea_ref,
    to_air_ref,
    from_air_ref,
    taps_in_ref,
    sea_gain_ref,
    sea_up_hbm,
    sea_down_hbm,
    waves_hbm,
    waves_back_hbm,
    air_out,
    sea_out,
    air,
    sea,
    legendre,
    spec_real,
    spec_imag,
    air_up,
    air_down,
    sea_up,
    sea_down,
    waves,
    waves_back,
    taps,
    wet_square,
    wet_full,
    flux_out,
    flux_in,
    forced,
    normed,
    columns,
    spec_send,
    gathered,
    flat,
    turned_rows,
    mixed_real,
    mixed_imag,
    filtered,
    returned,
    spatial,
    spectral,
    op_send,
    op_recv,
    op_sum,
    op_other,
    op_lone,
    both,
    gap,
    field,
    edges,
    strips,
    sides,
    corners,
    wide,
    stencil,
    load_sem,
    local_sem,
    flux_sem,
    column_sem,
    column_own,
    owner_sem,
    owner_own,
    back_sem,
    back_own,
    grid_sem,
    grid_own,
    op_sem,
    halo_sem,
):
    f32, bf16 = jnp.float32, jnp.bfloat16
    lat = lax.axis_index("lat")
    lon = lax.axis_index("lon")
    comp = lax.axis_index("comp")
    col_count = lax.axis_size(COLUMNS)
    devices = lax.axis_size(EVERY)
    group = devices // 4
    col = lon * 2 + comp
    me = lat * col_count + col
    tile = lat * 2 + comp
    tiles = lax.axis_size("lat") * 2
    lat_dev, lon_dev, width = air.shape
    rows, cols, sea_width = sea.shape
    band = lat_dev // col_count
    pairs = band // 2
    circle = lon_dev * col_count
    step = OCEAN_DILATION
    reach = STENCIL_TAPS // 2 * step
    slots = both.shape[0]

    def at_device(index):
        return (index // col_count, index % col_count // 2, index % 2)

    def at_tile(index, side):
        return (index // 2, side, index % 2)

    def remote(source, target, sems, k, where):
        place_in = k if isinstance(k, tuple) else (k,)
        return pltpu.make_async_remote_copy(
            src_ref=source,
            dst_ref=target,
            send_sem=sems.at[(0,) + place_in],
            recv_sem=sems.at[(1,) + place_in],
            device_id=where,
            device_id_type=MESH_ID,
        )

    def across(left, right):
        return lax.dot_general(left, right, (((1,), (1,)), ((), ())), preferred_element_type=f32)

    barrier = pltpu.get_barrier_semaphore()

    @pl.loop(1, devices)
    def _(k):
        pl.semaphore_signal(
            barrier, inc=1, device_id=at_device((me + k) % devices), device_id_type=MESH_ID
        )

    loads = {}
    for index, (name, source, target) in enumerate(
        (
            ("legendre", legendre_hbm, legendre),
            ("sea", sea_hbm, sea),
            ("air", atm_hbm, air),
            ("waves", waves_hbm, waves),
            ("sea_up", sea_up_hbm, sea_up),
            ("sea_down", sea_down_hbm, sea_down),
            ("real", real_hbm, spec_real),
            ("imag", imag_hbm, spec_imag),
            ("back", waves_back_hbm, waves_back),
            ("up", up_hbm, air_up),
            ("down", down_hbm, air_down),
        )
    ):
        loads[name] = pltpu.make_async_copy(source, target, load_sem.at[index])
    for name in ("legendre", "sea", "air"):
        loads[name].start()

    wet_square[...] = jnp.zeros_like(wet_square)
    wet_square[0:rows, :] = wet_ref[...].astype(f32)
    turned = jnp.transpose(wet_square[...])
    for i in range(rows):
        wet_full[i] = jnp.broadcast_to(turned[:, i : i + 1], (cols, 128))

    for a in range(STENCIL_TAPS):
        for b in range(STENCIL_TAPS):
            line = taps_in_ref[a, b].astype(f32)
            for k in range(2):
                taps[(k * STENCIL_TAPS + a) * STENCIL_TAPS + b] = line[k : k + 1]

    loads["legendre"].wait()
    kind = me // group
    odd = kind % 2
    place = me % group
    count = legendre.shape[0]
    edge = lat_total - 128
    row_at = lax.broadcasted_iota(jnp.int32, (lat_total, lat_total), 0)
    lane_at = lax.broadcasted_iota(jnp.int32, (lat_total, lat_total), 1)
    upper, diagonal = row_at <= lane_at, row_at == lane_at

    def operator(k):
        index = odd * ((count - k) % count) + (1 - odd) * k
        table = legendre[index]
        scaled = (table.astype(f32) * degree_ref[...][None, :]).astype(bf16)
        return across(table, scaled) * jnp.where((me == 0) & (index == 0), 0.5, 1.0).astype(f32)

    high_half = kind // 2

    def fill_operators(first_group):
        @pl.loop(first_group, first_group + 2)
        def _(which):
            tails, marks = [], []
            for spot in range(2):
                first, second = operator(4 * which + 2 * spot), operator(4 * which + 2 * spot + 1)
                square = jnp.where(upper, first, second).astype(bf16)
                op_send[which, spot * lat_total : (spot + 1) * lat_total] = square[:, 0:128]
                tails.append(square[:, 128:lat_total])
                line = jnp.sum(jnp.where(diagonal, second, 0.0), axis=0, keepdims=True)
                marks.append(line[:, 0:128])
                marks.append(
                    jnp.concatenate(
                        [line[:, 128:lat_total], jnp.zeros((1, 128 - edge), f32)], axis=1
                    )
                )

            op_send[which, 2 * lat_total : 3 * lat_total, 0 : 2 * edge] = jnp.concatenate(
                tails, axis=1
            )
            at = lax.broadcasted_iota(jnp.int32, (16, 128), 0)
            lines = jnp.zeros((16, 128), f32)
            for i in range(4):
                lines = jnp.where(at == i, marks[i], lines)
            op_send[which, 3 * lat_total : 3 * lat_total + 16] = lines.astype(bf16)

    fill_operators(2 * (1 - high_half))
    pl.semaphore_wait(barrier, devices - 1)
    across_kind = (kind + 2) % 4
    op_first = [
        remote(
            op_send.at[2 * (1 - high_half) + j],
            op_recv.at[j],
            op_sem,
            k,
            at_device(across_kind * group + place),
        )
        for k, j in enumerate((1 - odd, odd))
    ]
    op_first[0].start()
    spot_of = odd * (group - 1 - place) + (1 - odd) * place
    beside = kind + 1 - 2 * odd
    beside_place = odd * spot_of + (1 - odd) * (group - 1 - spot_of)
    op_second = remote(
        op_sum.at[1 - odd], op_other, op_sem, 2, at_device(beside * group + beside_place)
    )
    lone_moves = [
        remote(
            op_sum.at[0, pl.ds(start, lat_total)],
            op_lone.at[k],
            op_sem,
            3 + k,
            at_device((group - place) % group),
        )
        for k, start in enumerate((0, 2 * lat_total))
    ]

    def sum_operators(j):
        mine = op_send[2 * high_half + j].astype(f32)
        op_sum[j] = (mine + op_recv[j].astype(f32)).astype(bf16)

    def pass_operators():
        op_first[0].wait()
        sum_operators(1 - odd)
        op_second.start()

        @pl.when(kind == 1)
        def _():
            for move in lone_moves:
                move.start()

    def keep_operators():
        op_first[1].wait()
        sum_operators(odd)

    loads["sea"].wait()

    few = rows // 3
    for part in range(3):
        here = slice(part * few, (part + 1) * few)
        flux = across(sea[here].reshape(few * cols, sea_width), to_air_ref[...])
        flux = flux.reshape(few, cols, -1)
        flux = (flux * wet_full[here, :, 0 : flux.shape[2]]).astype(bf16)
        flux_out[0, 0, here] = flux[:, 0:lon_dev]
        flux_out[0, 1, here] = flux[:, lon_dev : 2 * lon_dev]

    partner = (lat, lon, 1 - comp)
    moves = []
    for part in range(2):
        moves.append(
            remote(flux_out.at[part, 1 - comp], flux_in.at[part, comp], flux_sem, part, partner)
        )
    moves[0].start()
    loads["air"].wait()

    for part in range(4):
        here = slice(part * rows // 2, (part + 1) * rows // 2)
        there = slice(part % 2 * rows // 2, (part % 2 + 1) * rows // 2)
        flux = across(air[here].reshape(rows // 2 * lon_dev, width), to_sea_ref[...])
        flux_out[1, part // 2, there] = flux.astype(bf16).reshape(rows // 2, lon_dev, -1)

    moves[1].start()
    kept = []
    for part in range(2):
        kept.append(
            pltpu.make_async_copy(
                flux_out.at[part, comp], flux_in.at[part, comp], local_sem.at[part]
            )
        )
        kept[-1].start()
    for name in (
        "waves", "sea_up", "sea_down", "real", "imag", "back", "up", "down"
    ):
        loads[name].start()
    for move in kept:
        move.wait()
    moves[0].wait()


    def column_moves(p):
        found = []
        for k in range(1, col_count):
            other = (col + k) % col_count
            found.append(
                remote(
                    normed.at[p, other],
                    columns.at[p, col],
                    column_sem,
                    (p, k - 1),
                    (lat, other // 2, other % 2),
                )
            )
        own = pltpu.make_async_copy(normed.at[p, col], columns.at[p, col], column_own.at[p])
        return found + [own]

    half_block = 2 * lon_dev
    for p in range(pairs):

        @pl.loop(0, col_count // 2)
        def _(jj):
            for j2 in range(2):
                j = 2 * jj + j2
                row = band * j + 2 * p
                flux = flux_in[0, row // rows, pl.ds(row % rows, 2)].reshape(half_block, -1)
                value = air[pl.ds(row, 2)].reshape(half_block, width).astype(f32)
                value = value + jnp.dot(flux, from_sea_ref[...], preferred_element_type=f32)
                forced[p, j] = value.reshape(2, lon_dev, width)
                value = layer_norm(value, gain_ref[0:1]).astype(bf16)
                normed[p, j] = value.reshape(2, lon_dev, width)

        for move in column_moves(p):
            move.start()

    moves[1].wait()

    @pl.loop(0, rows)
    def _(i):
        flux = jnp.concatenate([flux_in[1, 0, i], flux_in[1, 1, i]], axis=0)
        added = jnp.dot(flux, from_air_ref[...], preferred_element_type=f32)
        mask = wet_full[i]
        mask = jnp.concatenate([mask, mask], axis=1)
        field[0, i] = (sea[i].astype(f32) + mask * added).astype(bf16)

    half_reach = reach // 2
    far = tile - 1 + 2 * comp
    has_far = (far >= 0) & (far < tiles)

    def pack_strips(k):
        @pl.loop(0, rows // 2)
        def _(i):
            found = []
            for which in range(2):
                low = field[k, 2 * i + which, 0:16].astype(f32)
                high = field[k, 2 * i + which, cols - 16 : cols].astype(f32)
                found.append(jnp.where(lon == 0, high[8:16], low[0:8]))
            strips[k, i] = jnp.concatenate(found, axis=0).astype(bf16)

    def side_move(k):
        return remote(strips.at[k], sides.at[k], halo_sem.at[k], 0, at_tile(tile, 1 - lon))

    def edge_moves(k, which):
        target = far if which else tile + 1 - 2 * comp
        upper_half = comp if which else 1 - comp
        return (
            remote(
                field.at[k, pl.ds(reach * upper_half, reach)],
                edges.at[k, which],
                halo_sem.at[k],
                1 + 2 * which,
                at_tile(target, lon),
            ),
            remote(
                strips.at[k, pl.ds(half_reach * upper_half, half_reach)],
                corners.at[k, which],
                halo_sem.at[k],
                2 + 2 * which,
                at_tile(target, 1 - lon),
            ),
        )

    def send_halo(k):
        pack_strips(k)

        @pl.when(has_far)
        def _():
            for move in edge_moves(k, 1):
                move.start()

        side_move(k).start()
        for move in edge_moves(k, 0):
            move.start()

    def margins(first, pair, values):
        for which in range(2):
            part = values[8 * which : 8 * which + 8]
            wide[first + 2 * pair + which, 0:8] = jnp.where(lon == 1, part, 0.0)
            wide[first + 2 * pair + which, cols + 8 : cols + 16] = jnp.where(lon == 0, part, 0.0)

    def fill_edge(k, which, first):
        @pl.loop(0, reach)
        def _(i):
            wide[first + i, 8 : cols + 8] = edges[k, which, i].astype(f32)

        @pl.loop(0, half_reach)
        def _(i):
            margins(first, i, corners[k, which, i].astype(f32))

    def take_near(k):
        @pl.loop(0, rows)
        def _(i):
            wide[reach + i, 8 : cols + 8] = field[k, i].astype(f32)

        side_move(k).wait()
        for move in edge_moves(k, 0):
            move.wait()

        @pl.loop(0, rows // 2)
        def _(i):
            margins(reach, i, sides[k, i].astype(f32))

        fill_edge(k, 0, (reach + rows) * (1 - comp))

    def take_far(k):
        first = (reach + rows) * comp

        @pl.when(has_far)
        def _():
            for move in edge_moves(k, 1):
                move.wait()
            fill_edge(k, 1, first)

        @pl.when(jnp.logical_not(has_far))
        def _():
            @pl.loop(0, reach)
            def _(i):
                wide[first + i] = jnp.zeros(wide.shape[1:], f32)

    send_halo(0)
    op_first[1].start()
    fill_operators(2 * high_half)

    triple = reach // step
    slab = cols // 2

    def sea_half(k, upper_half):
        @pl.loop(0, step)
        def _(parity):
            base = upper_half * reach + parity
            for half in range(sea_width // 128):
                part = slice(half * 128, (half + 1) * 128)
                for side in range(2):
                    sums = [jnp.zeros((slab, 128), f32) for _ in range(triple)]
                    for a in range(STENCIL_TAPS + triple - 1):
                        for b in range(STENCIL_TAPS):
                            start = 8 - reach + b * step + side * slab
                            window = wide[base + a * step, start : start + slab, part]
                            for which in range(triple):
                                tap = a - which
                                if 0 <= tap < STENCIL_TAPS:
                                    weight = taps[
                                        (k * STENCIL_TAPS + tap) * STENCIL_TAPS + b, :, part
                                    ]
                                    sums[which] = sums[which] + window * weight
                    for which in range(triple):
                        at = which * cols + side * slab
                        stencil[at : at + slab, part] = sums[which]
            values = layer_norm(stencil[...], sea_gain_ref[k : k + 1]).astype(bf16)
            hidden = jax.nn.gelu(
                jnp.dot(values, sea_up[k], preferred_element_type=f32)
            ).astype(bf16)
            moved = jnp.dot(hidden, sea_down[k], preferred_element_type=f32)
            for which in range(triple):
                row = base + which * step
                centre = wide[row + reach, 8 : 8 + cols, :]
                value = (centre + moved[which * cols : (which + 1) * cols]).astype(bf16)
                if k == 0:
                    field[1, row] = value
                else:
                    mask = wet_full[row]
                    mask = jnp.concatenate([mask, mask], axis=1)
                    sea_out[row] = jnp.where(mask > 0.5, value, sea[row])

    def exchange(source, target, sems, own_sems):
        def away(p, k):
            other = (me + k) % devices
            return remote(
                source.at[p, other], target.at[p, me], sems, (p, k), at_device(other)
            )

        def own(p):
            return pltpu.make_async_copy(source.at[p, me], target.at[p, me], own_sems.at[p])

        def start(p):
            @pl.loop(1, devices)
            def _(k):
                away(p, k).start()

            own(p).start()

        def wait(p):
            own(p).wait()

            @pl.loop(1, devices)
            def _(k):
                away(p, k).wait()

        return start, wait

    start_owner, wait_owner = exchange(spec_send, gathered, owner_sem, owner_own)
    loads["waves"].wait()

    for p in range(pairs):
        for move in column_moves(p):
            move.wait()
        found = []
        for which in range(2):
            lines = jnp.concatenate([columns[p, b, which] for b in range(col_count)], axis=0)
            value = jnp.dot(waves[...], lines, preferred_element_type=f32)
            found.append(value.reshape(devices, 8, width))
        spec_send[p] = jnp.concatenate(found, axis=1).astype(bf16)
        start_owner(p)

    pass_operators()
    take_near(0)
    loads["sea_up"].wait()
    loads["sea_down"].wait()
    sea_half(0, 1 - comp)
    take_far(0)
    sea_half(0, comp)
    send_halo(1)
    keep_operators()

    loads["real"].wait()
    loads["imag"].wait()

    lane_parts = width // 128
    bunch = 2 * devices

    def mix_rows(p):
        wait_owner(p)
        value = gathered[p].astype(f32).reshape(16 * devices, width)
        for c in range(lane_parts):
            flat[p, c] = value[:, c * 128 : (c + 1) * 128]
        for q in range(8):
            for which in range(2):
                taken = [
                    flat[p, c, pl.ds(8 * which + q, devices, stride=16), :]
                    for c in range(lane_parts)
                ]
                at = q * bunch + which * devices
                turned_rows[at : at + devices] = jnp.concatenate(taken, axis=1).astype(bf16)
        for target, matrix in ((mixed_real, spec_real), (mixed_imag, spec_imag)):
            value = jnp.dot(turned_rows[...], matrix[...], preferred_element_type=f32)
            target[:, p * bunch : (p + 1) * bunch] = value.astype(bf16).reshape(8, bunch, width)

    for p in range(pairs - 1):
        mix_rows(p)

    op_second.wait()

    @pl.when(kind == 1)
    def _():
        for move in lone_moves:
            move.wait_send()

    @pl.when(kind == 0)
    def _():
        for move in lone_moves:
            move.wait_recv()

    pair_at, rest_at = row_at // (2 * devices), row_at % (2 * devices)
    source_at = band * (rest_at % devices) + 2 * pair_at + rest_at // devices
    order = jnp.where(lane_at == source_at, 1.0, 0.0).astype(bf16)
    unit = jnp.where(diagonal, 1.0, 0.0).astype(bf16)

    def unpack(packed, spot):
        lanes = slice(spot * edge, (spot + 1) * edge)
        square = jnp.concatenate(
            [
                packed[spot * lat_total : (spot + 1) * lat_total],
                packed[2 * lat_total : 3 * lat_total, lanes],
            ],
            axis=1,
        )
        flipped = across(unit, square)
        square = square.astype(f32)
        lines = packed[3 * lat_total : 3 * lat_total + 16].astype(f32)
        line = jnp.concatenate(
            [lines[2 * spot : 2 * spot + 1], lines[2 * spot + 1 : 2 * spot + 2, 0:edge]], axis=1
        )
        first = jnp.where(upper, square, flipped)
        second = jnp.where(upper, jnp.where(diagonal, line, flipped), square)
        return first, second

    scale = 2.0 / lat_total * quad_ref[...]
    for spot in range(2):
        same, other = unpack(op_sum.at[odd], spot), unpack(op_other, spot)
        for i in range(2):
            s = 2 * spot + i
            lone = (me == 0) & (s == 0)
            theirs = other[i]
            if s == 0:
                alone = jnp.concatenate([op_lone[0], op_lone[1, :, 0:edge]], axis=1)
                alone = jnp.where(upper, alone.astype(f32), across(unit, alone))
                theirs = jnp.where(kind == 0, alone, theirs)
            direct = jnp.where(odd == 0, same[i], theirs)
            mirror = jnp.where(odd == 0, theirs, same[i])

            def ordered(value):
                value = (value * scale).astype(bf16)
                value = jnp.dot(order, value, preferred_element_type=f32).astype(bf16)
                return across(value, order).astype(bf16)

            both[s, 0] = ordered(jnp.where(lone, direct, direct + mirror))
            both[s, 1] = ordered(jnp.where(lone, mirror, direct + mirror))
            gap[s] = ordered(jnp.where(lone, 0.0, direct - mirror))

    mix_rows(pairs - 1)

    def act(matrix, value):
        return jnp.dot(matrix, value, preferred_element_type=f32)

    for s in range(slots):
        re, im = 2 * s, 2 * s + 1
        cosine = act(both[s, 0], mixed_real[re]) - act(gap[s], mixed_imag[im])
        sine = act(gap[s], mixed_imag[re]) + act(both[s, 1], mixed_real[im])
        for q, value in ((re, cosine), (im, sine)):
            for p in range(pairs):
                for which in range(2):
                    at = p * bunch + which * devices
                    for c in range(lane_parts):
                        flat[p, c, pl.ds(8 * which + q, devices, stride=16), :] = value[
                            at : at + devices, c * 128 : (c + 1) * 128
                        ]

    start_back, wait_back = exchange(filtered, returned, back_sem, back_own)
    for p in range(pairs):
        value = jnp.concatenate([flat[p, c] for c in range(lane_parts)], axis=1)
        filtered[p] = value.astype(bf16).reshape(devices, 16, width)
        start_back(p)

    take_near(1)
    sea_half(1, 1 - comp)

    def grid_moves(p):
        found = []
        for k in range(1, col_count):
            other = (col + k) % col_count
            found.append(
                remote(
                    spatial.at[p, other],
                    spectral.at[p, col],
                    grid_sem,
                    (p, k - 1),
                    (lat, other // 2, other % 2),
                )
            )
        own = pltpu.make_async_copy(spatial.at[p, col], spectral.at[p, col], grid_own.at[p])
        return found + [own]

    def to_grid(p):
        wait_back(p)
        value = returned[p].astype(f32)
        for which in range(2):
            lines = value[:, 8 * which : 8 * which + 8].reshape(circle, width).astype(bf16)
            line = jnp.dot(waves_back[...], lines, preferred_element_type=f32).astype(bf16)
            for b in range(col_count):
                spatial[p, b, which] = line[b * lon_dev : (b + 1) * lon_dev]
        for move in grid_moves(p):
            move.start()

    def finish(p):
        for move in grid_moves(p):
            move.wait()

        @pl.loop(0, col_count // 2)
        def _(jj):
            here = pl.ds(2 * jj, 2)
            value = forced[p, here].reshape(2 * half_block, width)
            value = value + spectral[p, here].reshape(2 * half_block, width).astype(f32)
            inner = layer_norm(value, gain_ref[1:2]).astype(bf16)
            hidden = jax.nn.gelu(
                jnp.dot(inner, air_up[...], preferred_element_type=f32)
            ).astype(bf16)
            value = value + jnp.dot(hidden, air_down[...], preferred_element_type=f32)
            value = value.astype(bf16).reshape(2, 2, lon_dev, width)
            for j2 in range(2):
                air_out[pl.ds(band * (2 * jj + j2) + 2 * p, 2)] = value[j2]

    loads["back"].wait()
    loads["up"].wait()
    loads["down"].wait()
    to_grid(0)
    take_far(1)
    sea_half(1, comp)
    to_grid(1)
    finish(0)
    to_grid(2)
    finish(1)
    finish(2)


def whole_step(
    atm_state,
    ocean_state,
    wet_mask,
    legendre,
    quad_weight,
    spec_real,
    spec_imag,
    degree_gain,
    atm_gain,
    atm_up,
    atm_down,
    atm_to_surface,
    surface_to_atm,
    ocean_to_surface,
    surface_to_ocean,
    ocean_kernel,
    ocean_gain,
    ocean_up,
    ocean_down,
):
    bf16, f32 = jnp.bfloat16, jnp.float32
    devices = lax.axis_size(EVERY)
    col_count = lax.axis_size(COLUMNS)
    lat_dev, lon_dev, width = atm_state.shape
    rows, cols, sea_width = ocean_state.shape
    circle = lon_dev * col_count
    lat_total = legendre.shape[2]
    band = lat_dev // col_count
    reach = STENCIL_TAPS // 2 * OCEAN_DILATION
    slots = legendre.shape[0] // 4
    surface = atm_to_surface.shape[1]
    with jax.ensure_compile_time_eval():
        table = np.asarray(folded_waves(circle, devices).astype(f32))
    waves = jnp.asarray(table, f32).astype(bf16)
    waves_back = jnp.asarray(table.T, f32).astype(bf16)
    vmem = pl.BlockSpec(memory_space=pltpu.VMEM)
    hbm = pl.BlockSpec(memory_space=pl.ANY)
    pairs = band // 2
    tall = (pairs, devices, 16, width)
    patches = (pairs, col_count, 2, lon_dev, width)
    dma = pltpu.SemaphoreType.DMA
    return pl.pallas_call(
        functools.partial(whole_step_body, lat_total),
        out_shape=(
            jax.ShapeDtypeStruct(atm_state.shape, bf16),
            jax.ShapeDtypeStruct(ocean_state.shape, bf16),
        ),
        in_specs=[
            hbm, hbm, vmem, hbm, vmem, hbm, hbm, vmem, vmem, hbm, hbm,
            vmem, vmem, vmem, vmem, vmem, vmem, hbm, hbm, hbm, hbm,
        ],
        out_specs=(vmem, vmem),
        scratch_shapes=[
            pltpu.VMEM(atm_state.shape, bf16),
            pltpu.VMEM(ocean_state.shape, bf16),
            pltpu.VMEM((legendre.shape[0], lat_total, legendre.shape[1]), bf16),
            pltpu.VMEM(spec_real.shape, bf16),
            pltpu.VMEM(spec_imag.shape, bf16),
            pltpu.VMEM(atm_up.shape, bf16),
            pltpu.VMEM(atm_down.shape, bf16),
            pltpu.VMEM(ocean_up.shape, bf16),
            pltpu.VMEM(ocean_down.shape, bf16),
            pltpu.VMEM(waves.shape, bf16),
            pltpu.VMEM(waves.shape, bf16),
            pltpu.VMEM((2 * STENCIL_TAPS * STENCIL_TAPS, 1, sea_width), f32),
            pltpu.VMEM((128, 128), f32),
            pltpu.VMEM((rows, cols, 128), f32),
            pltpu.VMEM((2, 2, rows, lon_dev, surface), bf16),
            pltpu.VMEM((2, 2, rows, lon_dev, surface), bf16),
            pltpu.VMEM(patches, f32),
            pltpu.VMEM(patches, bf16),
            pltpu.VMEM(patches, bf16),
            pltpu.VMEM(tall, bf16),
            pltpu.VMEM(tall, bf16),
            pltpu.VMEM((pairs, width // 128, 16 * devices, 128), f32),
            pltpu.VMEM((16 * devices, width), bf16),
            pltpu.VMEM((8, lat_total, width), bf16),
            pltpu.VMEM((8, lat_total, width), bf16),
            pltpu.VMEM(tall, bf16),
            pltpu.VMEM(tall, bf16),
            pltpu.VMEM(patches, bf16),
            pltpu.VMEM(patches, bf16),
            pltpu.VMEM((4, 3 * lat_total + 16, 128), bf16),
            pltpu.VMEM((2, 3 * lat_total + 16, 128), bf16),
            pltpu.VMEM((2, 3 * lat_total + 16, 128), bf16),
            pltpu.VMEM((3 * lat_total + 16, 128), bf16),
            pltpu.VMEM((2, lat_total, 128), bf16),
            pltpu.VMEM((slots, 2, lat_total, lat_total), bf16),
            pltpu.VMEM((slots, lat_total, lat_total), bf16),
            pltpu.VMEM((2,) + ocean_state.shape, bf16),
            pltpu.VMEM((2, 2, reach, cols, sea_width), bf16),
            pltpu.VMEM((2, rows // 2, 16, sea_width), bf16),
            pltpu.VMEM((2, rows // 2, 16, sea_width), bf16),
            pltpu.VMEM((2, 2, reach // 2, 16, sea_width), bf16),
            pltpu.VMEM((rows + 2 * reach, cols + 16, sea_width), f32),
            pltpu.VMEM((reach // OCEAN_DILATION * cols, sea_width), f32),
            dma((11,)),
            dma((2,)),
            dma((2, 2)),
            dma((2, pairs, 3)),
            dma((pairs,)),
            dma((2, pairs, devices)),
            dma((pairs,)),
            dma((2, pairs, devices)),
            dma((pairs,)),
            dma((2, pairs, 3)),
            dma((pairs,)),
            dma((2, 5)),
            dma((2, 2, 5)),
        ],
        compiler_params=pltpu.CompilerParams(
            collective_id=0, has_side_effects=True, vmem_limit_bytes=60 * 1024 * 1024
        ),
    )(
        atm_state,
        ocean_state,
        wet_mask,
        jnp.swapaxes(legendre, 1, 2),
        quad_weight[None, :],
        spec_real,
        spec_imag,
        degree_gain,
        atm_gain,
        atm_up,
        atm_down,
        atm_to_surface.T,
        surface_to_atm,
        ocean_to_surface.T,
        surface_to_ocean,
        ocean_kernel.transpose(1, 2, 0, 3),
        ocean_gain,
        ocean_up,
        ocean_down,
        waves,
        waves_back,
    )


def local(
    atm_state,
    ocean_state,
    wet_mask,
    legendre,
    quad_weight,
    spec_real,
    spec_imag,
    degree_gain,
    atm_gain,
    atm_up,
    atm_down,
    atm_to_surface,
    surface_to_atm,
    ocean_to_surface,
    surface_to_ocean,
    ocean_kernel,
    ocean_gain,
    ocean_up,
    ocean_down,
):
    col_count = lax.axis_size(COLUMNS)
    lat_dev, lon_dev, _ = atm_state.shape
    circle = lon_dev * col_count
    if fits(atm_state, ocean_state, legendre):
        return whole_step(
            atm_state,
            ocean_state,
            wet_mask,
            legendre,
            quad_weight,
            spec_real,
            spec_imag,
            degree_gain,
            atm_gain,
            atm_up,
            atm_down,
            atm_to_surface,
            surface_to_atm,
            ocean_to_surface,
            surface_to_ocean,
            ocean_kernel,
            ocean_gain,
            ocean_up,
            ocean_down,
        )
    wet = wet_mask.astype(jnp.float32)[:, :, None]
    ocean_flux = (
        jnp.dot(ocean_state, ocean_to_surface, preferred_element_type=jnp.float32) * wet
    ).astype(jnp.bfloat16)
    atm_flux = jnp.dot(atm_state, atm_to_surface, preferred_element_type=jnp.float32).astype(
        jnp.bfloat16
    )
    flux_here = lax.all_to_all(ocean_flux, "comp", split_axis=1, concat_axis=0, tiled=True)
    flux_sea = lax.all_to_all(atm_flux, "comp", split_axis=0, concat_axis=1, tiled=True)
    forced = atm_state.astype(jnp.float32) + jnp.dot(
        flux_here, surface_to_atm, preferred_element_type=jnp.float32
    )
    normed = layer_norm(forced, atm_gain[0]).astype(jnp.bfloat16)
    run_spectral = (
        folded_spectral
        if folds(circle, lat_dev, col_count, lax.axis_size(EVERY))
        else plain_spectral
    )
    spectral, stages = run_spectral(
        normed, legendre, quad_weight, spec_real, spec_imag, degree_gain, circle
    )
    mixed = forced + spectral.astype(jnp.float32)
    normed_two = layer_norm(mixed, atm_gain[1]).astype(jnp.bfloat16)
    hidden = jax.nn.gelu(jnp.dot(normed_two, atm_up, preferred_element_type=jnp.float32)).astype(
        jnp.bfloat16
    )
    atm_out = (mixed + jnp.dot(hidden, atm_down, preferred_element_type=jnp.float32)).astype(
        jnp.bfloat16
    )
    ocean_in = (
        ocean_state.astype(jnp.float32)
        + wet * jnp.dot(flux_sea, surface_to_ocean, preferred_element_type=jnp.float32)
    ).astype(jnp.bfloat16)
    stencil_reach = STENCIL_TAPS // 2 * OCEAN_DILATION
    sides = ((("lat", "comp"), 0), ("lon", 1))
    current = ocean_in
    quick = ocean_in.shape[0] % (2 * OCEAN_DILATION) == 0 and ocean_in.shape[2] % 128 == 0
    for k in range(2):
        field = padded(current, sides, stencil_reach)
        weights = (ocean_kernel[k], ocean_gain[k], ocean_up[k], ocean_down[k])
        if quick:
            current = fast_ocean_block(field, *weights, stages[k])
        else:
            current = ocean_block(field, *weights)
    ocean_out = jnp.where(wet_mask[:, :, None] == 1, current, ocean_state)
    return (atm_out, ocean_out)


def solution(mesh):
    placed = (
        P("lat", ("lon", "comp"), None),
        P(("lat", "comp"), "lon", None),
        P(("lat", "comp"), "lon"),
        P(("lat", "lon", "comp"), None, None),
        P(),
        P(),
        P(),
        P(),
        P(),
        P(),
        P(),
        P(),
        P(),
        P(),
        P(),
        P(),
        P(),
        P(),
        P(),
    )

    return jax.shard_map(
        local,
        mesh=mesh,
        in_specs=placed,
        out_specs=(P("lat", ("lon", "comp"), None), P(("lat", "comp"), "lon", None)),
        check_vma=False,
    )
```

```python
import functools
import math

import jax
import jax.numpy as jnp
import numpy as np
from jax import lax
from jax.experimental import pallas as pl
from jax.experimental.pallas import tpu as pltpu
from jax.sharding import PartitionSpec as P

MODES = 512
STENCIL_TAPS = 7
OCEAN_DILATION = 2
COLUMNS = ("lon", "comp")
EVERY = ("lat", "lon", "comp")


epsilon = 1e-05


def padded(block, sides, width):
    for axis, dim in sides:
        count = lax.axis_size(axis)
        forward = [(i, i + 1) for i in range(count - 1)]
        backward = [(target, source) for source, target in forward]
        low = lax.ppermute(
            lax.slice_in_dim(block, block.shape[dim] - width, None, axis=dim), axis, forward
        )
        high = lax.ppermute(lax.slice_in_dim(block, 0, width, axis=dim), axis, backward)
        block = jnp.concatenate([low, block, high], axis=dim)
    return block


def layer_norm(values, gain):
    centred = values - jnp.mean(values, axis=-1, keepdims=True)
    spread = jnp.mean(centred * centred, axis=-1, keepdims=True)
    return centred * lax.rsqrt(spread + epsilon) * gain


def wave_table(row_index, circle):
    longitude = jnp.arange(circle, dtype=jnp.int32)
    wavenumber = row_index // 2
    phases = wavenumber[:, None] * longitude[None, :] % circle
    angles = phases.astype(jnp.float32) * (2.0 * math.pi / circle)
    waves = jnp.where((row_index % 2 == 0)[:, None], jnp.cos(angles), -jnp.sin(angles))
    return (wavenumber, waves)


def forward_table(row_index, circle):
    _, waves = wave_table(row_index, circle)
    return (waves.T / math.sqrt(circle)).astype(jnp.bfloat16)


def inverse_table(row_index, circle):
    wavenumber, waves = wave_table(row_index, circle)
    factor = jnp.where(wavenumber == 0, 1.0, 2.0).astype(jnp.float32)
    return (waves * factor[:, None] / math.sqrt(circle)).astype(jnp.bfloat16)


def reorder_rows(total_rows, owned, lat_count, col_count):
    positions = jnp.arange(total_rows, dtype=jnp.int32)
    stride = lat_count * owned
    return (
        owned * (positions % stride // owned * col_count + positions // stride) + positions % owned
    )


def spectral_filter(gathered, table, quad_weight, spec_real, spec_imag, degree_gain):
    count = table.shape[0]
    lat_total = table.shape[2]
    channels = gathered.shape[2]
    split_parts = gathered.reshape(lat_total, count, 2, channels)
    weighted = (table.astype(jnp.float32) * (quad_weight / lat_total)).astype(jnp.bfloat16)
    coeffs = jnp.einsum(
        "mln,nmpc->mplc", weighted, split_parts, preferred_element_type=jnp.float32
    ).astype(jnp.bfloat16)
    real_part = coeffs[:, 0]
    imag_part = coeffs[:, 1]
    mixed_real = jnp.dot(real_part, spec_real, preferred_element_type=jnp.float32) - jnp.dot(
        imag_part, spec_imag, preferred_element_type=jnp.float32
    )
    mixed_imag = jnp.dot(real_part, spec_imag, preferred_element_type=jnp.float32) + jnp.dot(
        imag_part, spec_real, preferred_element_type=jnp.float32
    )
    scaled = (jnp.stack([mixed_real, mixed_imag], axis=1) * degree_gain[:, None]).astype(
        jnp.bfloat16
    )
    returned = jnp.einsum(
        "mln,mplc->nmpc", table, scaled, preferred_element_type=jnp.float32
    ).astype(jnp.bfloat16)
    return returned.reshape(lat_total, 2 * count, channels)


def folds(circle, lat_dev, col_count, devices):
    return (
        MODES == 2 * circle
        and lat_dev % col_count == 0
        and devices % 4 == 0
        and (circle // 2) % devices == 0
        and (MODES // devices) % 4 == 0
    )


def place_of(kind, i, group):
    return kind * group + (group - 1 - i if kind % 2 else i)


def folded_waves(circle, devices):
    longitude = jnp.arange(circle, dtype=jnp.int32)
    position = jnp.arange(circle, dtype=jnp.int32)
    group = devices // 4
    owned = circle // devices
    owner = position // owned
    kind, place = owner // group, owner % group
    place = jnp.where(kind % 2 == 1, group - 1 - place, place)
    row_index = (4 * place + kind) * owned + position % owned
    wavenumber = jnp.where(row_index == 1, circle // 2, row_index // 2)
    phases = wavenumber[:, None] * longitude[None, :] % circle
    angles = phases.astype(jnp.float32) * (2.0 * math.pi / circle)
    cosine = ((row_index % 2 == 0) | (row_index == 1))[:, None]
    return jnp.where(cosine, jnp.cos(angles), -jnp.sin(angles)) / math.sqrt(circle)


def folded_operators(table, quad_weight, degree_gain):
    devices = lax.axis_size(EVERY)
    me = lax.axis_index(EVERY)
    count, _, lat_total = table.shape
    group = devices // 4
    part = count // 4
    family = me // group
    scaled = (table.astype(jnp.float32) * degree_gain[:, None]).astype(jnp.bfloat16)
    operators = jnp.einsum(
        "mlt,mlu->mtu", table, scaled, preferred_element_type=jnp.float32
    )
    operators = operators * (quad_weight / lat_total)
    first_scale = jnp.where(me == 0, 0.5, 1.0).astype(jnp.float32)
    scales = jnp.where(jnp.arange(count) == 0, first_scale, 1.0)
    operators = (operators * scales[:, None, None]).astype(jnp.bfloat16)
    turn = []
    for base in (group, 3 * group):
        for i in range(group):
            turn.append((base + (i + 1) % group, base + i))
    rotated = lax.ppermute(operators[:1], EVERY, turn)
    mirrored = jnp.concatenate([rotated, jnp.flip(operators[1:], axis=0)], axis=0)
    ordered = jnp.where(family % 2 == 1, mirrored, operators)
    received = [lax.dynamic_slice_in_dim(ordered, family * part, part, axis=0)]
    for shift in range(1, 4):
        pairs = []
        for i in range(group):
            for kind in range(4):
                pairs.append((place_of(kind, i, group), place_of(kind ^ shift, i, group)))
        piece = lax.dynamic_slice_in_dim(ordered, (family ^ shift) * part, part, axis=0)
        received.append(lax.ppermute(piece, EVERY, pairs))
    received = [value.astype(jnp.float32) for value in received]
    same = received[0] + received[2]
    other = received[1] + received[3]
    direct = jnp.where(family % 2 == 0, same, other)
    mirror = jnp.where(family % 2 == 0, other, same)
    lone = ((me == 0) & (jnp.arange(part) == 0))[:, None, None]
    both = direct + mirror
    gap = jnp.where(lone, 0.0, direct - mirror)
    top = jnp.concatenate([jnp.where(lone, direct, both), -gap], axis=2)
    bottom = jnp.concatenate([gap, jnp.where(lone, mirror, both)], axis=2)
    return (2.0 * top).astype(jnp.bfloat16), (2.0 * bottom).astype(jnp.bfloat16)


def folded_spectral(normed, legendre, quad_weight, spec_real, spec_imag, degree_gain, circle):
    width = normed.shape[2]
    top, bottom = folded_operators(legendre, quad_weight, degree_gain)
    slots = top.shape[0]
    waves = folded_waves(circle, lax.axis_size(EVERY)).astype(jnp.bfloat16)
    columns = lax.all_to_all(normed, COLUMNS, split_axis=0, concat_axis=1, tiled=True)
    spectrum = jnp.einsum(
        "rn,tnc->trc", waves, columns, preferred_element_type=jnp.float32
    ).astype(jnp.bfloat16)
    gathered = lax.all_to_all(spectrum, EVERY, split_axis=1, concat_axis=0, tiled=True)
    lat_total = gathered.shape[0]
    channels = jnp.concatenate([spec_real, spec_imag], axis=1)
    turned = gathered.reshape(lat_total, slots, 2, width).transpose(1, 2, 0, 3)
    mixed = jnp.dot(turned, channels, preferred_element_type=jnp.float32).astype(jnp.bfloat16)
    upper = jnp.concatenate([mixed[:, 0, :, :width], mixed[:, 1, :, width:]], axis=1)
    lower = jnp.concatenate([mixed[:, 0, :, width:], mixed[:, 1, :, :width]], axis=1)
    cosine = jnp.einsum("stu,suc->stc", top, upper, preferred_element_type=jnp.float32)
    sine = jnp.einsum("stu,suc->stc", bottom, lower, preferred_element_type=jnp.float32)
    filtered = jnp.stack([cosine, sine], axis=1).astype(jnp.bfloat16)
    filtered = filtered.reshape(2 * slots, lat_total, width).transpose(1, 0, 2)
    returned = lax.all_to_all(filtered, EVERY, split_axis=0, concat_axis=1, tiled=True)
    spatial = jnp.einsum(
        "rn,trc->tnc", waves, returned, preferred_element_type=jnp.float32
    ).astype(jnp.bfloat16)
    spectral = lax.all_to_all(spatial, COLUMNS, split_axis=1, concat_axis=0, tiled=True)
    return spectral, (spectrum, filtered)


def plain_spectral(normed, legendre, quad_weight, spec_real, spec_imag, degree_gain, circle):
    lat_count = lax.axis_size("lat")
    col_count = lax.axis_size(("lon", "comp"))
    total_rows = 2 * MODES
    owned = 2 * legendre.shape[0]
    natural = jnp.arange(total_rows, dtype=jnp.int32)
    columns = lax.all_to_all(normed, ("lon", "comp"), split_axis=2, concat_axis=1, tiled=True)
    forward = forward_table(natural, circle)
    inverse = inverse_table(reorder_rows(total_rows, owned, lat_count, col_count), circle)
    spectrum = jnp.einsum(
        "anc,nr->arc", columns, forward, preferred_element_type=jnp.float32
    ).astype(jnp.bfloat16)
    gathered = lax.all_to_all(
        lax.all_to_all(spectrum, "lat", split_axis=1, concat_axis=0, tiled=True),
        ("lon", "comp"),
        split_axis=1,
        concat_axis=2,
        tiled=True,
    )
    filtered = spectral_filter(gathered, legendre, quad_weight, spec_real, spec_imag, degree_gain)
    returned = lax.all_to_all(
        lax.all_to_all(filtered, "lat", split_axis=0, concat_axis=1, tiled=True),
        ("lon", "comp"),
        split_axis=2,
        concat_axis=1,
        tiled=True,
    )
    spatial = jnp.einsum(
        "arc,rn->anc", returned, inverse, preferred_element_type=jnp.float32
    ).astype(jnp.bfloat16)
    spectral = lax.all_to_all(spatial, COLUMNS, split_axis=1, concat_axis=2, tiled=True)
    return spectral, (spectrum, filtered)


def ocean_block(padded_field, kernel, gain, up_weight, down_weight):
    stencil_reach = STENCIL_TAPS // 2 * OCEAN_DILATION
    tile_height = padded_field.shape[0] - 2 * stencil_reach
    tile_breadth = padded_field.shape[1] - 2 * stencil_reach
    stencil = jnp.zeros((tile_height, tile_breadth, padded_field.shape[2]), jnp.float32)
    for row_offset_tap in range(STENCIL_TAPS):
        for column_tap in range(STENCIL_TAPS):
            stencil_window = padded_field[
                row_offset_tap * OCEAN_DILATION : row_offset_tap * OCEAN_DILATION + tile_height,
                column_tap * OCEAN_DILATION : column_tap * OCEAN_DILATION + tile_breadth,
            ]
            stencil = stencil + stencil_window.astype(jnp.float32) * kernel[
                row_offset_tap, column_tap
            ].astype(jnp.float32)
    normed = layer_norm(stencil, gain).astype(jnp.bfloat16)
    hidden = jax.nn.gelu(jnp.dot(normed, up_weight, preferred_element_type=jnp.float32)).astype(
        jnp.bfloat16
    )
    centre = padded_field[
        stencil_reach : stencil_reach + tile_height, stencil_reach : stencil_reach + tile_breadth
    ]
    return (
        centre.astype(jnp.float32)
        + jnp.dot(hidden, down_weight, preferred_element_type=jnp.float32)
    ).astype(jnp.bfloat16)


def ocean_kernel_body(
    field_ref, taps_ref, gain_ref, up_ref, down_ref, after_ref, out_ref, wide, normed
):
    rows, cols, width = out_ref.shape
    step = OCEAN_DILATION
    lanes = 128

    @pl.loop(0, rows + (STENCIL_TAPS - 1) * step)
    def _(row):
        wide[row] = field_ref[row].astype(jnp.float32)

    @pl.loop(0, rows // 2)
    def _(pair):
        base = pair // step * (2 * step) + pair % step
        for half in range(width // lanes):
            part = slice(half * lanes, (half + 1) * lanes)
            sums = [jnp.zeros((cols, lanes), jnp.float32) for _ in range(2)]
            for a in range(STENCIL_TAPS + 1):
                for b in range(STENCIL_TAPS):
                    window = wide[base + a * step, b * step : b * step + cols, part]
                    for which in range(2):
                        tap = a - which
                        if 0 <= tap < STENCIL_TAPS:
                            weight = taps_ref[tap * STENCIL_TAPS + b, :, part]
                            sums[which] = sums[which] + window * weight
            for which in range(2):
                normed[which * cols : (which + 1) * cols, part] = sums[which]
        stencil = normed[...]
        values = layer_norm(stencil, gain_ref[...]).astype(jnp.bfloat16)
        hidden = jax.nn.gelu(
            jnp.dot(values, up_ref[...], preferred_element_type=jnp.float32)
        ).astype(jnp.bfloat16)
        moved = jnp.dot(hidden, down_ref[...], preferred_element_type=jnp.float32)
        reach = STENCIL_TAPS // 2 * step
        for which in range(2):
            row = base + which * step
            centre = wide[row + reach, reach : reach + cols, :]
            out_ref[row] = (centre + moved[which * cols : (which + 1) * cols]).astype(
                out_ref.dtype
            )


def fast_ocean_block(field, kernel, gain, up_weight, down_weight, after):
    reach = STENCIL_TAPS // 2 * OCEAN_DILATION
    rows, cols, width = field.shape[0] - 2 * reach, field.shape[1] - 2 * reach, field.shape[2]
    hidden = up_weight.shape[1]
    taps = kernel.astype(jnp.float32).reshape(STENCIL_TAPS * STENCIL_TAPS, 1, width)
    whole = pl.BlockSpec(memory_space=pltpu.VMEM)
    cells = rows * cols
    return pl.pallas_call(
        ocean_kernel_body,
        out_shape=jax.ShapeDtypeStruct((rows, cols, width), jnp.bfloat16),
        in_specs=[whole] * 5 + [pl.BlockSpec(memory_space=pl.ANY)],
        out_specs=whole,
        scratch_shapes=[
            pltpu.VMEM(field.shape, jnp.float32),
            pltpu.VMEM((2 * cols, width), jnp.float32),
        ],
        compiler_params=pltpu.CompilerParams(vmem_limit_bytes=32 * 1024 * 1024),
        cost_estimate=pl.CostEstimate(
            flops=4 * cells * width * hidden + 98 * cells * width * 64,
            bytes_accessed=4 * field.size + 4 * up_weight.size,
            transcendentals=cells * hidden,
        ),
    )(field, taps, gain[None, :], up_weight, down_weight, after)


MESH_ID = pl.DeviceIdType.MESH


def fits(atm_state, ocean_state, legendre):
    devices = lax.axis_size(EVERY)
    col_count = lax.axis_size(COLUMNS)
    lat_dev, lon_dev, width = atm_state.shape
    rows, cols, sea_width = ocean_state.shape
    circle = lon_dev * col_count
    reach = STENCIL_TAPS // 2 * OCEAN_DILATION
    return (
        folds(circle, lat_dev, col_count, devices)
        and lax.axis_size("lon") == 2
        and lax.axis_size("comp") == 2
        and circle // devices == 8
        and legendre.shape[0] == 16
        and lat_dev // col_count == 6
        and lat_dev == 2 * rows
        and cols == 2 * lon_dev
        and cols == 128
        and rows == 2 * reach
        and rows % 6 == 0
        and reach % 2 == 0
        and rows % (2 * OCEAN_DILATION) == 0
        and 128 < legendre.shape[2] <= 192
        and legendre.shape[2] % 16 == 0
        and lon_dev % 16 == 0
        and width % 128 == 0
        and sea_width == 256
    )


def whole_step_body(
    lat_total,
    atm_hbm,
    sea_hbm,
    wet_hbm,
    legendre_hbm,
    quad_hbm,
    real_hbm,
    imag_hbm,
    degree_hbm,
    gain_hbm,
    up_hbm,
    down_hbm,
    to_sea_hbm,
    from_sea_hbm,
    to_air_hbm,
    from_air_hbm,
    taps_in_hbm,
    sea_gain_hbm,
    sea_up_hbm,
    sea_down_hbm,
    waves_hbm,
    waves_back_hbm,
    air_out,
    sea_out,
    wet_ref,
    quad_ref,
    degree_ref,
    gain_ref,
    to_sea_ref,
    from_sea_ref,
    to_air_ref,
    from_air_ref,
    taps_in_ref,
    sea_gain_ref,
    air,
    sea,
    legendre,
    spec_real,
    spec_imag,
    air_up,
    air_down,
    sea_up,
    sea_down,
    waves,
    waves_back,
    taps,
    wet_square,
    wet_full,
    flux_out,
    flux_in,
    forced,
    normed,
    columns,
    spec_send,
    gathered,
    flat,
    turned_rows,
    mixed_real,
    mixed_imag,
    filtered,
    returned,
    spatial,
    spectral,
    op_send,
    op_recv,
    op_sum,
    op_other,
    op_lone,
    both,
    gap,
    field,
    edges,
    strips,
    sides,
    corners,
    wide,
    stencil,
    load_sem,
    local_sem,
    flux_sem,
    column_sem,
    owner_sem,
    back_sem,
    grid_sem,
    op_sem,
    halo_sem,
):
    f32, bf16 = jnp.float32, jnp.bfloat16
    lat = lax.axis_index("lat")
    lon = lax.axis_index("lon")
    comp = lax.axis_index("comp")
    col_count = lax.axis_size(COLUMNS)
    devices = lax.axis_size(EVERY)
    group = devices // 4
    col = lon * 2 + comp
    me = lat * col_count + col
    tile = lat * 2 + comp
    tiles = lax.axis_size("lat") * 2
    lat_dev, lon_dev, width = air.shape
    rows, cols, sea_width = sea.shape
    band = lat_dev // col_count
    pairs = band // 2
    circle = lon_dev * col_count
    step = OCEAN_DILATION
    reach = STENCIL_TAPS // 2 * step
    slots = both.shape[0]

    def at_device(index):
        return (index // col_count, index % col_count // 2, index % 2)

    def at_tile(index, side):
        return (index // 2, side, index % 2)

    def remote(source, target, sems, k, where):
        place_in = k if isinstance(k, tuple) else (k,)
        return pltpu.make_async_remote_copy(
            src_ref=source,
            dst_ref=target,
            send_sem=sems.at[(0,) + place_in],
            recv_sem=sems.at[(1,) + place_in],
            device_id=where,
            device_id_type=MESH_ID,
        )

    def across(left, right):
        return lax.dot_general(left, right, (((1,), (1,)), ((), ())), preferred_element_type=f32)

    loads = {}
    for index, (name, source, target) in enumerate(
        (
            ("legendre", legendre_hbm, legendre),
            ("degree", degree_hbm, degree_ref),
            ("to_air", to_air_hbm, to_air_ref),
            ("wet", wet_hbm, wet_ref),
            ("sea", sea_hbm, sea),
            ("to_sea", to_sea_hbm, to_sea_ref),
            ("air", atm_hbm, air),
            ("from_sea", from_sea_hbm, from_sea_ref),
            ("gain", gain_hbm, gain_ref),
            ("from_air", from_air_hbm, from_air_ref),
            ("taps", taps_in_hbm, taps_in_ref),
            ("quad", quad_hbm, quad_ref),
            ("sea_gain", sea_gain_hbm, sea_gain_ref),
            ("waves", waves_hbm, waves),
            ("sea_up", sea_up_hbm, sea_up),
            ("sea_down", sea_down_hbm, sea_down),
            ("real", real_hbm, spec_real),
            ("imag", imag_hbm, spec_imag),
            ("back", waves_back_hbm, waves_back),
            ("up", up_hbm, air_up),
            ("down", down_hbm, air_down),
        )
    ):
        loads[name] = pltpu.make_async_copy(source, target, load_sem.at[index])
    early = 13
    for name in list(loads)[:early]:
        loads[name].start()

    barrier = pltpu.get_barrier_semaphore()

    @pl.loop(1, devices)
    def _(k):
        pl.semaphore_signal(
            barrier, inc=1, device_id=at_device((me + k) % devices), device_id_type=MESH_ID
        )

    loads["legendre"].wait()
    loads["degree"].wait()
    kind = me // group
    odd = kind % 2
    place = me % group
    count = legendre.shape[0]
    edge = lat_total - 128
    row_at = lax.broadcasted_iota(jnp.int32, (lat_total, lat_total), 0)
    lane_at = lax.broadcasted_iota(jnp.int32, (lat_total, lat_total), 1)
    upper, diagonal = row_at <= lane_at, row_at == lane_at

    def operator(k):
        index = odd * ((count - k) % count) + (1 - odd) * k
        table = legendre[index]
        scaled = (table.astype(f32) * degree_ref[...][None, :]).astype(bf16)
        return across(table, scaled) * jnp.where((me == 0) & (index == 0), 0.5, 1.0).astype(f32)

    high_half = kind // 2

    def fill_operators(first_group):
        @pl.loop(first_group, first_group + 2)
        def _(which):
            tails, marks = [], []
            for spot in range(2):
                first, second = operator(4 * which + 2 * spot), operator(4 * which + 2 * spot + 1)
                square = jnp.where(upper, first, second).astype(bf16)
                op_send[which, spot * lat_total : (spot + 1) * lat_total] = square[:, 0:128]
                tails.append(square[:, 128:lat_total])
                line = jnp.sum(jnp.where(diagonal, second, 0.0), axis=0, keepdims=True)
                marks.append(line[:, 0:128])
                marks.append(
                    jnp.concatenate(
                        [line[:, 128:lat_total], jnp.zeros((1, 128 - edge), f32)], axis=1
                    )
                )

            op_send[which, 2 * lat_total : 3 * lat_total, 0 : 2 * edge] = jnp.concatenate(
                tails, axis=1
            )
            at = lax.broadcasted_iota(jnp.int32, (16, 128), 0)
            lines = jnp.zeros((16, 128), f32)
            for i in range(4):
                lines = jnp.where(at == i, marks[i], lines)
            op_send[which, 3 * lat_total : 3 * lat_total + 16] = lines.astype(bf16)

    fill_operators(2 * (1 - high_half))
    pl.semaphore_wait(barrier, devices - 1)
    across_kind = (kind + 2) % 4
    op_first = [
        remote(
            op_send.at[2 * (1 - high_half) + j],
            op_recv.at[j],
            op_sem,
            k,
            at_device(across_kind * group + place),
        )
        for k, j in enumerate((1 - odd, odd))
    ]
    op_first[0].start()
    spot_of = odd * (group - 1 - place) + (1 - odd) * place
    beside = kind + 1 - 2 * odd
    beside_place = odd * spot_of + (1 - odd) * (group - 1 - spot_of)
    op_second = remote(
        op_sum.at[1 - odd], op_other, op_sem, 2, at_device(beside * group + beside_place)
    )
    lone_moves = [
        remote(
            op_sum.at[0, pl.ds(start, lat_total)],
            op_lone.at[k],
            op_sem,
            3 + k,
            at_device((group - place) % group),
        )
        for k, start in enumerate((0, 2 * lat_total))
    ]

    def sum_operators(j):
        mine = op_send[2 * high_half + j].astype(f32)
        op_sum[j] = (mine + op_recv[j].astype(f32)).astype(bf16)

    def pass_operators():
        op_first[0].wait()
        sum_operators(1 - odd)
        op_second.start()

        @pl.when(kind == 1)
        def _():
            for move in lone_moves:
                move.start()

    def keep_operators():
        op_first[1].wait()
        sum_operators(odd)

    loads["wet"].wait()
    wet_square[...] = jnp.zeros_like(wet_square)
    wet_square[0:rows, :] = wet_ref[...].astype(f32)
    turned = jnp.transpose(wet_square[...])
    for i in range(rows):
        wet_full[i] = jnp.broadcast_to(turned[:, i : i + 1], (cols, 128))

    loads["sea"].wait()
    loads["to_air"].wait()

    few = rows // 3
    for part in range(3):
        here = slice(part * few, (part + 1) * few)
        flux = across(sea[here].reshape(few * cols, sea_width), to_air_ref[...])
        flux = flux.reshape(few, cols, -1)
        flux = (flux * wet_full[here, :, 0 : flux.shape[2]]).astype(bf16)
        flux_out[0, 0, here] = flux[:, 0:lon_dev]
        flux_out[0, 1, here] = flux[:, lon_dev : 2 * lon_dev]

    partner = (lat, lon, 1 - comp)
    moves = []
    for part in range(2):
        moves.append(
            remote(flux_out.at[part, 1 - comp], flux_in.at[part, comp], flux_sem, part, partner)
        )
    moves[0].start()
    loads["air"].wait()
    loads["to_sea"].wait()

    for part in range(4):
        here = slice(part * rows // 2, (part + 1) * rows // 2)
        there = slice(part % 2 * rows // 2, (part % 2 + 1) * rows // 2)
        flux = across(air[here].reshape(rows // 2 * lon_dev, width), to_sea_ref[...])
        flux_out[1, part // 2, there] = flux.astype(bf16).reshape(rows // 2, lon_dev, -1)

    moves[1].start()
    kept = []
    for part in range(2):
        kept.append(
            pltpu.make_async_copy(
                flux_out.at[part, comp], flux_in.at[part, comp], local_sem.at[part]
            )
        )
        kept[-1].start()
    for name in list(loads)[early:]:
        loads[name].start()
    loads["from_sea"].wait()
    loads["gain"].wait()
    for move in kept:
        move.wait()
    moves[0].wait()


    def start_columns(p):
        for k in range(1, col_count):
            other = (col + k) % col_count
            remote(
                normed.at[p, other],
                columns.at[p, col],
                column_sem,
                p,
                (lat, other // 2, other % 2),
            ).start()
        pltpu.make_async_copy(normed.at[p, col], columns.at[p, col], column_sem.at[1, p]).start()

    def wait_columns(p):
        sent = normed.at[p, pl.ds(0, col_count - 1)]
        remote(sent, sent, column_sem, p, at_device(me)).wait_send()
        pltpu.make_async_copy(columns.at[p], columns.at[p], column_sem.at[1, p]).wait()

    half_block = 2 * lon_dev
    for p in range(pairs):

        @pl.loop(0, col_count // 2)
        def _(jj):
            for j2 in range(2):
                j = 2 * jj + j2
                row = band * j + 2 * p
                flux = flux_in[0, row // rows, pl.ds(row % rows, 2)].reshape(half_block, -1)
                value = air[pl.ds(row, 2)].reshape(half_block, width).astype(f32)
                value = value + jnp.dot(flux, from_sea_ref[...], preferred_element_type=f32)
                forced[p, j] = value.reshape(2, lon_dev, width)
                value = layer_norm(value, gain_ref[0:1]).astype(bf16)
                normed[p, j] = value.reshape(2, lon_dev, width)

        start_columns(p)

    loads["from_air"].wait()
    moves[1].wait()

    @pl.loop(0, rows)
    def _(i):
        flux = jnp.concatenate([flux_in[1, 0, i], flux_in[1, 1, i]], axis=0)
        added = jnp.dot(flux, from_air_ref[...], preferred_element_type=f32)
        mask = wet_full[i]
        mask = jnp.concatenate([mask, mask], axis=1)
        field[0, i] = (sea[i].astype(f32) + mask * added).astype(bf16)

    half_reach = reach // 2
    far = tile - 1 + 2 * comp
    has_far = (far >= 0) & (far < tiles)

    def pack_strips(k):
        @pl.loop(0, rows // 2)
        def _(i):
            found = []
            for which in range(2):
                low = field[k, 2 * i + which, 0:16].astype(f32)
                high = field[k, 2 * i + which, cols - 16 : cols].astype(f32)
                found.append(jnp.where(lon == 0, high[8:16], low[0:8]))
            strips[k, i] = jnp.concatenate(found, axis=0).astype(bf16)

    def side_move(k):
        return remote(strips.at[k], sides.at[k], halo_sem.at[k], 0, at_tile(tile, 1 - lon))

    def edge_moves(k, which):
        target = far if which else tile + 1 - 2 * comp
        upper_half = comp if which else 1 - comp
        return (
            remote(
                field.at[k, pl.ds(reach * upper_half, reach)],
                edges.at[k, which],
                halo_sem.at[k],
                1 + 2 * which,
                at_tile(target, lon),
            ),
            remote(
                strips.at[k, pl.ds(half_reach * upper_half, half_reach)],
                corners.at[k, which],
                halo_sem.at[k],
                2 + 2 * which,
                at_tile(target, 1 - lon),
            ),
        )

    def send_halo(k):
        pack_strips(k)

        @pl.when(has_far)
        def _():
            for move in edge_moves(k, 1):
                move.start()

        side_move(k).start()
        for move in edge_moves(k, 0):
            move.start()

    def margins(first, pair, values):
        for which in range(2):
            part = values[8 * which : 8 * which + 8]
            wide[first + 2 * pair + which, 0:8] = jnp.where(lon == 1, part, 0.0)
            wide[first + 2 * pair + which, cols + 8 : cols + 16] = jnp.where(lon == 0, part, 0.0)

    def fill_edge(k, which, first):
        @pl.loop(0, reach)
        def _(i):
            wide[first + i, 8 : cols + 8] = edges[k, which, i].astype(f32)

        @pl.loop(0, half_reach)
        def _(i):
            margins(first, i, corners[k, which, i].astype(f32))

    def take_near(k):
        @pl.loop(0, rows)
        def _(i):
            wide[reach + i, 8 : cols + 8] = field[k, i].astype(f32)

        side_move(k).wait()
        for move in edge_moves(k, 0):
            move.wait()

        @pl.loop(0, rows // 2)
        def _(i):
            margins(reach, i, sides[k, i].astype(f32))

        fill_edge(k, 0, (reach + rows) * (1 - comp))

    def take_far(k):
        first = (reach + rows) * comp

        @pl.when(has_far)
        def _():
            for move in edge_moves(k, 1):
                move.wait()
            fill_edge(k, 1, first)

        @pl.when(jnp.logical_not(has_far))
        def _():
            @pl.loop(0, reach)
            def _(i):
                wide[first + i] = jnp.zeros(wide.shape[1:], f32)

    send_halo(0)
    op_first[1].start()
    loads["taps"].wait()
    loads["quad"].wait()
    loads["sea_gain"].wait()

    for a in range(STENCIL_TAPS):
        for b in range(STENCIL_TAPS):
            line = taps_in_ref[a, b].astype(f32)
            for k in range(2):
                taps[(k * STENCIL_TAPS + a) * STENCIL_TAPS + b] = line[k : k + 1]

    fill_operators(2 * high_half)

    triple = reach // step
    slab = cols // 2

    def sea_half(k, upper_half, after=None):
        @pl.loop(0, step)
        def _(parity):
            base = upper_half * reach + parity
            for half in range(sea_width // 128):
                part = slice(half * 128, (half + 1) * 128)
                for side in range(2):
                    sums = [jnp.zeros((slab, 128), f32) for _ in range(triple)]
                    for a in range(STENCIL_TAPS + triple - 1):
                        for b in range(STENCIL_TAPS):
                            start = 8 - reach + b * step + side * slab
                            window = wide[base + a * step, start : start + slab, part]
                            for which in range(triple):
                                tap = a - which
                                if 0 <= tap < STENCIL_TAPS:
                                    weight = taps[
                                        (k * STENCIL_TAPS + tap) * STENCIL_TAPS + b, :, part
                                    ]
                                    sums[which] = sums[which] + window * weight
                    for which in range(triple):
                        at = which * cols + side * slab
                        stencil[at : at + slab, part] = sums[which]
            values = layer_norm(stencil[...], sea_gain_ref[k : k + 1]).astype(bf16)
            hidden = jax.nn.gelu(
                jnp.dot(values, sea_up[k], preferred_element_type=f32)
            ).astype(bf16)
            moved = jnp.dot(hidden, sea_down[k], preferred_element_type=f32)
            for which in range(triple):
                row = base + which * step
                centre = wide[row + reach, 8 : 8 + cols, :]
                value = (centre + moved[which * cols : (which + 1) * cols]).astype(bf16)
                if k == 0:
                    field[1, row] = value
                else:
                    mask = wet_full[row]
                    mask = jnp.concatenate([mask, mask], axis=1)
                    sea_out[row] = jnp.where(mask > 0.5, value, sea[row])

            if after is not None:
                after(parity)

    def exchange(source, target, sems):
        def start(p):
            @pl.loop(1, devices)
            def _(k):
                other = (me + k) % devices
                remote(source.at[p, other], target.at[p, me], sems, p, at_device(other)).start()

            pltpu.make_async_copy(source.at[p, me], target.at[p, me], sems.at[1, p]).start()

        def wait(p):
            sent = source.at[p, pl.ds(0, devices - 1)]
            remote(sent, sent, sems, p, at_device(me)).wait_send()
            pltpu.make_async_copy(target.at[p], target.at[p], sems.at[1, p]).wait()

        return start, wait

    start_owner, wait_owner = exchange(spec_send, gathered, owner_sem)
    loads["waves"].wait()

    for p in range(pairs):
        wait_columns(p)
        found = []
        for which in range(2):
            lines = jnp.concatenate([columns[p, b, which] for b in range(col_count)], axis=0)
            value = jnp.dot(waves[...], lines, preferred_element_type=f32)
            found.append(value.reshape(devices, 8, width))
        spec_send[p] = jnp.concatenate(found, axis=1).astype(bf16)
        start_owner(p)

    pass_operators()
    take_near(0)
    loads["sea_up"].wait()
    loads["sea_down"].wait()
    sea_half(0, 1 - comp)
    take_far(0)
    sea_half(0, comp)
    send_halo(1)
    keep_operators()

    loads["real"].wait()
    loads["imag"].wait()

    lane_parts = width // 128
    bunch = 2 * devices

    def mix_rows(p):
        wait_owner(p)
        value = gathered[p].astype(f32).reshape(16 * devices, width)
        for c in range(lane_parts):
            flat[p, c] = value[:, c * 128 : (c + 1) * 128]
        for q in range(8):
            for which in range(2):
                taken = [
                    flat[p, c, pl.ds(8 * which + q, devices, stride=16), :]
                    for c in range(lane_parts)
                ]
                at = q * bunch + which * devices
                turned_rows[at : at + devices] = jnp.concatenate(taken, axis=1).astype(bf16)
        for target, matrix in ((mixed_real, spec_real), (mixed_imag, spec_imag)):
            value = jnp.dot(turned_rows[...], matrix[...], preferred_element_type=f32)
            target[:, p * bunch : (p + 1) * bunch] = value.astype(bf16).reshape(8, bunch, width)

    for p in range(pairs - 1):
        mix_rows(p)

    op_second.wait()

    @pl.when(kind == 1)
    def _():
        for move in lone_moves:
            move.wait_send()

    @pl.when(kind == 0)
    def _():
        for move in lone_moves:
            move.wait_recv()

    pair_at, rest_at = row_at // (2 * devices), row_at % (2 * devices)
    source_at = band * (rest_at % devices) + 2 * pair_at + rest_at // devices
    order = jnp.where(lane_at == source_at, 1.0, 0.0).astype(bf16)
    unit = jnp.where(diagonal, 1.0, 0.0).astype(bf16)

    def unpack(packed, spot):
        lanes = slice(spot * edge, (spot + 1) * edge)
        square = jnp.concatenate(
            [
                packed[spot * lat_total : (spot + 1) * lat_total],
                packed[2 * lat_total : 3 * lat_total, lanes],
            ],
            axis=1,
        )
        flipped = across(unit, square)
        square = square.astype(f32)
        lines = packed[3 * lat_total : 3 * lat_total + 16].astype(f32)
        line = jnp.concatenate(
            [lines[2 * spot : 2 * spot + 1], lines[2 * spot + 1 : 2 * spot + 2, 0:edge]], axis=1
        )
        first = jnp.where(upper, square, flipped)
        second = jnp.where(upper, jnp.where(diagonal, line, flipped), square)
        return first, second

    scale = 2.0 / lat_total * quad_ref[...]
    for spot in range(2):
        same, other = unpack(op_sum.at[odd], spot), unpack(op_other, spot)
        for i in range(2):
            s = 2 * spot + i
            lone = (me == 0) & (s == 0)
            theirs = other[i]
            if s == 0:
                alone = jnp.concatenate([op_lone[0], op_lone[1, :, 0:edge]], axis=1)
                alone = jnp.where(upper, alone.astype(f32), across(unit, alone))
                theirs = jnp.where(kind == 0, alone, theirs)
            direct = jnp.where(odd == 0, same[i], theirs)
            mirror = jnp.where(odd == 0, theirs, same[i])

            def ordered(value):
                value = (value * scale).astype(bf16)
                value = jnp.dot(order, value, preferred_element_type=f32).astype(bf16)
                return across(value, order).astype(bf16)

            both[s, 0] = ordered(jnp.where(lone, direct, direct + mirror))
            both[s, 1] = ordered(jnp.where(lone, mirror, direct + mirror))
            gap[s] = ordered(jnp.where(lone, 0.0, direct - mirror))

    mix_rows(pairs - 1)

    def act(matrix, value):
        return jnp.dot(matrix, value, preferred_element_type=f32)

    for s in range(slots):
        re, im = 2 * s, 2 * s + 1
        cosine = act(both[s, 0], mixed_real[re]) - act(gap[s], mixed_imag[im])
        sine = act(gap[s], mixed_imag[re]) + act(both[s, 1], mixed_real[im])
        for q, value in ((re, cosine), (im, sine)):
            for p in range(pairs):
                for which in range(2):
                    at = p * bunch + which * devices
                    for c in range(lane_parts):
                        flat[p, c, pl.ds(8 * which + q, devices, stride=16), :] = value[
                            at : at + devices, c * 128 : (c + 1) * 128
                        ]

    start_back, wait_back = exchange(filtered, returned, back_sem)

    def send_back(p):
        value = jnp.concatenate([flat[p, c] for c in range(lane_parts)], axis=1)
        filtered[p] = value.astype(bf16).reshape(devices, 16, width)
        start_back(p)

    def send_later(parity):
        for p in range(1, pairs):

            @pl.when(parity == p - 1)
            def _():
                send_back(p)

    send_back(0)
    take_near(1)
    sea_half(1, 1 - comp, send_later)

    def start_grid(p, which):
        sems = grid_sem
        for k in range(1, col_count):
            other = (col + k) % col_count
            remote(
                spatial.at[p, other, which],
                spectral.at[p, col, which],
                sems,
                2 * p + which,
                (lat, other // 2, other % 2),
            ).start()
        pltpu.make_async_copy(
            spatial.at[p, col, which], spectral.at[p, col, which], sems.at[1, 2 * p + which]
        ).start()

    def wait_grid(p, which):
        sent = spatial.at[p, pl.ds(0, col_count - 1), which]
        remote(sent, sent, grid_sem, 2 * p + which, at_device(me)).wait_send()
        here = spectral.at[p, :, which]
        pltpu.make_async_copy(here, here, grid_sem.at[1, 2 * p + which]).wait()

    def to_grid(p):
        wait_back(p)
        for which in range(2):
            lines = returned[p, :, 8 * which : 8 * which + 8].astype(f32)
            lines = lines.reshape(circle, width).astype(bf16)
            line = jnp.dot(waves_back[...], lines, preferred_element_type=f32).astype(bf16)
            for b in range(col_count):
                spatial[p, b, which] = line[b * lon_dev : (b + 1) * lon_dev]
            start_grid(p, which)

    def finish(p):

        @pl.loop(0, 2)
        def _(which):
            wait_grid(p, which)
            value = forced[p, :, which].reshape(col_count * lon_dev, width)
            value = value + spectral[p, :, which].reshape(col_count * lon_dev, width).astype(f32)
            inner = layer_norm(value, gain_ref[1:2]).astype(bf16)
            hidden = jax.nn.gelu(
                jnp.dot(inner, air_up[...], preferred_element_type=f32)
            ).astype(bf16)
            value = value + jnp.dot(hidden, air_down[...], preferred_element_type=f32)
            value = value.astype(bf16).reshape(col_count, lon_dev, width)
            for j in range(col_count):
                air_out[band * j + 2 * p + which] = value[j]

    loads["back"].wait()
    loads["up"].wait()
    loads["down"].wait()
    take_far(1)

    def between(parity):
        @pl.when(parity == 0)
        def _():
            to_grid(0)

    sea_half(1, comp, between)
    to_grid(1)
    finish(0)
    to_grid(2)
    finish(1)
    finish(2)


def whole_step(
    atm_state,
    ocean_state,
    wet_mask,
    legendre,
    quad_weight,
    spec_real,
    spec_imag,
    degree_gain,
    atm_gain,
    atm_up,
    atm_down,
    atm_to_surface,
    surface_to_atm,
    ocean_to_surface,
    surface_to_ocean,
    ocean_kernel,
    ocean_gain,
    ocean_up,
    ocean_down,
):
    bf16, f32 = jnp.bfloat16, jnp.float32
    devices = lax.axis_size(EVERY)
    col_count = lax.axis_size(COLUMNS)
    lat_dev, lon_dev, width = atm_state.shape
    rows, cols, sea_width = ocean_state.shape
    circle = lon_dev * col_count
    lat_total = legendre.shape[2]
    band = lat_dev // col_count
    reach = STENCIL_TAPS // 2 * OCEAN_DILATION
    slots = legendre.shape[0] // 4
    surface = atm_to_surface.shape[1]
    with jax.ensure_compile_time_eval():
        table = np.asarray(folded_waves(circle, devices).astype(f32))
    waves = jnp.asarray(table, f32).astype(bf16)
    waves_back = jnp.asarray(table.T, f32).astype(bf16)
    vmem = pl.BlockSpec(memory_space=pltpu.VMEM)
    hbm = pl.BlockSpec(memory_space=pl.ANY)
    pairs = band // 2
    tall = (pairs, devices, 16, width)
    patches = (pairs, col_count, 2, lon_dev, width)
    dma = pltpu.SemaphoreType.DMA
    return pl.pallas_call(
        functools.partial(whole_step_body, lat_total),
        out_shape=(
            pltpu.VMEM(atm_state.shape, bf16),
            pltpu.VMEM(ocean_state.shape, bf16),
        ),
        in_specs=[
            hbm
        ] * 21,
        out_specs=(vmem, vmem),
        scratch_shapes=[
            pltpu.VMEM(wet_mask.shape, jnp.int32),
            pltpu.VMEM((1, lat_total), f32),
            pltpu.VMEM(degree_gain.shape, f32),
            pltpu.VMEM(atm_gain.shape, f32),
            pltpu.VMEM(atm_to_surface.shape[::-1], bf16),
            pltpu.VMEM(surface_to_atm.shape, bf16),
            pltpu.VMEM(ocean_to_surface.shape[::-1], bf16),
            pltpu.VMEM(surface_to_ocean.shape, bf16),
            pltpu.VMEM((STENCIL_TAPS, STENCIL_TAPS, 2, sea_width), bf16),
            pltpu.VMEM(ocean_gain.shape, f32),
            pltpu.VMEM(atm_state.shape, bf16),
            pltpu.VMEM(ocean_state.shape, bf16),
            pltpu.VMEM((legendre.shape[0], lat_total, legendre.shape[1]), bf16),
            pltpu.VMEM(spec_real.shape, bf16),
            pltpu.VMEM(spec_imag.shape, bf16),
            pltpu.VMEM(atm_up.shape, bf16),
            pltpu.VMEM(atm_down.shape, bf16),
            pltpu.VMEM(ocean_up.shape, bf16),
            pltpu.VMEM(ocean_down.shape, bf16),
            pltpu.VMEM(waves.shape, bf16),
            pltpu.VMEM(waves.shape, bf16),
            pltpu.VMEM((2 * STENCIL_TAPS * STENCIL_TAPS, 1, sea_width), f32),
            pltpu.VMEM((128, 128), f32),
            pltpu.VMEM((rows, cols, 128), f32),
            pltpu.VMEM((2, 2, rows, lon_dev, surface), bf16),
            pltpu.VMEM((2, 2, rows, lon_dev, surface), bf16),
            pltpu.VMEM(patches, f32),
            pltpu.VMEM(patches, bf16),
            pltpu.VMEM(patches, bf16),
            pltpu.VMEM(tall, bf16),
            pltpu.VMEM(tall, bf16),
            pltpu.VMEM((pairs, width // 128, 16 * devices, 128), f32),
            pltpu.VMEM((16 * devices, width), bf16),
            pltpu.VMEM((8, lat_total, width), bf16),
            pltpu.VMEM((8, lat_total, width), bf16),
            pltpu.VMEM(tall, bf16),
            pltpu.VMEM(tall, bf16),
            pltpu.VMEM(patches, bf16),
            pltpu.VMEM(patches, bf16),
            pltpu.VMEM((4, 3 * lat_total + 16, 128), bf16),
            pltpu.VMEM((2, 3 * lat_total + 16, 128), bf16),
            pltpu.VMEM((2, 3 * lat_total + 16, 128), bf16),
            pltpu.VMEM((3 * lat_total + 16, 128), bf16),
            pltpu.VMEM((2, lat_total, 128), bf16),
            pltpu.VMEM((slots, 2, lat_total, lat_total), bf16),
            pltpu.VMEM((slots, lat_total, lat_total), bf16),
            pltpu.VMEM((2,) + ocean_state.shape, bf16),
            pltpu.VMEM((2, 2, reach, cols, sea_width), bf16),
            pltpu.VMEM((2, rows // 2, 16, sea_width), bf16),
            pltpu.VMEM((2, rows // 2, 16, sea_width), bf16),
            pltpu.VMEM((2, 2, reach // 2, 16, sea_width), bf16),
            pltpu.VMEM((rows + 2 * reach, cols + 16, sea_width), f32),
            pltpu.VMEM((reach // OCEAN_DILATION * cols, sea_width), f32),
            dma((21,)),
            dma((2,)),
            dma((2, 2)),
            dma((2, pairs)),
            dma((2, pairs)),
            dma((2, pairs)),
            dma((2, 2 * pairs)),
            dma((2, 5)),
            dma((2, 2, 5)),
        ],
        compiler_params=pltpu.CompilerParams(
            collective_id=0, has_side_effects=True, vmem_limit_bytes=56 * 1024 * 1024
        ),
    )(
        atm_state,
        ocean_state,
        wet_mask,
        jnp.swapaxes(legendre, 1, 2),
        quad_weight[None, :],
        spec_real,
        spec_imag,
        degree_gain,
        atm_gain,
        atm_up,
        atm_down,
        atm_to_surface.T,
        surface_to_atm,
        ocean_to_surface.T,
        surface_to_ocean,
        ocean_kernel.transpose(1, 2, 0, 3),
        ocean_gain,
        ocean_up,
        ocean_down,
        waves,
        waves_back,
    )


def local(
    atm_state,
    ocean_state,
    wet_mask,
    legendre,
    quad_weight,
    spec_real,
    spec_imag,
    degree_gain,
    atm_gain,
    atm_up,
    atm_down,
    atm_to_surface,
    surface_to_atm,
    ocean_to_surface,
    surface_to_ocean,
    ocean_kernel,
    ocean_gain,
    ocean_up,
    ocean_down,
):
    col_count = lax.axis_size(COLUMNS)
    lat_dev, lon_dev, _ = atm_state.shape
    circle = lon_dev * col_count
    if fits(atm_state, ocean_state, legendre):
        return whole_step(
            atm_state,
            ocean_state,
            wet_mask,
            legendre,
            quad_weight,
            spec_real,
            spec_imag,
            degree_gain,
            atm_gain,
            atm_up,
            atm_down,
            atm_to_surface,
            surface_to_atm,
            ocean_to_surface,
            surface_to_ocean,
            ocean_kernel,
            ocean_gain,
            ocean_up,
            ocean_down,
        )
    wet = wet_mask.astype(jnp.float32)[:, :, None]
    ocean_flux = (
        jnp.dot(ocean_state, ocean_to_surface, preferred_element_type=jnp.float32) * wet
    ).astype(jnp.bfloat16)
    atm_flux = jnp.dot(atm_state, atm_to_surface, preferred_element_type=jnp.float32).astype(
        jnp.bfloat16
    )
    flux_here = lax.all_to_all(ocean_flux, "comp", split_axis=1, concat_axis=0, tiled=True)
    flux_sea = lax.all_to_all(atm_flux, "comp", split_axis=0, concat_axis=1, tiled=True)
    forced = atm_state.astype(jnp.float32) + jnp.dot(
        flux_here, surface_to_atm, preferred_element_type=jnp.float32
    )
    normed = layer_norm(forced, atm_gain[0]).astype(jnp.bfloat16)
    run_spectral = (
        folded_spectral
        if folds(circle, lat_dev, col_count, lax.axis_size(EVERY))
        else plain_spectral
    )
    spectral, stages = run_spectral(
        normed, legendre, quad_weight, spec_real, spec_imag, degree_gain, circle
    )
    mixed = forced + spectral.astype(jnp.float32)
    normed_two = layer_norm(mixed, atm_gain[1]).astype(jnp.bfloat16)
    hidden = jax.nn.gelu(jnp.dot(normed_two, atm_up, preferred_element_type=jnp.float32)).astype(
        jnp.bfloat16
    )
    atm_out = (mixed + jnp.dot(hidden, atm_down, preferred_element_type=jnp.float32)).astype(
        jnp.bfloat16
    )
    ocean_in = (
        ocean_state.astype(jnp.float32)
        + wet * jnp.dot(flux_sea, surface_to_ocean, preferred_element_type=jnp.float32)
    ).astype(jnp.bfloat16)
    stencil_reach = STENCIL_TAPS // 2 * OCEAN_DILATION
    sides = ((("lat", "comp"), 0), ("lon", 1))
    current = ocean_in
    quick = ocean_in.shape[0] % (2 * OCEAN_DILATION) == 0 and ocean_in.shape[2] % 128 == 0
    for k in range(2):
        field = padded(current, sides, stencil_reach)
        weights = (ocean_kernel[k], ocean_gain[k], ocean_up[k], ocean_down[k])
        if quick:
            current = fast_ocean_block(field, *weights, stages[k])
        else:
            current = ocean_block(field, *weights)
    ocean_out = jnp.where(wet_mask[:, :, None] == 1, current, ocean_state)
    return (atm_out, ocean_out)


def solution(mesh):
    placed = (
        P("lat", ("lon", "comp"), None),
        P(("lat", "comp"), "lon", None),
        P(("lat", "comp"), "lon"),
        P(("lat", "lon", "comp"), None, None),
        P(),
        P(),
        P(),
        P(),
        P(),
        P(),
        P(),
        P(),
        P(),
        P(),
        P(),
        P(),
        P(),
        P(),
        P(),
    )

    return jax.shard_map(
        local,
        mesh=mesh,
        in_specs=placed,
        out_specs=(P("lat", ("lon", "comp"), None), P(("lat", "comp"), "lon", None)),
        check_vma=False,
    )
```

```python
import functools
import math

import jax
import jax.numpy as jnp
import numpy as np
from jax import lax
from jax.experimental import pallas as pl
from jax.experimental.pallas import tpu as pltpu
from jax.sharding import PartitionSpec as P

MODES = 512
STENCIL_TAPS = 7
OCEAN_DILATION = 2
COLUMNS = ("lon", "comp")
EVERY = ("lat", "lon", "comp")


epsilon = 1e-05


def padded(block, sides, width):
    for axis, dim in sides:
        count = lax.axis_size(axis)
        forward = [(i, i + 1) for i in range(count - 1)]
        backward = [(target, source) for source, target in forward]
        low = lax.ppermute(
            lax.slice_in_dim(block, block.shape[dim] - width, None, axis=dim), axis, forward
        )
        high = lax.ppermute(lax.slice_in_dim(block, 0, width, axis=dim), axis, backward)
        block = jnp.concatenate([low, block, high], axis=dim)
    return block


def layer_norm(values, gain):
    centred = values - jnp.mean(values, axis=-1, keepdims=True)
    spread = jnp.mean(centred * centred, axis=-1, keepdims=True)
    return centred * lax.rsqrt(spread + epsilon) * gain


def wave_table(row_index, circle):
    longitude = jnp.arange(circle, dtype=jnp.int32)
    wavenumber = row_index // 2
    phases = wavenumber[:, None] * longitude[None, :] % circle
    angles = phases.astype(jnp.float32) * (2.0 * math.pi / circle)
    waves = jnp.where((row_index % 2 == 0)[:, None], jnp.cos(angles), -jnp.sin(angles))
    return (wavenumber, waves)


def forward_table(row_index, circle):
    _, waves = wave_table(row_index, circle)
    return (waves.T / math.sqrt(circle)).astype(jnp.bfloat16)


def inverse_table(row_index, circle):
    wavenumber, waves = wave_table(row_index, circle)
    factor = jnp.where(wavenumber == 0, 1.0, 2.0).astype(jnp.float32)
    return (waves * factor[:, None] / math.sqrt(circle)).astype(jnp.bfloat16)


def reorder_rows(total_rows, owned, lat_count, col_count):
    positions = jnp.arange(total_rows, dtype=jnp.int32)
    stride = lat_count * owned
    return (
        owned * (positions % stride // owned * col_count + positions // stride) + positions % owned
    )


def spectral_filter(gathered, table, quad_weight, spec_real, spec_imag, degree_gain):
    count = table.shape[0]
    lat_total = table.shape[2]
    channels = gathered.shape[2]
    split_parts = gathered.reshape(lat_total, count, 2, channels)
    weighted = (table.astype(jnp.float32) * (quad_weight / lat_total)).astype(jnp.bfloat16)
    coeffs = jnp.einsum(
        "mln,nmpc->mplc", weighted, split_parts, preferred_element_type=jnp.float32
    ).astype(jnp.bfloat16)
    real_part = coeffs[:, 0]
    imag_part = coeffs[:, 1]
    mixed_real = jnp.dot(real_part, spec_real, preferred_element_type=jnp.float32) - jnp.dot(
        imag_part, spec_imag, preferred_element_type=jnp.float32
    )
    mixed_imag = jnp.dot(real_part, spec_imag, preferred_element_type=jnp.float32) + jnp.dot(
        imag_part, spec_real, preferred_element_type=jnp.float32
    )
    scaled = (jnp.stack([mixed_real, mixed_imag], axis=1) * degree_gain[:, None]).astype(
        jnp.bfloat16
    )
    returned = jnp.einsum(
        "mln,mplc->nmpc", table, scaled, preferred_element_type=jnp.float32
    ).astype(jnp.bfloat16)
    return returned.reshape(lat_total, 2 * count, channels)


def folds(circle, lat_dev, col_count, devices):
    return (
        MODES == 2 * circle
        and lat_dev % col_count == 0
        and devices % 4 == 0
        and (circle // 2) % devices == 0
        and (MODES // devices) % 4 == 0
    )


def place_of(kind, i, group):
    return kind * group + (group - 1 - i if kind % 2 else i)


def folded_waves(circle, devices):
    longitude = jnp.arange(circle, dtype=jnp.int32)
    position = jnp.arange(circle, dtype=jnp.int32)
    group = devices // 4
    owned = circle // devices
    owner = position // owned
    kind, place = owner // group, owner % group
    place = jnp.where(kind % 2 == 1, group - 1 - place, place)
    row_index = (4 * place + kind) * owned + position % owned
    wavenumber = jnp.where(row_index == 1, circle // 2, row_index // 2)
    phases = wavenumber[:, None] * longitude[None, :] % circle
    angles = phases.astype(jnp.float32) * (2.0 * math.pi / circle)
    cosine = ((row_index % 2 == 0) | (row_index == 1))[:, None]
    return jnp.where(cosine, jnp.cos(angles), -jnp.sin(angles)) / math.sqrt(circle)


def folded_operators(table, quad_weight, degree_gain):
    devices = lax.axis_size(EVERY)
    me = lax.axis_index(EVERY)
    count, _, lat_total = table.shape
    group = devices // 4
    part = count // 4
    family = me // group
    scaled = (table.astype(jnp.float32) * degree_gain[:, None]).astype(jnp.bfloat16)
    operators = jnp.einsum(
        "mlt,mlu->mtu", table, scaled, preferred_element_type=jnp.float32
    )
    operators = operators * (quad_weight / lat_total)
    first_scale = jnp.where(me == 0, 0.5, 1.0).astype(jnp.float32)
    scales = jnp.where(jnp.arange(count) == 0, first_scale, 1.0)
    operators = (operators * scales[:, None, None]).astype(jnp.bfloat16)
    turn = []
    for base in (group, 3 * group):
        for i in range(group):
            turn.append((base + (i + 1) % group, base + i))
    rotated = lax.ppermute(operators[:1], EVERY, turn)
    mirrored = jnp.concatenate([rotated, jnp.flip(operators[1:], axis=0)], axis=0)
    ordered = jnp.where(family % 2 == 1, mirrored, operators)
    received = [lax.dynamic_slice_in_dim(ordered, family * part, part, axis=0)]
    for shift in range(1, 4):
        pairs = []
        for i in range(group):
            for kind in range(4):
                pairs.append((place_of(kind, i, group), place_of(kind ^ shift, i, group)))
        piece = lax.dynamic_slice_in_dim(ordered, (family ^ shift) * part, part, axis=0)
        received.append(lax.ppermute(piece, EVERY, pairs))
    received = [value.astype(jnp.float32) for value in received]
    same = received[0] + received[2]
    other = received[1] + received[3]
    direct = jnp.where(family % 2 == 0, same, other)
    mirror = jnp.where(family % 2 == 0, other, same)
    lone = ((me == 0) & (jnp.arange(part) == 0))[:, None, None]
    both = direct + mirror
    gap = jnp.where(lone, 0.0, direct - mirror)
    top = jnp.concatenate([jnp.where(lone, direct, both), -gap], axis=2)
    bottom = jnp.concatenate([gap, jnp.where(lone, mirror, both)], axis=2)
    return (2.0 * top).astype(jnp.bfloat16), (2.0 * bottom).astype(jnp.bfloat16)


def folded_spectral(normed, legendre, quad_weight, spec_real, spec_imag, degree_gain, circle):
    width = normed.shape[2]
    top, bottom = folded_operators(legendre, quad_weight, degree_gain)
    slots = top.shape[0]
    waves = folded_waves(circle, lax.axis_size(EVERY)).astype(jnp.bfloat16)
    columns = lax.all_to_all(normed, COLUMNS, split_axis=0, concat_axis=1, tiled=True)
    spectrum = jnp.einsum(
        "rn,tnc->trc", waves, columns, preferred_element_type=jnp.float32
    ).astype(jnp.bfloat16)
    gathered = lax.all_to_all(spectrum, EVERY, split_axis=1, concat_axis=0, tiled=True)
    lat_total = gathered.shape[0]
    channels = jnp.concatenate([spec_real, spec_imag], axis=1)
    turned = gathered.reshape(lat_total, slots, 2, width).transpose(1, 2, 0, 3)
    mixed = jnp.dot(turned, channels, preferred_element_type=jnp.float32).astype(jnp.bfloat16)
    upper = jnp.concatenate([mixed[:, 0, :, :width], mixed[:, 1, :, width:]], axis=1)
    lower = jnp.concatenate([mixed[:, 0, :, width:], mixed[:, 1, :, :width]], axis=1)
    cosine = jnp.einsum("stu,suc->stc", top, upper, preferred_element_type=jnp.float32)
    sine = jnp.einsum("stu,suc->stc", bottom, lower, preferred_element_type=jnp.float32)
    filtered = jnp.stack([cosine, sine], axis=1).astype(jnp.bfloat16)
    filtered = filtered.reshape(2 * slots, lat_total, width).transpose(1, 0, 2)
    returned = lax.all_to_all(filtered, EVERY, split_axis=0, concat_axis=1, tiled=True)
    spatial = jnp.einsum(
        "rn,trc->tnc", waves, returned, preferred_element_type=jnp.float32
    ).astype(jnp.bfloat16)
    spectral = lax.all_to_all(spatial, COLUMNS, split_axis=1, concat_axis=0, tiled=True)
    return spectral, (spectrum, filtered)


def plain_spectral(normed, legendre, quad_weight, spec_real, spec_imag, degree_gain, circle):
    lat_count = lax.axis_size("lat")
    col_count = lax.axis_size(("lon", "comp"))
    total_rows = 2 * MODES
    owned = 2 * legendre.shape[0]
    natural = jnp.arange(total_rows, dtype=jnp.int32)
    columns = lax.all_to_all(normed, ("lon", "comp"), split_axis=2, concat_axis=1, tiled=True)
    forward = forward_table(natural, circle)
    inverse = inverse_table(reorder_rows(total_rows, owned, lat_count, col_count), circle)
    spectrum = jnp.einsum(
        "anc,nr->arc", columns, forward, preferred_element_type=jnp.float32
    ).astype(jnp.bfloat16)
    gathered = lax.all_to_all(
        lax.all_to_all(spectrum, "lat", split_axis=1, concat_axis=0, tiled=True),
        ("lon", "comp"),
        split_axis=1,
        concat_axis=2,
        tiled=True,
    )
    filtered = spectral_filter(gathered, legendre, quad_weight, spec_real, spec_imag, degree_gain)
    returned = lax.all_to_all(
        lax.all_to_all(filtered, "lat", split_axis=0, concat_axis=1, tiled=True),
        ("lon", "comp"),
        split_axis=2,
        concat_axis=1,
        tiled=True,
    )
    spatial = jnp.einsum(
        "arc,rn->anc", returned, inverse, preferred_element_type=jnp.float32
    ).astype(jnp.bfloat16)
    spectral = lax.all_to_all(spatial, COLUMNS, split_axis=1, concat_axis=2, tiled=True)
    return spectral, (spectrum, filtered)


def ocean_block(padded_field, kernel, gain, up_weight, down_weight):
    stencil_reach = STENCIL_TAPS // 2 * OCEAN_DILATION
    tile_height = padded_field.shape[0] - 2 * stencil_reach
    tile_breadth = padded_field.shape[1] - 2 * stencil_reach
    stencil = jnp.zeros((tile_height, tile_breadth, padded_field.shape[2]), jnp.float32)
    for row_offset_tap in range(STENCIL_TAPS):
        for column_tap in range(STENCIL_TAPS):
            stencil_window = padded_field[
                row_offset_tap * OCEAN_DILATION : row_offset_tap * OCEAN_DILATION + tile_height,
                column_tap * OCEAN_DILATION : column_tap * OCEAN_DILATION + tile_breadth,
            ]
            stencil = stencil + stencil_window.astype(jnp.float32) * kernel[
                row_offset_tap, column_tap
            ].astype(jnp.float32)
    normed = layer_norm(stencil, gain).astype(jnp.bfloat16)
    hidden = jax.nn.gelu(jnp.dot(normed, up_weight, preferred_element_type=jnp.float32)).astype(
        jnp.bfloat16
    )
    centre = padded_field[
        stencil_reach : stencil_reach + tile_height, stencil_reach : stencil_reach + tile_breadth
    ]
    return (
        centre.astype(jnp.float32)
        + jnp.dot(hidden, down_weight, preferred_element_type=jnp.float32)
    ).astype(jnp.bfloat16)


def ocean_kernel_body(
    field_ref, taps_ref, gain_ref, up_ref, down_ref, after_ref, out_ref, wide, normed
):
    rows, cols, width = out_ref.shape
    step = OCEAN_DILATION
    lanes = 128

    @pl.loop(0, rows + (STENCIL_TAPS - 1) * step)
    def _(row):
        wide[row] = field_ref[row].astype(jnp.float32)

    @pl.loop(0, rows // 2)
    def _(pair):
        base = pair // step * (2 * step) + pair % step
        for half in range(width // lanes):
            part = slice(half * lanes, (half + 1) * lanes)
            sums = [jnp.zeros((cols, lanes), jnp.float32) for _ in range(2)]
            for a in range(STENCIL_TAPS + 1):
                for b in range(STENCIL_TAPS):
                    window = wide[base + a * step, b * step : b * step + cols, part]
                    for which in range(2):
                        tap = a - which
                        if 0 <= tap < STENCIL_TAPS:
                            weight = taps_ref[tap * STENCIL_TAPS + b, :, part]
                            sums[which] = sums[which] + window * weight
            for which in range(2):
                normed[which * cols : (which + 1) * cols, part] = sums[which]
        stencil = normed[...]
        values = layer_norm(stencil, gain_ref[...]).astype(jnp.bfloat16)
        hidden = jax.nn.gelu(
            jnp.dot(values, up_ref[...], preferred_element_type=jnp.float32)
        ).astype(jnp.bfloat16)
        moved = jnp.dot(hidden, down_ref[...], preferred_element_type=jnp.float32)
        reach = STENCIL_TAPS // 2 * step
        for which in range(2):
            row = base + which * step
            centre = wide[row + reach, reach : reach + cols, :]
            out_ref[row] = (centre + moved[which * cols : (which + 1) * cols]).astype(
                out_ref.dtype
            )


def fast_ocean_block(field, kernel, gain, up_weight, down_weight, after):
    reach = STENCIL_TAPS // 2 * OCEAN_DILATION
    rows, cols, width = field.shape[0] - 2 * reach, field.shape[1] - 2 * reach, field.shape[2]
    hidden = up_weight.shape[1]
    taps = kernel.astype(jnp.float32).reshape(STENCIL_TAPS * STENCIL_TAPS, 1, width)
    whole = pl.BlockSpec(memory_space=pltpu.VMEM)
    cells = rows * cols
    return pl.pallas_call(
        ocean_kernel_body,
        out_shape=jax.ShapeDtypeStruct((rows, cols, width), jnp.bfloat16),
        in_specs=[whole] * 5 + [pl.BlockSpec(memory_space=pl.ANY)],
        out_specs=whole,
        scratch_shapes=[
            pltpu.VMEM(field.shape, jnp.float32),
            pltpu.VMEM((2 * cols, width), jnp.float32),
        ],
        compiler_params=pltpu.CompilerParams(vmem_limit_bytes=32 * 1024 * 1024),
        cost_estimate=pl.CostEstimate(
            flops=4 * cells * width * hidden + 98 * cells * width * 64,
            bytes_accessed=4 * field.size + 4 * up_weight.size,
            transcendentals=cells * hidden,
        ),
    )(field, taps, gain[None, :], up_weight, down_weight, after)


MESH_ID = pl.DeviceIdType.MESH


def fits(atm_state, ocean_state, legendre):
    devices = lax.axis_size(EVERY)
    col_count = lax.axis_size(COLUMNS)
    lat_dev, lon_dev, width = atm_state.shape
    rows, cols, sea_width = ocean_state.shape
    circle = lon_dev * col_count
    reach = STENCIL_TAPS // 2 * OCEAN_DILATION
    return (
        folds(circle, lat_dev, col_count, devices)
        and lax.axis_size("lon") == 2
        and lax.axis_size("comp") == 2
        and circle // devices == 8
        and legendre.shape[0] == 16
        and lat_dev // col_count == 6
        and lat_dev == 2 * rows
        and cols == 2 * lon_dev
        and cols == 128
        and rows == 2 * reach
        and rows % 6 == 0
        and reach % 2 == 0
        and rows % (2 * OCEAN_DILATION) == 0
        and 128 < legendre.shape[2] <= 192
        and legendre.shape[2] % 16 == 0
        and lon_dev % 16 == 0
        and width % 128 == 0
        and sea_width == 256
    )


def whole_step_body(
    lat_total,
    atm_hbm,
    sea_hbm,
    wet_hbm,
    legendre_hbm,
    quad_hbm,
    real_hbm,
    imag_hbm,
    degree_hbm,
    gain_hbm,
    up_hbm,
    down_hbm,
    to_sea_hbm,
    from_sea_hbm,
    to_air_hbm,
    from_air_hbm,
    taps_in_hbm,
    sea_gain_hbm,
    sea_up_hbm,
    sea_down_hbm,
    waves_hbm,
    waves_back_hbm,
    air_out,
    sea_out,
    wet_ref,
    quad_ref,
    degree_ref,
    gain_ref,
    to_sea_ref,
    from_sea_ref,
    to_air_ref,
    from_air_ref,
    taps_in_ref,
    sea_gain_ref,
    air,
    sea,
    legendre,
    spec_real,
    spec_imag,
    air_up,
    air_down,
    sea_up,
    sea_down,
    waves,
    waves_back,
    taps,
    wet_square,
    wet_full,
    flux_out,
    flux_in,
    forced,
    normed,
    columns,
    spec_send,
    gathered,
    flat,
    turned_rows,
    mixed_real,
    mixed_imag,
    filtered,
    returned,
    spatial,
    spectral,
    op_send,
    op_recv,
    op_sum,
    op_other,
    op_lone,
    both,
    gap,
    field,
    edges,
    strips,
    sides,
    corners,
    wide,
    stencil,
    load_sem,
    local_sem,
    flux_sem,
    column_sem,
    owner_sem,
    back_sem,
    grid_sem,
    op_sem,
    halo_sem,
):
    f32, bf16 = jnp.float32, jnp.bfloat16
    lat = lax.axis_index("lat")
    lon = lax.axis_index("lon")
    comp = lax.axis_index("comp")
    col_count = lax.axis_size(COLUMNS)
    devices = lax.axis_size(EVERY)
    group = devices // 4
    col = lon * 2 + comp
    me = lat * col_count + col
    tile = lat * 2 + comp
    tiles = lax.axis_size("lat") * 2
    lat_dev, lon_dev, width = air.shape
    rows, cols, sea_width = sea.shape
    band = lat_dev // col_count
    pairs = band // 2
    circle = lon_dev * col_count
    step = OCEAN_DILATION
    reach = STENCIL_TAPS // 2 * step
    slots = both.shape[0]

    def at_device(index):
        return (index // col_count, index % col_count // 2, index % 2)

    def at_tile(index, side):
        return (index // 2, side, index % 2)

    def remote(source, target, sems, k, where):
        place_in = k if isinstance(k, tuple) else (k,)
        return pltpu.make_async_remote_copy(
            src_ref=source,
            dst_ref=target,
            send_sem=sems.at[(0,) + place_in],
            recv_sem=sems.at[(1,) + place_in],
            device_id=where,
            device_id_type=MESH_ID,
        )

    def across(left, right):
        return lax.dot_general(left, right, (((1,), (1,)), ((), ())), preferred_element_type=f32)

    loads = {}
    for index, (name, source, target) in enumerate(
        (
            ("legendre", legendre_hbm, legendre),
            ("degree", degree_hbm, degree_ref),
            ("to_air", to_air_hbm, to_air_ref),
            ("wet", wet_hbm, wet_ref),
            ("sea", sea_hbm, sea),
            ("to_sea", to_sea_hbm, to_sea_ref),
            ("air", atm_hbm, air),
            ("from_sea", from_sea_hbm, from_sea_ref),
            ("gain", gain_hbm, gain_ref),
            ("from_air", from_air_hbm, from_air_ref),
            ("taps", taps_in_hbm, taps_in_ref),
            ("quad", quad_hbm, quad_ref),
            ("sea_gain", sea_gain_hbm, sea_gain_ref),
            ("waves", waves_hbm, waves),
            ("sea_up", sea_up_hbm, sea_up),
            ("sea_down", sea_down_hbm, sea_down),
            ("real", real_hbm, spec_real),
            ("imag", imag_hbm, spec_imag),
            ("back", waves_back_hbm, waves_back),
            ("up", up_hbm, air_up),
            ("down", down_hbm, air_down),
        )
    ):
        loads[name] = pltpu.make_async_copy(source, target, load_sem.at[index])
    early = 13
    for name in list(loads)[:early]:
        loads[name].start()

    barrier = pltpu.get_barrier_semaphore()

    @pl.loop(1, devices)
    def _(k):
        pl.semaphore_signal(
            barrier, inc=1, device_id=at_device((me + k) % devices), device_id_type=MESH_ID
        )

    loads["legendre"].wait()
    loads["degree"].wait()
    kind = me // group
    odd = kind % 2
    place = me % group
    count = legendre.shape[0]
    edge = lat_total - 128
    row_at = lax.broadcasted_iota(jnp.int32, (lat_total, lat_total), 0)
    lane_at = lax.broadcasted_iota(jnp.int32, (lat_total, lat_total), 1)
    upper, diagonal = row_at <= lane_at, row_at == lane_at

    def operator(k):
        index = odd * ((count - k) % count) + (1 - odd) * k
        table = legendre[index]
        scaled = (table.astype(f32) * degree_ref[...][None, :]).astype(bf16)
        return across(table, scaled) * jnp.where((me == 0) & (index == 0), 0.5, 1.0).astype(f32)

    high_half = kind // 2

    def fill_operators(first_group):
        @pl.loop(first_group, first_group + 2)
        def _(which):
            tails, marks = [], []
            for spot in range(2):
                first, second = operator(4 * which + 2 * spot), operator(4 * which + 2 * spot + 1)
                square = jnp.where(upper, first, second).astype(bf16)
                op_send[which, spot * lat_total : (spot + 1) * lat_total] = square[:, 0:128]
                tails.append(square[:, 128:lat_total])
                line = jnp.sum(jnp.where(diagonal, second, 0.0), axis=0, keepdims=True)
                marks.append(line[:, 0:128])
                marks.append(
                    jnp.concatenate(
                        [line[:, 128:lat_total], jnp.zeros((1, 128 - edge), f32)], axis=1
                    )
                )

            op_send[which, 2 * lat_total : 3 * lat_total, 0 : 2 * edge] = jnp.concatenate(
                tails, axis=1
            )
            at = lax.broadcasted_iota(jnp.int32, (16, 128), 0)
            lines = jnp.zeros((16, 128), f32)
            for i in range(4):
                lines = jnp.where(at == i, marks[i], lines)
            op_send[which, 3 * lat_total : 3 * lat_total + 16] = lines.astype(bf16)

    fill_operators(2 * (1 - high_half))
    pl.semaphore_wait(barrier, devices - 1)
    across_kind = (kind + 2) % 4
    op_first = [
        remote(
            op_send.at[2 * (1 - high_half) + j],
            op_recv.at[j],
            op_sem,
            k,
            at_device(across_kind * group + place),
        )
        for k, j in enumerate((1 - odd, odd))
    ]
    op_first[0].start()
    spot_of = odd * (group - 1 - place) + (1 - odd) * place
    beside = kind + 1 - 2 * odd
    beside_place = odd * spot_of + (1 - odd) * (group - 1 - spot_of)
    op_second = remote(
        op_sum.at[1 - odd], op_other, op_sem, 2, at_device(beside * group + beside_place)
    )
    lone_moves = [
        remote(
            op_sum.at[0, pl.ds(start, lat_total)],
            op_lone.at[k],
            op_sem,
            3 + k,
            at_device((group - place) % group),
        )
        for k, start in enumerate((0, 2 * lat_total))
    ]

    def sum_operators(j):
        mine = op_send[2 * high_half + j].astype(f32)
        op_sum[j] = (mine + op_recv[j].astype(f32)).astype(bf16)

    def pass_operators():
        op_first[0].wait()
        sum_operators(1 - odd)
        op_second.start()

        @pl.when(kind == 1)
        def _():
            for move in lone_moves:
                move.start()

    def keep_operators():
        op_first[1].wait()
        sum_operators(odd)

    loads["wet"].wait()
    wet_square[...] = jnp.zeros_like(wet_square)
    wet_square[0:rows, :] = wet_ref[...].astype(f32)
    turned = jnp.transpose(wet_square[...])
    for i in range(rows):
        wet_full[i] = jnp.broadcast_to(turned[:, i : i + 1], (cols, 128))

    loads["sea"].wait()
    loads["to_air"].wait()

    few = rows // 3
    for part in range(3):
        here = slice(part * few, (part + 1) * few)
        flux = across(sea[here].reshape(few * cols, sea_width), to_air_ref[...])
        flux = flux.reshape(few, cols, -1)
        flux = (flux * wet_full[here, :, 0 : flux.shape[2]]).astype(bf16)
        flux_out[0, 0, here] = flux[:, 0:lon_dev]
        flux_out[0, 1, here] = flux[:, lon_dev : 2 * lon_dev]

    partner = (lat, lon, 1 - comp)
    moves = []
    for part in range(2):
        moves.append(
            remote(flux_out.at[part, 1 - comp], flux_in.at[part, comp], flux_sem, part, partner)
        )
    moves[0].start()
    loads["air"].wait()
    loads["to_sea"].wait()

    for part in range(4):
        here = slice(part * rows // 2, (part + 1) * rows // 2)
        there = slice(part % 2 * rows // 2, (part % 2 + 1) * rows // 2)
        flux = across(air[here].reshape(rows // 2 * lon_dev, width), to_sea_ref[...])
        flux_out[1, part // 2, there] = flux.astype(bf16).reshape(rows // 2, lon_dev, -1)

    moves[1].start()
    kept = []
    for part in range(2):
        kept.append(
            pltpu.make_async_copy(
                flux_out.at[part, comp], flux_in.at[part, comp], local_sem.at[part]
            )
        )
        kept[-1].start()
    for name in list(loads)[early:]:
        loads[name].start()
    loads["from_sea"].wait()
    loads["gain"].wait()
    for move in kept:
        move.wait()
    moves[0].wait()


    def start_columns(p):
        for k in range(1, col_count):
            other = (col + k) % col_count
            remote(
                normed.at[p, other],
                columns.at[p, col],
                column_sem,
                p,
                (lat, other // 2, other % 2),
            ).start()
        pltpu.make_async_copy(normed.at[p, col], columns.at[p, col], column_sem.at[1, p]).start()

    def wait_columns(p):
        sent = normed.at[p, pl.ds(0, col_count - 1)]
        remote(sent, sent, column_sem, p, at_device(me)).wait_send()
        pltpu.make_async_copy(columns.at[p], columns.at[p], column_sem.at[1, p]).wait()

    half_block = 2 * lon_dev
    for p in range(pairs):

        @pl.loop(0, col_count // 2)
        def _(jj):
            for j2 in range(2):
                j = 2 * jj + j2
                row = band * j + 2 * p
                flux = flux_in[0, row // rows, pl.ds(row % rows, 2)].reshape(half_block, -1)
                value = air[pl.ds(row, 2)].reshape(half_block, width).astype(f32)
                value = value + jnp.dot(flux, from_sea_ref[...], preferred_element_type=f32)
                forced[p, j] = value.reshape(2, lon_dev, width)
                value = layer_norm(value, gain_ref[0:1]).astype(bf16)
                normed[p, j] = value.reshape(2, lon_dev, width)

        start_columns(p)

    loads["from_air"].wait()
    moves[1].wait()

    @pl.loop(0, rows)
    def _(i):
        flux = jnp.concatenate([flux_in[1, 0, i], flux_in[1, 1, i]], axis=0)
        added = jnp.dot(flux, from_air_ref[...], preferred_element_type=f32)
        mask = wet_full[i]
        mask = jnp.concatenate([mask, mask], axis=1)
        field[0, i] = (sea[i].astype(f32) + mask * added).astype(bf16)

    half_reach = reach // 2
    far = tile - 1 + 2 * comp
    has_far = (far >= 0) & (far < tiles)

    def pack_strips(k):
        @pl.loop(0, rows // 2)
        def _(i):
            found = []
            for which in range(2):
                low = field[k, 2 * i + which, 0:16].astype(f32)
                high = field[k, 2 * i + which, cols - 16 : cols].astype(f32)
                found.append(jnp.where(lon == 0, high[8:16], low[0:8]))
            strips[k, i] = jnp.concatenate(found, axis=0).astype(bf16)

    def side_move(k):
        return remote(strips.at[k], sides.at[k], halo_sem.at[k], 0, at_tile(tile, 1 - lon))

    def edge_moves(k, which):
        target = far if which else tile + 1 - 2 * comp
        upper_half = comp if which else 1 - comp
        return (
            remote(
                field.at[k, pl.ds(reach * upper_half, reach)],
                edges.at[k, which],
                halo_sem.at[k],
                1 + 2 * which,
                at_tile(target, lon),
            ),
            remote(
                strips.at[k, pl.ds(half_reach * upper_half, half_reach)],
                corners.at[k, which],
                halo_sem.at[k],
                2 + 2 * which,
                at_tile(target, 1 - lon),
            ),
        )

    def send_halo(k):
        pack_strips(k)

        @pl.when(has_far)
        def _():
            for move in edge_moves(k, 1):
                move.start()

        side_move(k).start()
        for move in edge_moves(k, 0):
            move.start()

    def margins(first, pair, values):
        for which in range(2):
            part = values[8 * which : 8 * which + 8]
            wide[first + 2 * pair + which, 0:8] = jnp.where(lon == 1, part, 0.0)
            wide[first + 2 * pair + which, cols + 8 : cols + 16] = jnp.where(lon == 0, part, 0.0)

    def fill_edge(k, which, first):
        @pl.loop(0, reach)
        def _(i):
            wide[first + i, 8 : cols + 8] = edges[k, which, i].astype(f32)

        @pl.loop(0, half_reach)
        def _(i):
            margins(first, i, corners[k, which, i].astype(f32))

    def take_near(k):
        @pl.loop(0, rows)
        def _(i):
            wide[reach + i, 8 : cols + 8] = field[k, i].astype(f32)

        side_move(k).wait()
        for move in edge_moves(k, 0):
            move.wait()

        @pl.loop(0, rows // 2)
        def _(i):
            margins(reach, i, sides[k, i].astype(f32))

        fill_edge(k, 0, (reach + rows) * (1 - comp))

    def take_far(k):
        first = (reach + rows) * comp

        @pl.when(has_far)
        def _():
            for move in edge_moves(k, 1):
                move.wait()
            fill_edge(k, 1, first)

        @pl.when(jnp.logical_not(has_far))
        def _():
            @pl.loop(0, reach)
            def _(i):
                wide[first + i] = jnp.zeros(wide.shape[1:], f32)

    send_halo(0)
    op_first[1].start()
    loads["taps"].wait()
    loads["quad"].wait()
    loads["sea_gain"].wait()

    for a in range(STENCIL_TAPS):
        for b in range(STENCIL_TAPS):
            line = taps_in_ref[a, b].astype(f32)
            for k in range(2):
                taps[(k * STENCIL_TAPS + a) * STENCIL_TAPS + b] = line[k : k + 1]

    fill_operators(2 * high_half)

    triple = reach // step
    slab = cols // 2

    def sea_half(k, upper_half, after=None):
        @pl.loop(0, step)
        def _(parity):
            base = upper_half * reach + parity
            for half in range(sea_width // 128):
                part = slice(half * 128, (half + 1) * 128)
                for side in range(2):
                    sums = [jnp.zeros((slab, 128), f32) for _ in range(triple)]
                    for a in range(STENCIL_TAPS + triple - 1):
                        for b in range(STENCIL_TAPS):
                            start = 8 - reach + b * step + side * slab
                            window = wide[base + a * step, start : start + slab, part]
                            for which in range(triple):
                                tap = a - which
                                if 0 <= tap < STENCIL_TAPS:
                                    weight = taps[
                                        (k * STENCIL_TAPS + tap) * STENCIL_TAPS + b, :, part
                                    ]
                                    sums[which] = sums[which] + window * weight
                    for which in range(triple):
                        at = which * cols + side * slab
                        stencil[at : at + slab, part] = sums[which]
            values = layer_norm(stencil[...], sea_gain_ref[k : k + 1]).astype(bf16)
            hidden = jax.nn.gelu(
                jnp.dot(values, sea_up[k], preferred_element_type=f32)
            ).astype(bf16)
            moved = jnp.dot(hidden, sea_down[k], preferred_element_type=f32)
            for which in range(triple):
                row = base + which * step
                centre = wide[row + reach, 8 : 8 + cols, :]
                value = (centre + moved[which * cols : (which + 1) * cols]).astype(bf16)
                if k == 0:
                    field[1, row] = value
                else:
                    mask = wet_full[row]
                    mask = jnp.concatenate([mask, mask], axis=1)
                    sea_out[row] = jnp.where(mask > 0.5, value, sea[row])

            if after is not None:
                after(parity)

    def exchange(source, target, sems):
        def start(p):
            @pl.loop(1, devices)
            def _(k):
                other = (me + 1 + (k + devices // 2 - 2) % (devices - 1)) % devices
                remote(source.at[p, other], target.at[p, me], sems, p, at_device(other)).start()

            pltpu.make_async_copy(source.at[p, me], target.at[p, me], sems.at[1, p]).start()

        def wait(p):
            sent = source.at[p, pl.ds(0, devices - 1)]
            remote(sent, sent, sems, p, at_device(me)).wait_send()
            pltpu.make_async_copy(target.at[p], target.at[p], sems.at[1, p]).wait()

        return start, wait

    start_owner, wait_owner = exchange(spec_send, gathered, owner_sem)
    loads["waves"].wait()

    for p in range(pairs):
        wait_columns(p)
        found = []
        for which in range(2):
            lines = jnp.concatenate([columns[p, b, which] for b in range(col_count)], axis=0)
            value = jnp.dot(waves[...], lines, preferred_element_type=f32)
            found.append(value.reshape(devices, 8, width))
        spec_send[p] = jnp.concatenate(found, axis=1).astype(bf16)
        start_owner(p)

    pass_operators()
    take_near(0)
    loads["sea_up"].wait()
    loads["sea_down"].wait()
    sea_half(0, 1 - comp)
    take_far(0)
    sea_half(0, comp)
    keep_operators()

    loads["real"].wait()
    loads["imag"].wait()

    lane_parts = width // 128
    bunch = 2 * devices

    def mix_rows(p):
        wait_owner(p)
        if p == pairs - 1:
            send_halo(1)
        value = gathered[p].astype(f32).reshape(16 * devices, width)
        for c in range(lane_parts):
            flat[p, c] = value[:, c * 128 : (c + 1) * 128]
        for q in range(8):
            for which in range(2):
                taken = [
                    flat[p, c, pl.ds(8 * which + q, devices, stride=16), :]
                    for c in range(lane_parts)
                ]
                at = q * bunch + which * devices
                turned_rows[at : at + devices] = jnp.concatenate(taken, axis=1).astype(bf16)
        for target, matrix in ((mixed_real, spec_real), (mixed_imag, spec_imag)):
            value = jnp.dot(turned_rows[...], matrix[...], preferred_element_type=f32)
            target[:, p * bunch : (p + 1) * bunch] = value.astype(bf16).reshape(8, bunch, width)

    op_second.wait()

    @pl.when(kind == 1)
    def _():
        for move in lone_moves:
            move.wait_send()

    @pl.when(kind == 0)
    def _():
        for move in lone_moves:
            move.wait_recv()

    pair_at, rest_at = row_at // (2 * devices), row_at % (2 * devices)
    source_at = band * (rest_at % devices) + 2 * pair_at + rest_at // devices
    order = jnp.where(lane_at == source_at, 1.0, 0.0).astype(bf16)
    unit = jnp.where(diagonal, 1.0, 0.0).astype(bf16)

    def unpack(packed, spot):
        lanes = slice(spot * edge, (spot + 1) * edge)
        square = jnp.concatenate(
            [
                packed[spot * lat_total : (spot + 1) * lat_total],
                packed[2 * lat_total : 3 * lat_total, lanes],
            ],
            axis=1,
        )
        flipped = across(unit, square)
        square = square.astype(f32)
        lines = packed[3 * lat_total : 3 * lat_total + 16].astype(f32)
        line = jnp.concatenate(
            [lines[2 * spot : 2 * spot + 1], lines[2 * spot + 1 : 2 * spot + 2, 0:edge]], axis=1
        )
        first = jnp.where(upper, square, flipped)
        second = jnp.where(upper, jnp.where(diagonal, line, flipped), square)
        return first, second

    scale = 2.0 / lat_total * quad_ref[...]
    for spot in range(2):
        same, other = unpack(op_sum.at[odd], spot), unpack(op_other, spot)
        for i in range(2):
            s = 2 * spot + i
            lone = (me == 0) & (s == 0)
            theirs = other[i]
            if s == 0:
                alone = jnp.concatenate([op_lone[0], op_lone[1, :, 0:edge]], axis=1)
                alone = jnp.where(upper, alone.astype(f32), across(unit, alone))
                theirs = jnp.where(kind == 0, alone, theirs)
            direct = jnp.where(odd == 0, same[i], theirs)
            mirror = jnp.where(odd == 0, theirs, same[i])

            def ordered(value):
                value = (value * scale).astype(bf16)
                value = jnp.dot(order, value, preferred_element_type=f32).astype(bf16)
                return across(value, order).astype(bf16)

            both[s, 0] = ordered(jnp.where(lone, direct, direct + mirror))
            if s == 0:
                both[s, 1] = ordered(jnp.where(lone, mirror, direct + mirror))
            gap[s] = ordered(jnp.where(lone, 0.0, direct - mirror))

    for p in range(pairs):
        mix_rows(p)

    def act(matrix, value):
        return jnp.dot(matrix, value, preferred_element_type=f32)

    def act_on(first, last):
        here = slice(first * bunch, last * bunch)
        for s in range(slots):
            re, im = 2 * s, 2 * s + 1
            crossed = jnp.concatenate([mixed_imag[im], mixed_imag[re]], axis=1)
            crossed = act(gap[s, here], crossed)
            if s == 0:
                cosine = act(both[s, 0, here], mixed_real[re])
                sine = act(both[s, 1, here], mixed_real[im])
            else:
                straight = jnp.concatenate([mixed_real[re], mixed_real[im]], axis=1)
                straight = act(both[s, 0, here], straight)
                cosine, sine = straight[:, 0:width], straight[:, width : 2 * width]
            cosine = cosine - crossed[:, 0:width]
            sine = sine + crossed[:, width : 2 * width]
            for q, value in ((re, cosine), (im, sine)):
                for p in range(first, last):
                    for which in range(2):
                        at = (p - first) * bunch + which * devices
                        for c in range(lane_parts):
                            flat[p, c, pl.ds(8 * which + q, devices, stride=16), :] = value[
                                at : at + devices, c * 128 : (c + 1) * 128
                            ]

    start_back, wait_back = exchange(filtered, returned, back_sem)

    def send_back(p):
        value = jnp.concatenate([flat[p, c] for c in range(lane_parts)], axis=1)
        filtered[p] = value.astype(bf16).reshape(devices, 16, width)
        start_back(p)

    def send_later(parity):
        for p in range(1, pairs):

            @pl.when(parity == p - 1)
            def _():
                send_back(p)

    act_on(0, 1)
    send_back(0)
    act_on(1, pairs)
    take_near(1)
    sea_half(1, 1 - comp, send_later)

    def start_grid(p, which):
        sems = grid_sem
        for k in range(1, col_count):
            other = (col + k) % col_count
            remote(
                spatial.at[p, other, which],
                spectral.at[p, col, which],
                sems,
                2 * p + which,
                (lat, other // 2, other % 2),
            ).start()
        pltpu.make_async_copy(
            spatial.at[p, col, which], spectral.at[p, col, which], sems.at[1, 2 * p + which]
        ).start()

    def wait_grid(p, which):
        sent = spatial.at[p, pl.ds(0, col_count - 1), which]
        remote(sent, sent, grid_sem, 2 * p + which, at_device(me)).wait_send()
        here = spectral.at[p, :, which]
        pltpu.make_async_copy(here, here, grid_sem.at[1, 2 * p + which]).wait()

    def to_grid(p):
        wait_back(p)
        for which in range(2):
            lines = returned[p, :, 8 * which : 8 * which + 8].astype(f32)
            lines = lines.reshape(circle, width).astype(bf16)
            line = jnp.dot(waves_back[...], lines, preferred_element_type=f32).astype(bf16)
            for b in range(col_count):
                spatial[p, b, which] = line[b * lon_dev : (b + 1) * lon_dev]
            start_grid(p, which)

    def finish(p):

        @pl.loop(0, 2)
        def _(which):
            wait_grid(p, which)
            value = forced[p, :, which].reshape(col_count * lon_dev, width)
            value = value + spectral[p, :, which].reshape(col_count * lon_dev, width).astype(f32)
            inner = layer_norm(value, gain_ref[1:2]).astype(bf16)
            hidden = jax.nn.gelu(
                jnp.dot(inner, air_up[...], preferred_element_type=f32)
            ).astype(bf16)
            value = value + jnp.dot(hidden, air_down[...], preferred_element_type=f32)
            value = value.astype(bf16).reshape(col_count, lon_dev, width)
            for j in range(col_count):
                air_out[band * j + 2 * p + which] = value[j]

    loads["back"].wait()
    loads["up"].wait()
    loads["down"].wait()
    take_far(1)

    def between(parity):
        @pl.when(parity == 0)
        def _():
            to_grid(0)

    sea_half(1, comp, between)
    to_grid(1)
    finish(0)
    to_grid(2)
    finish(1)
    finish(2)


def put_body(air, sea, air_hbm, sea_hbm, sems):
    moves = (
        pltpu.make_async_copy(air, air_hbm, sems.at[0]),
        pltpu.make_async_copy(sea, sea_hbm, sems.at[1]),
    )
    for move in moves:
        move.start()
    for move in moves:
        move.wait()


def whole_step(
    atm_state,
    ocean_state,
    wet_mask,
    legendre,
    quad_weight,
    spec_real,
    spec_imag,
    degree_gain,
    atm_gain,
    atm_up,
    atm_down,
    atm_to_surface,
    surface_to_atm,
    ocean_to_surface,
    surface_to_ocean,
    ocean_kernel,
    ocean_gain,
    ocean_up,
    ocean_down,
):
    bf16, f32 = jnp.bfloat16, jnp.float32
    devices = lax.axis_size(EVERY)
    col_count = lax.axis_size(COLUMNS)
    lat_dev, lon_dev, width = atm_state.shape
    rows, cols, sea_width = ocean_state.shape
    circle = lon_dev * col_count
    lat_total = legendre.shape[2]
    band = lat_dev // col_count
    reach = STENCIL_TAPS // 2 * OCEAN_DILATION
    slots = legendre.shape[0] // 4
    surface = atm_to_surface.shape[1]
    with jax.ensure_compile_time_eval():
        table = np.asarray(folded_waves(circle, devices).astype(f32))
    waves = jnp.asarray(table, f32).astype(bf16)
    waves_back = jnp.asarray(table.T, f32).astype(bf16)
    vmem = pl.BlockSpec(memory_space=pltpu.VMEM)
    hbm = pl.BlockSpec(memory_space=pl.ANY)
    pairs = band // 2
    tall = (pairs, devices, 16, width)
    patches = (pairs, col_count, 2, lon_dev, width)
    dma = pltpu.SemaphoreType.DMA
    results = pl.pallas_call(
        functools.partial(whole_step_body, lat_total),
        out_shape=(
            pltpu.VMEM(atm_state.shape, bf16),
            pltpu.VMEM(ocean_state.shape, bf16),
        ),
        in_specs=[
            hbm
        ] * 21,
        out_specs=(vmem, vmem),
        scratch_shapes=[
            pltpu.VMEM(wet_mask.shape, jnp.int32),
            pltpu.VMEM((1, lat_total), f32),
            pltpu.VMEM(degree_gain.shape, f32),
            pltpu.VMEM(atm_gain.shape, f32),
            pltpu.VMEM(atm_to_surface.shape[::-1], bf16),
            pltpu.VMEM(surface_to_atm.shape, bf16),
            pltpu.VMEM(ocean_to_surface.shape[::-1], bf16),
            pltpu.VMEM(surface_to_ocean.shape, bf16),
            pltpu.VMEM((STENCIL_TAPS, STENCIL_TAPS, 2, sea_width), bf16),
            pltpu.VMEM(ocean_gain.shape, f32),
            pltpu.VMEM(atm_state.shape, bf16),
            pltpu.VMEM(ocean_state.shape, bf16),
            pltpu.VMEM((legendre.shape[0], lat_total, legendre.shape[1]), bf16),
            pltpu.VMEM(spec_real.shape, bf16),
            pltpu.VMEM(spec_imag.shape, bf16),
            pltpu.VMEM(atm_up.shape, bf16),
            pltpu.VMEM(atm_down.shape, bf16),
            pltpu.VMEM(ocean_up.shape, bf16),
            pltpu.VMEM(ocean_down.shape, bf16),
            pltpu.VMEM(waves.shape, bf16),
            pltpu.VMEM(waves.shape, bf16),
            pltpu.VMEM((2 * STENCIL_TAPS * STENCIL_TAPS, 1, sea_width), f32),
            pltpu.VMEM((128, 128), f32),
            pltpu.VMEM((rows, cols, 128), f32),
            pltpu.VMEM((2, 2, rows, lon_dev, surface), bf16),
            pltpu.VMEM((2, 2, rows, lon_dev, surface), bf16),
            pltpu.VMEM(patches, f32),
            pltpu.VMEM(patches, bf16),
            pltpu.VMEM(patches, bf16),
            pltpu.VMEM(tall, bf16),
            pltpu.VMEM(tall, bf16),
            pltpu.VMEM((pairs, width // 128, 16 * devices, 128), f32),
            pltpu.VMEM((16 * devices, width), bf16),
            pltpu.VMEM((8, lat_total, width), bf16),
            pltpu.VMEM((8, lat_total, width), bf16),
            pltpu.VMEM(tall, bf16),
            pltpu.VMEM(tall, bf16),
            pltpu.VMEM(patches, bf16),
            pltpu.VMEM(patches, bf16),
            pltpu.VMEM((4, 3 * lat_total + 16, 128), bf16),
            pltpu.VMEM((2, 3 * lat_total + 16, 128), bf16),
            pltpu.VMEM((2, 3 * lat_total + 16, 128), bf16),
            pltpu.VMEM((3 * lat_total + 16, 128), bf16),
            pltpu.VMEM((2, lat_total, 128), bf16),
            pltpu.VMEM((slots, 2, lat_total, lat_total), bf16),
            pltpu.VMEM((slots, lat_total, lat_total), bf16),
            pltpu.VMEM((2,) + ocean_state.shape, bf16),
            pltpu.VMEM((2, 2, reach, cols, sea_width), bf16),
            pltpu.VMEM((2, rows // 2, 16, sea_width), bf16),
            pltpu.VMEM((2, rows // 2, 16, sea_width), bf16),
            pltpu.VMEM((2, 2, reach // 2, 16, sea_width), bf16),
            pltpu.VMEM((rows + 2 * reach, cols + 16, sea_width), f32),
            pltpu.VMEM((reach // OCEAN_DILATION * cols, sea_width), f32),
            dma((21,)),
            dma((2,)),
            dma((2, 2)),
            dma((2, pairs)),
            dma((2, pairs)),
            dma((2, pairs)),
            dma((2, 2 * pairs)),
            dma((2, 5)),
            dma((2, 2, 5)),
        ],
        compiler_params=pltpu.CompilerParams(
            collective_id=0, has_side_effects=True, vmem_limit_bytes=56 * 1024 * 1024
        ),
    )(
        atm_state,
        ocean_state,
        wet_mask,
        jnp.swapaxes(legendre, 1, 2),
        quad_weight[None, :],
        spec_real,
        spec_imag,
        degree_gain,
        atm_gain,
        atm_up,
        atm_down,
        atm_to_surface.T,
        surface_to_atm,
        ocean_to_surface.T,
        surface_to_ocean,
        ocean_kernel.transpose(1, 2, 0, 3),
        ocean_gain,
        ocean_up,
        ocean_down,
        waves,
        waves_back,
    )
    return pl.pallas_call(
        put_body,
        out_shape=(
            jax.ShapeDtypeStruct(atm_state.shape, bf16),
            jax.ShapeDtypeStruct(ocean_state.shape, bf16),
        ),
        in_specs=[pl.BlockSpec(memory_space=pl.ANY)] * 2,
        out_specs=(hbm, hbm),
        scratch_shapes=[dma((2,))],
        compiler_params=pltpu.CompilerParams(vmem_limit_bytes=2 * 1024 * 1024),
    )(*results)


def local(
    atm_state,
    ocean_state,
    wet_mask,
    legendre,
    quad_weight,
    spec_real,
    spec_imag,
    degree_gain,
    atm_gain,
    atm_up,
    atm_down,
    atm_to_surface,
    surface_to_atm,
    ocean_to_surface,
    surface_to_ocean,
    ocean_kernel,
    ocean_gain,
    ocean_up,
    ocean_down,
):
    col_count = lax.axis_size(COLUMNS)
    lat_dev, lon_dev, _ = atm_state.shape
    circle = lon_dev * col_count
    if fits(atm_state, ocean_state, legendre):
        return whole_step(
            atm_state,
            ocean_state,
            wet_mask,
            legendre,
            quad_weight,
            spec_real,
            spec_imag,
            degree_gain,
            atm_gain,
            atm_up,
            atm_down,
            atm_to_surface,
            surface_to_atm,
            ocean_to_surface,
            surface_to_ocean,
            ocean_kernel,
            ocean_gain,
            ocean_up,
            ocean_down,
        )
    wet = wet_mask.astype(jnp.float32)[:, :, None]
    ocean_flux = (
        jnp.dot(ocean_state, ocean_to_surface, preferred_element_type=jnp.float32) * wet
    ).astype(jnp.bfloat16)
    atm_flux = jnp.dot(atm_state, atm_to_surface, preferred_element_type=jnp.float32).astype(
        jnp.bfloat16
    )
    flux_here = lax.all_to_all(ocean_flux, "comp", split_axis=1, concat_axis=0, tiled=True)
    flux_sea = lax.all_to_all(atm_flux, "comp", split_axis=0, concat_axis=1, tiled=True)
    forced = atm_state.astype(jnp.float32) + jnp.dot(
        flux_here, surface_to_atm, preferred_element_type=jnp.float32
    )
    normed = layer_norm(forced, atm_gain[0]).astype(jnp.bfloat16)
    run_spectral = (
        folded_spectral
        if folds(circle, lat_dev, col_count, lax.axis_size(EVERY))
        else plain_spectral
    )
    spectral, stages = run_spectral(
        normed, legendre, quad_weight, spec_real, spec_imag, degree_gain, circle
    )
    mixed = forced + spectral.astype(jnp.float32)
    normed_two = layer_norm(mixed, atm_gain[1]).astype(jnp.bfloat16)
    hidden = jax.nn.gelu(jnp.dot(normed_two, atm_up, preferred_element_type=jnp.float32)).astype(
        jnp.bfloat16
    )
    atm_out = (mixed + jnp.dot(hidden, atm_down, preferred_element_type=jnp.float32)).astype(
        jnp.bfloat16
    )
    ocean_in = (
        ocean_state.astype(jnp.float32)
        + wet * jnp.dot(flux_sea, surface_to_ocean, preferred_element_type=jnp.float32)
    ).astype(jnp.bfloat16)
    stencil_reach = STENCIL_TAPS // 2 * OCEAN_DILATION
    sides = ((("lat", "comp"), 0), ("lon", 1))
    current = ocean_in
    quick = ocean_in.shape[0] % (2 * OCEAN_DILATION) == 0 and ocean_in.shape[2] % 128 == 0
    for k in range(2):
        field = padded(current, sides, stencil_reach)
        weights = (ocean_kernel[k], ocean_gain[k], ocean_up[k], ocean_down[k])
        if quick:
            current = fast_ocean_block(field, *weights, stages[k])
        else:
            current = ocean_block(field, *weights)
    ocean_out = jnp.where(wet_mask[:, :, None] == 1, current, ocean_state)
    return (atm_out, ocean_out)


def solution(mesh):
    placed = (
        P("lat", ("lon", "comp"), None),
        P(("lat", "comp"), "lon", None),
        P(("lat", "comp"), "lon"),
        P(("lat", "lon", "comp"), None, None),
        P(),
        P(),
        P(),
        P(),
        P(),
        P(),
        P(),
        P(),
        P(),
        P(),
        P(),
        P(),
        P(),
        P(),
        P(),
    )

    return jax.shard_map(
        local,
        mesh=mesh,
        in_specs=placed,
        out_specs=(P("lat", ("lon", "comp"), None), P(("lat", "comp"), "lon", None)),
        check_vma=False,
    )
```
